128 devices in a mesh: rep: 32 (over y, z, x_lo), grp: 4 (over x_hi, core).
Axes of the slice: x: 4 (x_hi: 2, x_lo: 2; x = x_hi * 2 + x_lo), y: 4, z: 4, core: 2. Of those that a mesh axis runs over, the one named last changes fastest.
Arguments:
- tokens: bfloat16 [64, 1024, 768], P('rep', 'grp'), may hold values from -6 to 6
- segment: int32 [64, 1024], P('rep'), may hold values from 0 to 1, as said below
- piece_start: int32 [64, 1024], P('rep'), may hold values from 0 to 1023, as said below
- w_query: bfloat16 [768, 768], P('grp'), may hold values from -0.21875 to 0.21875
- w_key: bfloat16 [768, 768], P('grp'), may hold values from -0.21875 to 0.21875
- w_value: bfloat16 [768, 768], P('grp'), may hold values from -0.21875 to 0.21875
- w_out: bfloat16 [768, 768], P('grp'), may hold values from -3.5 to 3.5
- w_gate: bfloat16 [768, 3072], P('grp'), may hold values from -0.21875 to 0.21875
- w_up: bfloat16 [768, 3072], P('grp'), may hold values from -0.21875 to 0.21875
- w_down: bfloat16 [3072, 768], P('grp'), may hold values from -0.109375 to 0.109375
- cotangent: bfloat16 [64, 1024, 768], P('rep', 'grp'), may hold values from -6 to 6
Outputs:
- output: bfloat16 [64, 1024, 768], P('rep', 'grp')
- grad_tokens: bfloat16 [64, 1024, 768], P('rep', 'grp')
- grad_query: float32 [768, 768], P('grp')
- grad_key: float32 [768, 768], P('grp')
- grad_value: float32 [768, 768], P('grp')
- grad_out: float32 [768, 768], P('grp')
- grad_gate: float32 [768, 3072], P('grp')
- grad_up: float32 [768, 3072], P('grp')
- grad_down: float32 [3072, 768], P('grp')
The draws below stay inside these ranges and needn't reach their ends.
Inputs may be any that keep to these rules, and one draw needn't show every extreme that they name: `segment`: along a sequence the numbers start at 0, never fall, rise by one at a time, and rise only at the first position of a picture piece. `piece_start`: each sequence holds 2 picture pieces of 256 positions, the k-th lying within positions k * (512) to (k + 1) * 512 - 1; a piece's positions hold its first position, all other positions their own.
All inputs are finite; a program needn't handle non-finite values.
Results may differ from the reference program's by a relative error of at most 0.029.
Values may be sent and summed in bfloat16 or wider, within the bound.
No kernel may reach another device: no remote copies, remote signals or barrier semaphores. Data moves between devices by JAX's collectives and lax.ppermute only.
A program may use at most 256 MiB of HBM per device.

```python
import jax
import jax.numpy as jnp
from jax import lax

D = 768
HEADS = 12
HDIM = 64
FF = 3072
PIECE = 256
SEQ = 1024
SEQS = 64
NPIECE = 2


def layout_parts(key):
    span_len = SEQ // NPIECE
    offsets = jax.random.randint(jax.random.fold_in(key, 11), (SEQS, NPIECE), 0, span_len - PIECE + 1)
    firsts = offsets + span_len * jnp.arange(NPIECE, dtype=jnp.int32)[None, :]
    new_doc = jax.random.randint(jax.random.fold_in(key, 12), (SEQS, NPIECE), 0, 2)
    new_doc = new_doc * (jnp.arange(NPIECE, dtype=jnp.int32)[None, :] > 0).astype(jnp.int32)
    places = jnp.arange(SEQ, dtype=jnp.int32)
    inside = (places[None, None, :] >= firsts[:, :, None]) & (places[None, None, :] < firsts[:, :, None] + PIECE)
    starts = places[None, :] + jnp.sum(jnp.where(inside, firsts[:, :, None] - places[None, None, :], 0), axis=1)
    segment = jnp.sum(jnp.where(places[None, None, :] >= firsts[:, :, None], new_doc[:, :, None], 0), axis=1)
    return (segment.astype(jnp.int32), starts.astype(jnp.int32))


def draw_segment(key, part):
    return layout_parts(key)[0]


def draw_piece_start(key, part):
    return layout_parts(key)[1]


def block_scale(key, extent, shards, least, largest):
    def one(position, parts):
        steps = jax.random.uniform(jax.random.fold_in(jax.random.fold_in(key, 6), position), (parts,), jnp.float32, least / len(shards), largest / len(shards))
        return jnp.repeat(jnp.exp(steps), extent[position] // parts).reshape((-1,) + (1,) * (len(extent) - position - 1))

    factor_of = one(*shards[0])
    for cut in shards[1:]:
        factor_of = factor_of * one(*cut)
    return factor_of


def bell_draw(rng, dims, scale, bound, cuts=(), kind=jnp.bfloat16):
    entries = jax.random.normal(rng, dims, jnp.float32) * scale
    if len(cuts) > 0:
        entries = block_scale(rng, dims, cuts, -0.22, 0.18) * entries
    return jnp.clip(entries, min=-bound, max=bound).astype(kind)


def setup_inputs(seed: int = 0) -> dict:
    splits = jax.random.split(jax.random.key(seed), 12)
    return {
        "tokens": bell_draw(splits[0], (SEQS, SEQ, D), 1.0, 6.0, ((0, 32), (1, 4))),
        "segment": draw_segment(jax.random.fold_in(splits[11], 71), 0),
        "piece_start": draw_piece_start(jax.random.fold_in(splits[11], 71), 0),
        "w_query": bell_draw(splits[3], (D, D), D ** -0.5, 0.21875, ((0, 4),)),
        "w_key": bell_draw(splits[4], (D, D), D ** -0.5, 0.21875, ((0, 4),)),
        "w_value": bell_draw(splits[5], (D, D), D ** -0.5, 0.21875, ((0, 4),)),
        "w_out": bell_draw(splits[6], (D, D), (max(1, 4 * D // SEQ)) ** -0.5, 3.5, ((0, 4),)),
        "w_gate": bell_draw(splits[7], (D, FF), D ** -0.5, 0.21875, ((0, 4),)),
        "w_up": bell_draw(splits[8], (D, FF), D ** -0.5, 0.21875, ((0, 4),)),
        "w_down": bell_draw(splits[9], (FF, D), FF ** -0.5, 0.109375, ((0, 4),)),
        "cotangent": bell_draw(splits[10], (SEQS, SEQ, D), 1.0, 6.0, ((0, 32), (1, 4))),
    }


@jax.custom_vjp
def low(v):
    return lax.optimization_barrier(v.astype(jnp.bfloat16)).astype(jnp.float32)

@jax.custom_vjp
def low_back(v):
    return v

def low_keep(v):
    return (low(v), None)

def low_pass(kept, grad):
    return (grad,)

def back_keep(v):
    return (v, None)

def back_low(kept, grad):
    return (low(grad),)
low.defvjp(low_keep, low_pass)
low_back.defvjp(back_keep, back_low)

def matmul(left, right):
    return jnp.dot(left, right, precision=lax.Precision.HIGHEST)

def layer_norm(hidden):
    centred = hidden - lax.optimization_barrier(jnp.mean(hidden, axis=-1, keepdims=True))
    spread = lax.optimization_barrier(jnp.mean(centred * centred, axis=-1, keepdims=True))
    return centred * lax.rsqrt(spread + 1e-05)

def rotate(heads, cosine, sine):
    half = heads.shape[-1] // 2
    first = heads[..., :half]
    second = heads[..., half:]
    return jnp.concatenate([first * cosine - second * sine, second * cosine + first * sine], axis=-1)

def gated(gate, upper):
    return gate / (1.0 + jnp.exp(-gate)) * upper

def forward(hidden, w_query, w_key, w_value, w_out, w_gate, w_up, w_down, allowed, cosine, sine):
    normed = low(layer_norm(hidden))
    query = low(rotate(low_back(matmul(normed, w_query)).reshape(SEQ, HEADS, HDIM), cosine, sine))
    keys = low(rotate(low_back(matmul(normed, w_key)).reshape(SEQ, HEADS, HDIM), cosine, sine))
    values = low(low_back(matmul(normed, w_value))).reshape(SEQ, HEADS, HDIM)
    raw = low_back(jnp.einsum('qhd,khd->hqk', query, keys, precision=lax.Precision.HIGHEST))
    scores = jnp.where(allowed[None], raw * HDIM ** (-0.5), -1e+30)
    highest = lax.optimization_barrier(jnp.max(scores, axis=-1, keepdims=True))
    expd = jnp.exp(scores - highest)
    probs = low(expd / lax.optimization_barrier(jnp.sum(expd, axis=-1, keepdims=True)))
    mixed = jnp.einsum('hqk,khd->qhd', probs, values, precision=lax.Precision.HIGHEST).reshape(SEQ, D)
    after = hidden + low_back(matmul(low(low_back(mixed)), w_out))
    normed_two = low(layer_norm(after))
    gate = low_back(matmul(normed_two, w_gate))
    upper = low_back(matmul(normed_two, w_up))
    active = low(gated(gate, upper))
    return after + low_back(matmul(active, w_down))

def reference(tokens, segment, piece_start, w_query, w_key, w_value, w_out, w_gate, w_up, w_down, cotangent):
    params = tuple((weight.astype(jnp.float32) for weight in (w_query, w_key, w_value, w_out, w_gate, w_up, w_down)))
    places = jnp.arange(SEQ, dtype=jnp.int32)
    inverse = 10000.0 ** (-jnp.arange(0, HDIM, 2).astype(jnp.float32) / HDIM)
    angles = places.astype(jnp.float32)[:, None] * inverse[None, :]
    cosine = jnp.cos(angles)[:, None, :]
    sine = jnp.sin(angles)[:, None, :]

    def one(totals, item):
        source, seg_row, start_row, grad_row = item
        causal = places[None, :] <= places[:, None]
        same_piece = start_row[:, None] == start_row[None, :]
        allowed = (seg_row[:, None] == seg_row[None, :]) & (causal | same_piece)

        def layer(inputs, *matrices):
            return forward(inputs, *matrices, allowed, cosine, sine)
        result, pull = jax.vjp(layer, source.astype(jnp.float32), *params)
        grads = pull(grad_row.astype(jnp.float32))
        totals = tuple((total + grad for total, grad in zip(totals, grads[1:])))
        return (totals, (result.astype(jnp.bfloat16), grads[0].astype(jnp.bfloat16)))
    zeros = tuple((jnp.zeros(weight.shape, jnp.float32) for weight in params))
    totals, stacked = lax.scan(one, zeros, (tokens, segment, piece_start, cotangent))
    return (stacked[0], stacked[1], totals[0], totals[1], totals[2], totals[3], totals[4], totals[5], totals[6])
```

```python
import jax
import jax.numpy as jnp
from jax import lax
from jax.sharding import Mesh
from jax.sharding import PartitionSpec as P

HEADS = 12
HDIM = 64
REP = ("y", "z", "xl")
GRP = ("xh", "c")


def layer_norm(hidden):
    centred = hidden - jnp.mean(hidden, axis=-1, keepdims=True)
    spread = jnp.mean(centred * centred, axis=-1, keepdims=True)
    return centred * lax.rsqrt(spread + 1e-05)


def rotate(heads, cosine, sine):
    half = heads.shape[-1] // 2
    first = heads[..., :half]
    second = heads[..., half:]
    return jnp.concatenate(
        [first * cosine - second * sine, second * cosine + first * sine], axis=-1
    )


def gated(gate, upper):
    return gate / (1.0 + jnp.exp(-gate)) * upper


def matmul(left, right):
    return jnp.dot(left, right, preferred_element_type=jnp.float32)


def contract_rows(left, right):
    return lax.dot_general(
        left, right, (((0,), (0,)), ((), ())), preferred_element_type=jnp.float32
    )


def contract_cols(left, right):
    return lax.dot_general(
        left, right, (((1,), (1,)), ((), ())), preferred_element_type=jnp.float32
    )


def shift(x, axis, n, step):
    return lax.ppermute(x, axis, [(i, (i + step) % n) for i in range(n)])


def ring_gather(piece, axis, n):
    if n == 1:
        return piece[None]
    me = lax.axis_index(axis)
    if n == 2:
        other = shift(piece, axis, 2, 1)
        return jnp.where(me == 0, jnp.stack([piece, other]), jnp.stack([other, piece]))
    got = {0: piece}
    back = piece
    ahead = piece
    for step in range(1, n // 2 + 1):
        back = shift(back, axis, n, 1)
        got[(-step) % n] = back
        if step < n - step:
            ahead = shift(ahead, axis, n, -1)
            got[step % n] = ahead
    stacked = jnp.stack([got[k] for k in range(n)])
    return jnp.take(stacked, (jnp.arange(n) - me) % n, axis=0)


def ring_reduce(chunks, axis, n):
    if n == 1:
        return chunks[0]
    me = lax.axis_index(axis)
    if n == 2:
        sent = shift(jnp.take(chunks, 1 - me, axis=0).astype(jnp.bfloat16), axis, 2, 1)
        return jnp.take(chunks, me, axis=0) + sent.astype(jnp.float32)
    half = chunks.shape[-1] // 2
    parts = []
    for direction, sl in ((1, slice(0, half)), (-1, slice(half, None))):
        part = chunks[..., sl]
        acc = jnp.take(part, (me - direction) % n, axis=0)
        for step in range(n - 1):
            got = shift(acc.astype(jnp.bfloat16), axis, n, direction)
            acc = got.astype(jnp.float32) + jnp.take(part, (me - direction * (step + 2)) % n, axis=0)
        parts.append(acc)
    return jnp.concatenate(parts, axis=-1)


def gather_weights(shards, sizes):
    ny, nz = sizes["y"], sizes["z"]
    y = lax.axis_index("y")
    z = lax.axis_index("z")
    g = lax.axis_index("xh") * 2 + lax.axis_index("c")
    flat = jnp.concatenate([s.reshape(-1) for s in shards])
    length = flat.shape[0]
    pieces = flat.reshape(ny * nz, length // (ny * nz))
    mine = jnp.take(pieces, y * nz + z, axis=0)
    crossed = lax.ppermute(mine, ("xl", "xh"), [(i, 3 - i) for i in range(4)])
    along_z = ring_gather(crossed, "z", nz)
    along_y = ring_gather(along_z.reshape(-1), "y", ny)
    other_side = along_y.reshape(-1)
    pair = jnp.stack([flat, other_side])
    partner = lax.ppermute(pair, "c", [(0, 1), (1, 0)])
    relative = jnp.stack([flat, partner[0], other_side, partner[1]])
    whole = jnp.take(relative, jnp.arange(4) ^ g, axis=0)
    out = []
    start = 0
    for s in shards:
        count = s.size
        out.append(whole[:, start:start + count].reshape(4 * s.shape[0], s.shape[1]))
        start += count
    return out


def reduce_grads(grads, sizes):
    ny, nz, nl = sizes["y"], sizes["z"], sizes["xl"]
    g = lax.axis_index("xh") * 2 + lax.axis_index("c")
    xl = lax.axis_index("xl")
    flat = jnp.concatenate([w.reshape(4, -1) for w in grads], axis=1)
    length = flat.shape[1]
    relative = jnp.take(flat, jnp.arange(4) ^ g, axis=0)
    send = jnp.stack([relative[1], relative[3]]).astype(jnp.bfloat16)
    got = lax.ppermute(send, "c", [(0, 1), (1, 0)]).astype(jnp.float32)
    pair = jnp.stack([relative[0], relative[2]]) + got
    chunk = length // (ny * nz * nl)
    red = ring_reduce(pair.reshape(2, ny, length // ny).transpose(1, 0, 2), "y", ny)
    red = ring_reduce(red.reshape(2, nz, length // (ny * nz)).transpose(1, 0, 2), "z", nz)
    halves = red.reshape(2, nl, chunk)
    own_keep = jnp.take(halves[0], xl, axis=0)
    own_send = jnp.take(halves[0], 1 - xl, axis=0)
    oth_keep = jnp.take(halves[1], 1 - xl, axis=0)
    oth_send = jnp.take(halves[1], xl, axis=0)
    got = lax.ppermute(
        jnp.stack([own_send, oth_send]).astype(jnp.bfloat16), "xl", [(0, 1), (1, 0)]
    ).astype(jnp.float32)
    own = own_keep + got[0]
    oth = oth_keep + got[1]
    crossed = lax.ppermute(oth.astype(jnp.bfloat16), ("xl", "xh"), [(i, 3 - i) for i in range(4)])
    own = own + crossed.astype(jnp.float32)
    own = own.astype(jnp.bfloat16)
    full = ring_gather(own, "xl", nl).reshape(-1)
    full = ring_gather(full, "z", nz).reshape(-1)
    full = ring_gather(full, "y", ny).reshape(-1)
    out = []
    start = 0
    for w in grads:
        count = w.size // 4
        out.append(full[start:start + count].reshape(w.shape[0] // 4, w.shape[1]).astype(jnp.float32))
        start += count
    return out


def to_sequence(x):
    xh = lax.axis_index("xh")
    c = lax.axis_index("c")
    first = lax.ppermute(jnp.take(x, c, axis=0), GRP, [(0, 0), (1, 2), (2, 1), (3, 3)])
    second = lax.ppermute(jnp.take(x, 1 - c, axis=0), GRP, [(0, 2), (1, 0), (2, 3), (3, 1)])
    return jnp.where(xh == 0, jnp.concatenate([first, second]), jnp.concatenate([second, first]))


def from_sequence(x):
    xh = lax.axis_index("xh")
    c = lax.axis_index("c")
    length = x.shape[0] // 2
    first = jnp.where(xh == 0, x[:length], x[length:])
    second = jnp.where(xh == 0, x[length:], x[:length])
    first = lax.ppermute(first, GRP, [(0, 0), (1, 2), (2, 1), (3, 3)])
    second = lax.ppermute(second, GRP, [(2, 0), (0, 1), (3, 2), (1, 3)])
    return jnp.where(c == 0, jnp.stack([first, second]), jnp.stack([second, first]))


def body(
    tokens, segment, piece_start, w_query, w_key, w_value, w_out, w_gate, w_up, w_down, cotangent
):
    sizes = {"y": lax.axis_size("y"), "z": lax.axis_size("z"), "xl": lax.axis_size("xl")}
    width = tokens.shape[2]
    local_length = tokens.shape[1] * 2
    full_length = segment.shape[1]
    head_count = HEADS
    head_size = HDIM
    scale = head_size ** (-0.5)
    xh = lax.axis_index("xh")
    c = lax.axis_index("c")
    first_row = c * local_length
    rows = first_row + jnp.arange(local_length, dtype=jnp.int32)
    columns = jnp.arange(full_length, dtype=jnp.int32)
    inverse = 10000.0 ** (-jnp.arange(0, head_size, 2).astype(jnp.float32) / head_size)
    angles = rows.astype(jnp.float32)[:, None] * inverse[None, :]
    cosine = jnp.cos(angles)[:, None, :]
    sine = jnp.sin(angles)[:, None, :]

    shards = (w_query, w_key, w_value, w_out, w_gate, w_up, w_down)
    query_weight, key_weight, value_weight, out_weight, gate_weight, up_weight, down_weight = (
        gather_weights(shards, sizes)
    )

    hidden = to_sequence(tokens).astype(jnp.float32)
    grad_result = to_sequence(cotangent)
    seg_row = jnp.take(segment, xh, axis=0)
    start_row = jnp.take(piece_start, xh, axis=0)

    def swap_halves(mine):
        other = lax.ppermute(mine, "c", [(0, 1), (1, 0)])
        return jnp.where(c == 0, jnp.concatenate([mine, other]), jnp.concatenate([other, mine]))

    normed, norm_one_back = jax.vjp(layer_norm, hidden)
    normed_low = normed.astype(jnp.bfloat16)
    query_heads = rotate(
        matmul(normed_low, query_weight).reshape(local_length, head_count, head_size),
        cosine,
        sine,
    ).astype(jnp.bfloat16)
    keys = (
        rotate(
            matmul(normed_low, key_weight).reshape(local_length, head_count, head_size),
            cosine,
            sine,
        )
        .reshape(local_length, width)
        .astype(jnp.bfloat16)
    )
    values = matmul(normed_low, value_weight).astype(jnp.bfloat16)
    both = swap_halves(jnp.concatenate([keys, values], axis=1))
    key_heads = both[:, :width].reshape(full_length, head_count, head_size)
    value_heads = both[:, width:].reshape(full_length, head_count, head_size)
    seg_local = lax.dynamic_slice_in_dim(seg_row, first_row, local_length)
    start_local = lax.dynamic_slice_in_dim(start_row, first_row, local_length)
    causal = columns[None, :] <= rows[:, None]
    same_piece = start_local[:, None] == start_row[None, :]
    allowed = (seg_local[:, None] == seg_row[None, :]) & (causal | same_piece)

    def scores_of(heads_in):
        raw = jnp.einsum("qhd,khd->hqk", heads_in, key_heads, preferred_element_type=jnp.float32)
        return jnp.where(allowed[None], raw * scale, -1e30)

    scores = scores_of(query_heads)
    highest = jnp.max(scores, axis=-1, keepdims=True)
    expd = jnp.exp(scores - highest)
    total = jnp.sum(expd, axis=-1, keepdims=True)
    log_total = highest + jnp.log(total)
    probs_low = (expd / total).astype(jnp.bfloat16)
    mixed = jnp.einsum("hqk,khd->qhd", probs_low, value_heads, preferred_element_type=jnp.float32)
    mixed_low = mixed.reshape(local_length, width).astype(jnp.bfloat16)
    after = hidden + matmul(mixed_low, out_weight)
    normed_two, norm_two_back = jax.vjp(layer_norm, after)
    normed_two_low = normed_two.astype(jnp.bfloat16)
    gate = matmul(normed_two_low, gate_weight)
    upper = matmul(normed_two_low, up_weight)
    active, gate_back = jax.vjp(gated, gate, upper)
    active_low = active.astype(jnp.bfloat16)
    result = after + matmul(active_low, down_weight)
    output = from_sequence(result.astype(jnp.bfloat16))

    grads = [None] * 7
    grads[6] = contract_rows(active_low, grad_result)
    grad_active = contract_cols(grad_result, down_weight)
    grad_gate, grad_upper = gate_back(grad_active)
    gate_low = grad_gate.astype(jnp.bfloat16)
    upper_low = grad_upper.astype(jnp.bfloat16)
    grads[4] = contract_rows(normed_two_low, gate_low)
    grads[5] = contract_rows(normed_two_low, upper_low)
    grad_normed_two = contract_cols(gate_low, gate_weight) + contract_cols(upper_low, up_weight)
    grad_after = grad_result.astype(jnp.float32) + norm_two_back(grad_normed_two)[0]
    after_low = grad_after.astype(jnp.bfloat16)
    grads[3] = contract_rows(mixed_low, after_low)
    grad_mixed = (
        contract_cols(after_low, out_weight)
        .astype(jnp.bfloat16)
        .reshape(local_length, head_count, head_size)
    )
    probs = jnp.exp(scores_of(query_heads) - log_total)
    grad_probs = jnp.einsum("qhd,khd->hqk", grad_mixed, value_heads, preferred_element_type=jnp.float32)
    inner = jnp.sum(probs * grad_probs, axis=-1, keepdims=True)
    grad_raw = (probs * (grad_probs - inner) * scale).astype(jnp.bfloat16)
    grad_query = jnp.einsum("hqk,khd->qhd", grad_raw, key_heads, preferred_element_type=jnp.float32)
    again_low = probs.astype(jnp.bfloat16)
    grad_keys = jnp.einsum(
        "hqk,qhd->khd", grad_raw, query_heads, preferred_element_type=jnp.float32
    ).reshape(full_length, width)
    grad_values = jnp.einsum(
        "hqk,qhd->khd", again_low, grad_mixed, preferred_element_type=jnp.float32
    ).reshape(full_length, width)
    grad_kv = jnp.concatenate([grad_keys, grad_values], axis=1)
    mine_kv = jnp.where(c == 0, grad_kv[:local_length], grad_kv[local_length:])
    theirs_kv = jnp.where(c == 0, grad_kv[local_length:], grad_kv[:local_length])
    own_kv = mine_kv + lax.ppermute(theirs_kv, "c", [(0, 1), (1, 0)])
    own_keys = own_kv[:, :width]
    own_values = own_kv[:, width:]
    query_low = (
        rotate(grad_query, cosine, -sine).reshape(local_length, width).astype(jnp.bfloat16)
    )
    keys_low = (
        rotate(own_keys.reshape(local_length, head_count, head_size), cosine, -sine)
        .reshape(local_length, width)
        .astype(jnp.bfloat16)
    )
    values_low = own_values.astype(jnp.bfloat16)
    grads[0] = contract_rows(normed_low, query_low)
    grads[1] = contract_rows(normed_low, keys_low)
    grads[2] = contract_rows(normed_low, values_low)
    grad_normed = (
        contract_cols(query_low, query_weight)
        + contract_cols(keys_low, key_weight)
        + contract_cols(values_low, value_weight)
    )
    grad_hidden = grad_after + norm_one_back(grad_normed)[0]
    input_grads = from_sequence(grad_hidden.astype(jnp.bfloat16))

    owned = reduce_grads(grads[6:7], sizes)
    owned = reduce_grads(grads[4:6], sizes) + owned
    owned = reduce_grads(grads[3:4], sizes) + owned
    owned = reduce_grads(grads[0:3], sizes) + owned
    return (output, input_grads, *owned)


def solution(mesh):
    rep, grp = mesh.devices.shape
    side = int(round((rep // 2) ** 0.5))
    devices = mesh.devices.reshape(side, rep // (2 * side), 2, grp // 2, 2)
    fine = Mesh(devices, ("y", "z", "xl", "xh", "c"))
    seqs = P(REP, GRP, None)
    rows = P(GRP, None)
    placed = (seqs, P(REP, None), P(REP, None), rows, rows, rows, rows, rows, rows, rows, seqs)
    return jax.shard_map(
        body,
        mesh=fine,
        in_specs=placed,
        out_specs=(seqs, seqs, rows, rows, rows, rows, rows, rows, rows),
        check_vma=False,
    )
```

```python
import jax
import jax.numpy as jnp
from jax import lax
from jax.sharding import Mesh
from jax.sharding import PartitionSpec as P

HEADS = 12
HDIM = 64
REP = ("y", "z", "xl")
GRP = ("xh", "c")


def layer_norm(hidden):
    centred = hidden - jnp.mean(hidden, axis=-1, keepdims=True)
    spread = jnp.mean(centred * centred, axis=-1, keepdims=True)
    return centred * lax.rsqrt(spread + 1e-05)


def rotate(heads, cosine, sine):
    half = heads.shape[-1] // 2
    first = heads[..., :half]
    second = heads[..., half:]
    return jnp.concatenate(
        [first * cosine - second * sine, second * cosine + first * sine], axis=-1
    )


def gated(gate, upper):
    return gate / (1.0 + jnp.exp(-gate)) * upper


def matmul(left, right):
    return jnp.dot(left, right, preferred_element_type=jnp.float32)


def contract_rows(left, right):
    return lax.dot_general(
        left, right, (((0,), (0,)), ((), ())), preferred_element_type=jnp.float32
    )


def contract_cols(left, right):
    return lax.dot_general(
        left, right, (((1,), (1,)), ((), ())), preferred_element_type=jnp.float32
    )


def shift(x, axis, n, step):
    return lax.ppermute(x, axis, [(i, (i + step) % n) for i in range(n)])


def place(buf, piece, index, dim):
    start = [0] * buf.ndim
    start[dim] = index * piece.shape[dim]
    return lax.dynamic_update_slice(buf, piece, start)


def ring_gather(piece, axis, n, dim):
    if n == 1:
        return piece
    me = lax.axis_index(axis)
    shape = list(piece.shape)
    shape[dim] *= n
    buf = place(jnp.zeros(shape, piece.dtype), piece, me, dim)
    if n == 2:
        return place(buf, shift(piece, axis, 2, 1), 1 - me, dim)
    back = piece
    ahead = piece
    for step in range(1, n // 2 + 1):
        if step < n - step:
            back = shift(back, axis, n, 1)
            ahead = shift(ahead, axis, n, -1)
            buf = place(buf, back, (me - step) % n, dim)
            buf = place(buf, ahead, (me + step) % n, dim)
        else:
            half = piece.shape[dim] // 2
            first = shift(lax.slice_in_dim(back, 0, half, axis=dim), axis, n, 1)
            second = shift(lax.slice_in_dim(ahead, half, piece.shape[dim], axis=dim), axis, n, -1)
            buf = place(buf, jnp.concatenate([first, second], axis=dim), (me + step) % n, dim)
    return buf


def ring_reduce(x, axis, n, dim, hdim):
    if n == 1:
        return x
    me = lax.axis_index(axis)
    size = x.shape[dim] // n

    def chunk(k, part):
        return lax.dynamic_slice_in_dim(part, k * size, size, axis=dim)

    if n == 2:
        sent = shift(chunk(1 - me, x).astype(jnp.bfloat16), axis, 2, 1)
        return chunk(me, x) + sent.astype(jnp.float32)
    half = x.shape[hdim] // 2
    parts = []
    for direction, lo, hi in ((1, 0, half), (-1, half, x.shape[hdim])):
        part = lax.slice_in_dim(x, lo, hi, axis=hdim)
        acc = chunk((me - direction) % n, part)
        for step in range(n - 1):
            got = shift(acc.astype(jnp.bfloat16), axis, n, direction)
            acc = got.astype(jnp.float32) + chunk((me - direction * (step + 2)) % n, part)
        parts.append(acc)
    return jnp.concatenate(parts, axis=hdim)


def cross(x):
    return lax.ppermute(x, ("xl", "xh"), [(i, 3 - i) for i in range(4)])


def swap_core(x):
    return lax.ppermute(x, "c", [(0, 1), (1, 0)])


def absolute(parts, rows):
    g = lax.axis_index("xh") * 2 + lax.axis_index("c")
    buf = jnp.zeros((4 * rows,) + parts[0].shape[1:], parts[0].dtype)
    for j, part in enumerate(parts):
        buf = place(buf, part, jnp.bitwise_xor(g, j), 0)
    return buf


def gather_group(own, axis, n):
    size = own.shape[0] // n
    me = lax.axis_index(axis)
    mine = lax.dynamic_slice_in_dim(own, me * size, size, axis=0)
    other = ring_gather(cross(mine), axis, n, 0)
    partner = swap_core(jnp.concatenate([own, other]))
    rows = own.shape[0]
    return [own, partner[:rows], other, partner[rows:]]


def gather_weights(shards, sizes):
    w_query, w_key, w_value, w_out, w_gate, w_up, w_down = shards
    first = jnp.concatenate([w_query, w_key, w_value, w_out, w_down])
    second = jnp.concatenate([w_gate, w_up])
    first_parts = gather_group(first, "y", sizes["y"])
    second_parts = gather_group(second, "z", sizes["z"])
    out = []
    start = 0
    for s in (w_query, w_key, w_value, w_out, w_down):
        rows = s.shape[0]
        out.append(absolute([p[start:start + rows] for p in first_parts], rows))
        start += rows
    start = 0
    for s in (w_gate, w_up):
        rows = s.shape[0]
        out.append(absolute([p[start:start + rows] for p in second_parts], rows))
        start += rows
    q, k, v, o, d, gt, up = out
    return q, k, v, o, gt, up, d


def reduce_group(grads, axes, sizes):
    g = lax.axis_index("xh") * 2 + lax.axis_index("c")
    xl = lax.axis_index("xl")

    def shard(w, j):
        rows = w.shape[0] // 4
        return lax.dynamic_slice_in_dim(w, jnp.bitwise_xor(g, j) * rows, rows, axis=0)

    send = jnp.concatenate([shard(w, 1) for w in grads] + [shard(w, 3) for w in grads])
    got = swap_core(send.astype(jnp.bfloat16)).astype(jnp.float32)
    total = got.shape[0] // 2
    own = jnp.concatenate([shard(w, 0) for w in grads]) + got[:total]
    oth = jnp.concatenate([shard(w, 2) for w in grads]) + got[total:]
    pair = jnp.stack([own, oth])
    for axis, dim, hdim in axes:
        pair = ring_reduce(pair, axis, sizes[axis], dim, hdim)
    size = pair.shape[2] // 2
    own_keep = lax.dynamic_slice_in_dim(pair[0], xl * size, size, axis=1)
    own_send = lax.dynamic_slice_in_dim(pair[0], (1 - xl) * size, size, axis=1)
    oth_keep = lax.dynamic_slice_in_dim(pair[1], (1 - xl) * size, size, axis=1)
    oth_send = lax.dynamic_slice_in_dim(pair[1], xl * size, size, axis=1)
    got = lax.ppermute(
        jnp.stack([own_send, oth_send]).astype(jnp.bfloat16), "xl", [(0, 1), (1, 0)]
    ).astype(jnp.float32)
    mine = own_keep + got[0] + cross((oth_keep + got[1]).astype(jnp.bfloat16)).astype(jnp.float32)
    full = ring_gather(mine.astype(jnp.bfloat16), "xl", 2, 1)
    for axis, dim, _ in reversed(axes):
        full = ring_gather(full, axis, sizes[axis], dim - 1)
    out = []
    start = 0
    for w in grads:
        rows = w.shape[0] // 4
        out.append(full[start:start + rows].astype(jnp.float32))
        start += rows
    return out


def to_sequence(x):
    xh = lax.axis_index("xh")
    c = lax.axis_index("c")
    first = lax.ppermute(lax.dynamic_index_in_dim(x, c, 0, False), GRP, [(0, 0), (1, 2), (2, 1), (3, 3)])
    second = lax.ppermute(lax.dynamic_index_in_dim(x, 1 - c, 0, False), GRP, [(0, 2), (1, 0), (2, 3), (3, 1)])
    return jnp.where(xh == 0, jnp.concatenate([first, second]), jnp.concatenate([second, first]))


def from_sequence(x):
    xh = lax.axis_index("xh")
    c = lax.axis_index("c")
    length = x.shape[0] // 2
    first = jnp.where(xh == 0, x[:length], x[length:])
    second = jnp.where(xh == 0, x[length:], x[:length])
    first = lax.ppermute(first, GRP, [(0, 0), (1, 2), (2, 1), (3, 3)])
    second = lax.ppermute(second, GRP, [(2, 0), (0, 1), (3, 2), (1, 3)])
    return jnp.where(c == 0, jnp.stack([first, second]), jnp.stack([second, first]))


def body(
    tokens, segment, piece_start, w_query, w_key, w_value, w_out, w_gate, w_up, w_down, cotangent
):
    sizes = {"y": lax.axis_size("y"), "z": lax.axis_size("z"), "xl": lax.axis_size("xl")}
    width = tokens.shape[2]
    local_length = tokens.shape[1] * 2
    full_length = segment.shape[1]
    head_count = HEADS
    head_size = HDIM
    scale = head_size ** (-0.5)
    xh = lax.axis_index("xh")
    c = lax.axis_index("c")
    first_row = c * local_length
    rows = first_row + jnp.arange(local_length, dtype=jnp.int32)
    columns = jnp.arange(full_length, dtype=jnp.int32)
    inverse = 10000.0 ** (-jnp.arange(0, head_size, 2).astype(jnp.float32) / head_size)
    angles = rows.astype(jnp.float32)[:, None] * inverse[None, :]
    cosine = jnp.cos(angles)[:, None, :]
    sine = jnp.sin(angles)[:, None, :]

    shards = (w_query, w_key, w_value, w_out, w_gate, w_up, w_down)
    query_weight, key_weight, value_weight, out_weight, gate_weight, up_weight, down_weight = (
        gather_weights(shards, sizes)
    )

    hidden = to_sequence(tokens).astype(jnp.float32)
    grad_result = to_sequence(cotangent)
    seg_row = lax.dynamic_index_in_dim(segment, xh, 0, False)
    start_row = lax.dynamic_index_in_dim(piece_start, xh, 0, False)

    def swap_halves(mine):
        other = lax.ppermute(mine, "c", [(0, 1), (1, 0)])
        return jnp.where(c == 0, jnp.concatenate([mine, other]), jnp.concatenate([other, mine]))

    normed, norm_one_back = jax.vjp(layer_norm, hidden)
    normed_low = normed.astype(jnp.bfloat16)
    query_heads = rotate(
        matmul(normed_low, query_weight).reshape(local_length, head_count, head_size),
        cosine,
        sine,
    ).astype(jnp.bfloat16)
    keys = (
        rotate(
            matmul(normed_low, key_weight).reshape(local_length, head_count, head_size),
            cosine,
            sine,
        )
        .reshape(local_length, width)
        .astype(jnp.bfloat16)
    )
    values = matmul(normed_low, value_weight).astype(jnp.bfloat16)
    both = swap_halves(jnp.concatenate([keys, values], axis=1))
    key_heads = both[:, :width].reshape(full_length, head_count, head_size)
    value_heads = both[:, width:].reshape(full_length, head_count, head_size)
    seg_local = lax.dynamic_slice_in_dim(seg_row, first_row, local_length)
    start_local = lax.dynamic_slice_in_dim(start_row, first_row, local_length)
    causal = columns[None, :] <= rows[:, None]
    same_piece = start_local[:, None] == start_row[None, :]
    allowed = (seg_local[:, None] == seg_row[None, :]) & (causal | same_piece)

    def scores_of(heads_in):
        raw = jnp.einsum("qhd,khd->hqk", heads_in, key_heads, preferred_element_type=jnp.float32)
        return jnp.where(allowed[None], raw * scale, -1e30)

    scores = scores_of(query_heads)
    highest = jnp.max(scores, axis=-1, keepdims=True)
    expd = jnp.exp(scores - highest)
    total = jnp.sum(expd, axis=-1, keepdims=True)
    log_total = highest + jnp.log(total)
    probs_low = (expd / total).astype(jnp.bfloat16)
    mixed = jnp.einsum("hqk,khd->qhd", probs_low, value_heads, preferred_element_type=jnp.float32)
    mixed_low = mixed.reshape(local_length, width).astype(jnp.bfloat16)
    after = hidden + matmul(mixed_low, out_weight)
    normed_two, norm_two_back = jax.vjp(layer_norm, after)
    normed_two_low = normed_two.astype(jnp.bfloat16)
    gate = matmul(normed_two_low, gate_weight)
    upper = matmul(normed_two_low, up_weight)
    active, gate_back = jax.vjp(gated, gate, upper)
    active_low = active.astype(jnp.bfloat16)
    result = after + matmul(active_low, down_weight)
    output = from_sequence(result.astype(jnp.bfloat16))

    grads = [None] * 7
    grads[6] = contract_rows(active_low, grad_result)
    grad_active = contract_cols(grad_result, down_weight)
    grad_gate, grad_upper = gate_back(grad_active)
    gate_low = grad_gate.astype(jnp.bfloat16)
    upper_low = grad_upper.astype(jnp.bfloat16)
    grads[4] = contract_rows(normed_two_low, gate_low)
    grads[5] = contract_rows(normed_two_low, upper_low)
    grad_normed_two = contract_cols(gate_low, gate_weight) + contract_cols(upper_low, up_weight)
    grad_after = grad_result.astype(jnp.float32) + norm_two_back(grad_normed_two)[0]
    after_low = grad_after.astype(jnp.bfloat16)
    grads[3] = contract_rows(mixed_low, after_low)
    grad_mixed = (
        contract_cols(after_low, out_weight)
        .astype(jnp.bfloat16)
        .reshape(local_length, head_count, head_size)
    )
    probs = jnp.exp(scores_of(query_heads) - log_total)
    grad_probs = jnp.einsum("qhd,khd->hqk", grad_mixed, value_heads, preferred_element_type=jnp.float32)
    inner = jnp.sum(probs * grad_probs, axis=-1, keepdims=True)
    grad_raw = (probs * (grad_probs - inner) * scale).astype(jnp.bfloat16)
    grad_query = jnp.einsum("hqk,khd->qhd", grad_raw, key_heads, preferred_element_type=jnp.float32)
    again_low = probs.astype(jnp.bfloat16)
    grad_keys = jnp.einsum(
        "hqk,qhd->khd", grad_raw, query_heads, preferred_element_type=jnp.float32
    ).reshape(full_length, width)
    grad_values = jnp.einsum(
        "hqk,qhd->khd", again_low, grad_mixed, preferred_element_type=jnp.float32
    ).reshape(full_length, width)
    grad_kv = jnp.concatenate([grad_keys, grad_values], axis=1)
    mine_kv = jnp.where(c == 0, grad_kv[:local_length], grad_kv[local_length:])
    theirs_kv = jnp.where(c == 0, grad_kv[local_length:], grad_kv[:local_length])
    own_kv = mine_kv + lax.ppermute(theirs_kv, "c", [(0, 1), (1, 0)])
    own_keys = own_kv[:, :width]
    own_values = own_kv[:, width:]
    query_low = (
        rotate(grad_query, cosine, -sine).reshape(local_length, width).astype(jnp.bfloat16)
    )
    keys_low = (
        rotate(own_keys.reshape(local_length, head_count, head_size), cosine, -sine)
        .reshape(local_length, width)
        .astype(jnp.bfloat16)
    )
    values_low = own_values.astype(jnp.bfloat16)
    grads[0] = contract_rows(normed_low, query_low)
    grads[1] = contract_rows(normed_low, keys_low)
    grads[2] = contract_rows(normed_low, values_low)
    grad_normed = (
        contract_cols(query_low, query_weight)
        + contract_cols(keys_low, key_weight)
        + contract_cols(values_low, value_weight)
    )
    grad_hidden = grad_after + norm_one_back(grad_normed)[0]
    input_grads = from_sequence(grad_hidden.astype(jnp.bfloat16))

    wide = reduce_group([grads[4], grads[5]], (("y", 1, 2), ("z", 2, 1)), sizes)
    narrow = reduce_group(
        [grads[6], grads[3], grads[0], grads[1], grads[2]], (("y", 1, 2), ("z", 1, 2)), sizes
    )
    owned = [narrow[2], narrow[3], narrow[4], narrow[1], wide[0], wide[1], narrow[0]]
    return (output, input_grads, *owned)


def solution(mesh):
    rep, grp = mesh.devices.shape
    side = int(round((rep // 2) ** 0.5))
    devices = mesh.devices.reshape(side, rep // (2 * side), 2, grp // 2, 2)
    fine = Mesh(devices, ("y", "z", "xl", "xh", "c"))
    seqs = P(REP, GRP, None)
    rows = P(GRP, None)
    placed = (seqs, P(REP, None), P(REP, None), rows, rows, rows, rows, rows, rows, rows, seqs)
    return jax.shard_map(
        body,
        mesh=fine,
        in_specs=placed,
        out_specs=(seqs, seqs, rows, rows, rows, rows, rows, rows, rows),
        check_vma=False,
    )
```

```python
import jax
import jax.numpy as jnp
from jax import lax
from jax.sharding import Mesh
from jax.sharding import PartitionSpec as P

HEADS = 12
HDIM = 64
REP = ("y", "z", "xl")
GRP = ("xh", "c")


def layer_norm(hidden):
    centred = hidden - jnp.mean(hidden, axis=-1, keepdims=True)
    spread = jnp.mean(centred * centred, axis=-1, keepdims=True)
    return centred * lax.rsqrt(spread + 1e-05)


def rotate(heads, cosine, sine):
    half = heads.shape[-1] // 2
    first = heads[..., :half]
    second = heads[..., half:]
    return jnp.concatenate(
        [first * cosine - second * sine, second * cosine + first * sine], axis=-1
    )


def gated(gate, upper):
    return gate / (1.0 + jnp.exp(-gate)) * upper


def matmul(left, right):
    return jnp.dot(left, right, preferred_element_type=jnp.float32)


def contract_rows(left, right):
    return lax.dot_general(
        left, right, (((0,), (0,)), ((), ())), preferred_element_type=jnp.float32
    )


def contract_cols(left, right):
    return lax.dot_general(
        left, right, (((1,), (1,)), ((), ())), preferred_element_type=jnp.float32
    )


def shift(x, axis, n, step):
    return lax.ppermute(x, axis, [(i, (i + step) % n) for i in range(n)])


def place(buf, piece, index, dim):
    start = [0] * buf.ndim
    start[dim] = index * piece.shape[dim]
    return lax.dynamic_update_slice(buf, piece, start)


def ring_gather(piece, axis, n, dim):
    if n == 1:
        return piece
    me = lax.axis_index(axis)
    shape = list(piece.shape)
    shape[dim] *= n
    buf = place(jnp.zeros(shape, piece.dtype), piece, me, dim)
    if n == 2:
        return place(buf, shift(piece, axis, 2, 1), 1 - me, dim)
    back = piece
    ahead = piece
    for step in range(1, n // 2 + 1):
        if step < n - step:
            back = shift(back, axis, n, 1)
            ahead = shift(ahead, axis, n, -1)
            buf = place(buf, back, (me - step) % n, dim)
            buf = place(buf, ahead, (me + step) % n, dim)
        else:
            half = piece.shape[dim] // 2
            first = shift(lax.slice_in_dim(back, 0, half, axis=dim), axis, n, 1)
            second = shift(lax.slice_in_dim(ahead, half, piece.shape[dim], axis=dim), axis, n, -1)
            buf = place(buf, jnp.concatenate([first, second], axis=dim), (me + step) % n, dim)
    return buf


def ring_reduce(x, axis, n, dim, hdim):
    if n == 1:
        return x
    me = lax.axis_index(axis)
    size = x.shape[dim] // n

    def chunk(k, part):
        return lax.dynamic_slice_in_dim(part, k * size, size, axis=dim)

    if n == 2:
        sent = shift(chunk(1 - me, x).astype(jnp.bfloat16), axis, 2, 1)
        return chunk(me, x) + sent.astype(jnp.float32)
    half = x.shape[hdim] // 2
    parts = []
    for direction, lo, hi in ((1, 0, half), (-1, half, x.shape[hdim])):
        part = lax.slice_in_dim(x, lo, hi, axis=hdim)
        acc = chunk((me - direction) % n, part)
        for step in range(n - 1):
            got = shift(acc.astype(jnp.bfloat16), axis, n, direction)
            acc = got.astype(jnp.float32) + chunk((me - direction * (step + 2)) % n, part)
        parts.append(acc)
    return jnp.concatenate(parts, axis=hdim)


def cross(x):
    return lax.ppermute(x, ("xl", "xh"), [(i, 3 - i) for i in range(4)])


def swap_core(x):
    return lax.ppermute(x, "c", [(0, 1), (1, 0)])


def absolute(parts, rows):
    g = lax.axis_index("xh") * 2 + lax.axis_index("c")
    buf = jnp.zeros((4 * rows,) + parts[0].shape[1:], parts[0].dtype)
    for j, part in enumerate(parts):
        buf = place(buf, part, jnp.bitwise_xor(g, j), 0)
    return buf


def gather_group(own, axis, n):
    size = own.shape[0] // n
    me = lax.axis_index(axis)
    mine = lax.dynamic_slice_in_dim(own, me * size, size, axis=0)
    other = ring_gather(cross(mine), axis, n, 0)
    partner = swap_core(jnp.concatenate([own, other]))
    rows = own.shape[0]
    return [own, partner[:rows], other, partner[rows:]]


def gather_weights(shards, sizes):
    w_query, w_key, w_value, w_out, w_gate, w_up, w_down = shards
    plan = (
        ((w_query, w_key, w_value), "y"),
        ((w_out,), "z"),
        ((w_gate,), "y"),
        ((w_up,), "z"),
        ((w_down,), "z"),
    )
    out = []
    for group, axis in plan:
        parts = gather_group(jnp.concatenate(group) if len(group) > 1 else group[0], axis, sizes[axis])
        start = 0
        for s in group:
            rows = s.shape[0]
            out.append(absolute([p[start:start + rows] for p in parts], rows))
            start += rows
    return out


def reduce_group(grads, axes, sizes):
    g = lax.axis_index("xh") * 2 + lax.axis_index("c")
    xl = lax.axis_index("xl")

    def shard(w, j):
        rows = w.shape[0] // 4
        return lax.dynamic_slice_in_dim(w, jnp.bitwise_xor(g, j) * rows, rows, axis=0)

    send = jnp.concatenate([shard(w, 1) for w in grads] + [shard(w, 3) for w in grads])
    got = swap_core(send.astype(jnp.bfloat16)).astype(jnp.float32)
    total = got.shape[0] // 2
    own = jnp.concatenate([shard(w, 0) for w in grads]) + got[:total]
    oth = jnp.concatenate([shard(w, 2) for w in grads]) + got[total:]
    pair = jnp.stack([own, oth])
    for axis, dim, hdim in axes:
        pair = ring_reduce(pair, axis, sizes[axis], dim, hdim)
    size = pair.shape[2] // 2
    own_keep = lax.dynamic_slice_in_dim(pair[0], xl * size, size, axis=1)
    own_send = lax.dynamic_slice_in_dim(pair[0], (1 - xl) * size, size, axis=1)
    oth_keep = lax.dynamic_slice_in_dim(pair[1], (1 - xl) * size, size, axis=1)
    oth_send = lax.dynamic_slice_in_dim(pair[1], xl * size, size, axis=1)
    got = lax.ppermute(
        jnp.stack([own_send, oth_send]).astype(jnp.bfloat16), "xl", [(0, 1), (1, 0)]
    ).astype(jnp.float32)
    mine = own_keep + got[0] + cross((oth_keep + got[1]).astype(jnp.bfloat16)).astype(jnp.float32)
    full = ring_gather(mine.astype(jnp.bfloat16), "xl", 2, 1)
    for axis, dim, _ in reversed(axes):
        full = ring_gather(full, axis, sizes[axis], dim - 1)
    out = []
    start = 0
    for w in grads:
        rows = w.shape[0] // 4
        out.append(full[start:start + rows].astype(jnp.float32))
        start += rows
    return out


def to_sequence(x):
    xh = lax.axis_index("xh")
    c = lax.axis_index("c")
    first = lax.ppermute(lax.dynamic_index_in_dim(x, c, 0, False), GRP, [(0, 0), (1, 2), (2, 1), (3, 3)])
    second = lax.ppermute(lax.dynamic_index_in_dim(x, 1 - c, 0, False), GRP, [(0, 2), (1, 0), (2, 3), (3, 1)])
    return jnp.where(xh == 0, jnp.concatenate([first, second]), jnp.concatenate([second, first]))


def from_sequence(x):
    xh = lax.axis_index("xh")
    c = lax.axis_index("c")
    length = x.shape[0] // 2
    first = jnp.where(xh == 0, x[:length], x[length:])
    second = jnp.where(xh == 0, x[length:], x[:length])
    first = lax.ppermute(first, GRP, [(0, 0), (1, 2), (2, 1), (3, 3)])
    second = lax.ppermute(second, GRP, [(2, 0), (0, 1), (3, 2), (1, 3)])
    return jnp.where(c == 0, jnp.stack([first, second]), jnp.stack([second, first]))


def body(
    tokens, segment, piece_start, w_query, w_key, w_value, w_out, w_gate, w_up, w_down, cotangent
):
    sizes = {"y": lax.axis_size("y"), "z": lax.axis_size("z"), "xl": lax.axis_size("xl")}
    width = tokens.shape[2]
    local_length = tokens.shape[1] * 2
    full_length = segment.shape[1]
    head_count = HEADS
    head_size = HDIM
    scale = head_size ** (-0.5)
    xh = lax.axis_index("xh")
    c = lax.axis_index("c")
    first_row = c * local_length
    rows = first_row + jnp.arange(local_length, dtype=jnp.int32)
    columns = jnp.arange(full_length, dtype=jnp.int32)
    inverse = 10000.0 ** (-jnp.arange(0, head_size, 2).astype(jnp.float32) / head_size)
    angles = rows.astype(jnp.float32)[:, None] * inverse[None, :]
    cosine = jnp.cos(angles)[:, None, :]
    sine = jnp.sin(angles)[:, None, :]

    shards = (w_query, w_key, w_value, w_out, w_gate, w_up, w_down)
    query_weight, key_weight, value_weight, out_weight, gate_weight, up_weight, down_weight = (
        gather_weights(shards, sizes)
    )

    hidden = to_sequence(tokens).astype(jnp.float32)
    grad_result = to_sequence(cotangent)
    seg_row = lax.dynamic_index_in_dim(segment, xh, 0, False)
    start_row = lax.dynamic_index_in_dim(piece_start, xh, 0, False)

    def swap_halves(mine):
        other = lax.ppermute(mine, "c", [(0, 1), (1, 0)])
        return jnp.where(c == 0, jnp.concatenate([mine, other]), jnp.concatenate([other, mine]))

    normed, norm_one_back = jax.vjp(layer_norm, hidden)
    normed_low = normed.astype(jnp.bfloat16)
    query_heads = rotate(
        matmul(normed_low, query_weight).reshape(local_length, head_count, head_size),
        cosine,
        sine,
    ).astype(jnp.bfloat16)
    keys = (
        rotate(
            matmul(normed_low, key_weight).reshape(local_length, head_count, head_size),
            cosine,
            sine,
        )
        .reshape(local_length, width)
        .astype(jnp.bfloat16)
    )
    values = matmul(normed_low, value_weight).astype(jnp.bfloat16)
    both = swap_halves(jnp.concatenate([keys, values], axis=1))
    def heads(x, length):
        return x.reshape(length, head_count, head_size).transpose(1, 0, 2)

    def unheads(x):
        return x.transpose(1, 0, 2).reshape(x.shape[1], width)

    key_heads = heads(both[:, :width], full_length)
    value_heads = heads(both[:, width:], full_length)
    query_major = heads(query_heads.reshape(local_length, width), local_length)
    seg_local = lax.dynamic_slice_in_dim(seg_row, first_row, local_length)
    start_local = lax.dynamic_slice_in_dim(start_row, first_row, local_length)
    causal = columns[None, :] <= rows[:, None]
    same_piece = start_local[:, None] == start_row[None, :]
    allowed = (seg_local[:, None] == seg_row[None, :]) & (causal | same_piece)

    def scores_of(heads_in):
        raw = jnp.einsum("hqd,hkd->hqk", heads_in, key_heads, preferred_element_type=jnp.float32)
        return jnp.where(allowed[None], raw * scale, -1e30)

    scores = scores_of(query_major)
    highest = jnp.max(scores, axis=-1, keepdims=True)
    expd = jnp.exp(scores - highest)
    total = jnp.sum(expd, axis=-1, keepdims=True)
    log_total = highest + jnp.log(total)
    probs_low = lax.optimization_barrier((expd / total).astype(jnp.bfloat16))
    mixed = unheads(
        jnp.einsum("hqk,hkd->hqd", probs_low, value_heads, preferred_element_type=jnp.float32)
    )
    mixed_low = mixed.reshape(local_length, width).astype(jnp.bfloat16)
    after = hidden + matmul(mixed_low, out_weight)
    normed_two, norm_two_back = jax.vjp(layer_norm, after)
    normed_two_low = normed_two.astype(jnp.bfloat16)
    gate = matmul(normed_two_low, gate_weight)
    upper = matmul(normed_two_low, up_weight)
    active, gate_back = jax.vjp(gated, gate, upper)
    active_low = active.astype(jnp.bfloat16)
    result = after + matmul(active_low, down_weight)
    output = from_sequence(result.astype(jnp.bfloat16))

    grads = [None] * 7
    grads[6] = contract_rows(active_low, grad_result)
    grad_active = contract_cols(grad_result, down_weight)
    grad_gate, grad_upper = gate_back(grad_active)
    gate_low = grad_gate.astype(jnp.bfloat16)
    upper_low = grad_upper.astype(jnp.bfloat16)
    grads[4] = contract_rows(normed_two_low, gate_low)
    grads[5] = contract_rows(normed_two_low, upper_low)
    grad_normed_two = contract_cols(gate_low, gate_weight) + contract_cols(upper_low, up_weight)
    grad_after = grad_result.astype(jnp.float32) + norm_two_back(grad_normed_two)[0]
    after_low = grad_after.astype(jnp.bfloat16)
    grads[3] = contract_rows(mixed_low, after_low)
    grad_mixed = (
        contract_cols(after_low, out_weight)
        .astype(jnp.bfloat16)
        .reshape(local_length, head_count, head_size)
    )
    mixed_major = heads(grad_mixed.reshape(local_length, width), local_length)
    probs = jnp.exp(scores_of(query_major) - log_total)
    grad_probs = jnp.einsum(
        "hqd,hkd->hqk", mixed_major, value_heads, preferred_element_type=jnp.float32
    )
    inner = jnp.sum(probs * grad_probs, axis=-1, keepdims=True)
    grad_raw = lax.optimization_barrier((probs * (grad_probs - inner) * scale).astype(jnp.bfloat16))
    grad_query = unheads(
        jnp.einsum("hqk,hkd->hqd", grad_raw, key_heads, preferred_element_type=jnp.float32)
    ).reshape(local_length, head_count, head_size)
    grad_keys = unheads(
        jnp.einsum("hqk,hqd->hkd", grad_raw, query_major, preferred_element_type=jnp.float32)
    )
    grad_values = unheads(
        jnp.einsum("hqk,hqd->hkd", probs_low, mixed_major, preferred_element_type=jnp.float32)
    )
    grad_kv = jnp.concatenate([grad_keys, grad_values], axis=1)
    mine_kv = jnp.where(c == 0, grad_kv[:local_length], grad_kv[local_length:])
    theirs_kv = jnp.where(c == 0, grad_kv[local_length:], grad_kv[:local_length])
    own_kv = mine_kv + lax.ppermute(theirs_kv, "c", [(0, 1), (1, 0)])
    own_keys = own_kv[:, :width]
    own_values = own_kv[:, width:]
    query_low = (
        rotate(grad_query, cosine, -sine).reshape(local_length, width).astype(jnp.bfloat16)
    )
    keys_low = (
        rotate(own_keys.reshape(local_length, head_count, head_size), cosine, -sine)
        .reshape(local_length, width)
        .astype(jnp.bfloat16)
    )
    values_low = own_values.astype(jnp.bfloat16)
    grads[0] = contract_rows(normed_low, query_low)
    grads[1] = contract_rows(normed_low, keys_low)
    grads[2] = contract_rows(normed_low, values_low)
    grad_normed = (
        contract_cols(query_low, query_weight)
        + contract_cols(keys_low, key_weight)
        + contract_cols(values_low, value_weight)
    )
    grad_hidden = grad_after + norm_one_back(grad_normed)[0]
    input_grads = from_sequence(grad_hidden.astype(jnp.bfloat16))

    yz = (("y", 1, 2), ("z", 1, 2))
    zy = (("z", 1, 2), ("y", 1, 2))
    down = reduce_group([grads[6]], yz, sizes)
    gate = reduce_group([grads[4]], zy, sizes)
    up = reduce_group([grads[5]], yz, sizes)
    out = reduce_group([grads[3]], zy, sizes)
    qkv = reduce_group([grads[0], grads[1], grads[2]], yz, sizes)
    owned = [qkv[0], qkv[1], qkv[2], out[0], gate[0], up[0], down[0]]
    return (output, input_grads, *owned)


def solution(mesh):
    rep, grp = mesh.devices.shape
    side = int(round((rep // 2) ** 0.5))
    devices = mesh.devices.reshape(side, rep // (2 * side), 2, grp // 2, 2)
    fine = Mesh(devices, ("y", "z", "xl", "xh", "c"))
    seqs = P(REP, GRP, None)
    rows = P(GRP, None)
    placed = (seqs, P(REP, None), P(REP, None), rows, rows, rows, rows, rows, rows, rows, seqs)
    return jax.shard_map(
        body,
        mesh=fine,
        in_specs=placed,
        out_specs=(seqs, seqs, rows, rows, rows, rows, rows, rows, rows),
        check_vma=False,
    )
```

```python
import jax
import jax.numpy as jnp
from jax import lax
from jax.sharding import Mesh
from jax.sharding import PartitionSpec as P

HEADS = 12
HDIM = 64
REP = ("y", "z", "xl")
GRP = ("xh", "c")


def layer_norm(hidden):
    centred = hidden - jnp.mean(hidden, axis=-1, keepdims=True)
    spread = jnp.mean(centred * centred, axis=-1, keepdims=True)
    return centred * lax.rsqrt(spread + 1e-05)


def rotate(heads, cosine, sine):
    half = heads.shape[-1] // 2
    first = heads[..., :half]
    second = heads[..., half:]
    return jnp.concatenate(
        [first * cosine - second * sine, second * cosine + first * sine], axis=-1
    )


def gated(gate, upper):
    return gate / (1.0 + jnp.exp(-gate)) * upper


def matmul(left, right):
    return jnp.dot(left, right, preferred_element_type=jnp.float32)


def contract_rows(left, right):
    return lax.dot_general(
        left, right, (((0,), (0,)), ((), ())), preferred_element_type=jnp.float32
    )


def contract_cols(left, right):
    return lax.dot_general(
        left, right, (((1,), (1,)), ((), ())), preferred_element_type=jnp.float32
    )


def shift(x, axis, n, step):
    return lax.ppermute(x, axis, [(i, (i + step) % n) for i in range(n)])


def place(buf, piece, index, dim):
    start = [0] * buf.ndim
    start[dim] = index * piece.shape[dim]
    return lax.dynamic_update_slice(buf, piece, start)


def ring_gather(piece, axis, n, dim, direct=False):
    if n == 1:
        return piece
    me = lax.axis_index(axis)
    shape = list(piece.shape)
    shape[dim] *= n
    buf = place(jnp.zeros(shape, piece.dtype), piece, me, dim)
    if n == 2 or direct:
        for k in range(1, n):
            buf = place(buf, shift(piece, axis, n, k), (me - k) % n, dim)
        return buf
    back = piece
    ahead = piece
    for step in range(1, n // 2 + 1):
        if step < n - step:
            back = shift(back, axis, n, 1)
            ahead = shift(ahead, axis, n, -1)
            buf = place(buf, back, (me - step) % n, dim)
            buf = place(buf, ahead, (me + step) % n, dim)
        else:
            half = piece.shape[dim] // 2
            first = shift(lax.slice_in_dim(back, 0, half, axis=dim), axis, n, 1)
            second = shift(lax.slice_in_dim(ahead, half, piece.shape[dim], axis=dim), axis, n, -1)
            buf = place(buf, jnp.concatenate([first, second], axis=dim), (me + step) % n, dim)
    return buf


def ring_reduce(x, axis, n, dim, hdim, direct=False):
    if n == 1:
        return x
    me = lax.axis_index(axis)
    size = x.shape[dim] // n

    def chunk(k):
        return lax.dynamic_slice_in_dim(x, (k % n) * size, size, axis=dim)

    def low(v):
        return v.astype(jnp.bfloat16)

    if n == 2 or direct:
        acc = chunk(me)
        for k in range(1, n):
            acc = acc + shift(low(chunk(me + k)), axis, n, k).astype(jnp.float32)
        return acc
    assert n == 4
    half = x.shape[hdim] // 2

    def part(k, which):
        c = chunk(k)
        return lax.slice_in_dim(c, 0, half, axis=hdim) if which == 0 else lax.slice_in_dim(
            c, half, c.shape[hdim], axis=hdim
        )

    from_ahead = shift(low(jnp.stack([part(me - 2, 0), part(me - 1, 1)])), axis, n, -1)
    from_back = shift(low(jnp.stack([part(me + 2, 1), part(me + 1, 0)])), axis, n, 1)
    relay_ahead = shift(low(from_ahead[0].astype(jnp.float32) + part(me - 1, 0)), axis, n, -1)
    relay_back = shift(low(from_back[0].astype(jnp.float32) + part(me + 1, 1)), axis, n, 1)
    first = part(me, 0) + from_back[1].astype(jnp.float32) + relay_ahead.astype(jnp.float32)
    second = part(me, 1) + from_ahead[1].astype(jnp.float32) + relay_back.astype(jnp.float32)
    return jnp.concatenate([first, second], axis=hdim)


def cross(x):
    return lax.ppermute(x, ("xl", "xh"), [(i, 3 - i) for i in range(4)])


def swap_core(x):
    return lax.ppermute(x, "c", [(0, 1), (1, 0)])


def absolute(parts, rows):
    g = lax.axis_index("xh") * 2 + lax.axis_index("c")
    buf = jnp.zeros((4 * rows,) + parts[0].shape[1:], parts[0].dtype)
    for j, part in enumerate(parts):
        buf = place(buf, part, jnp.bitwise_xor(g, j), 0)
    return buf


def gather_group(own, axis, n, direct):
    size = own.shape[0] // n
    me = lax.axis_index(axis)
    mine = lax.dynamic_slice_in_dim(own, me * size, size, axis=0)
    other = ring_gather(cross(mine), axis, n, 0, direct)
    partner = swap_core(jnp.concatenate([own, other]))
    rows = own.shape[0]
    return [own, partner[:rows], other, partner[rows:]]


def gather_weights(shards, sizes):
    w_query, w_key, w_value, w_out, w_gate, w_up, w_down = shards
    plan = (
        ((w_query, w_key, w_value), "y", True),
        ((w_out, w_down), "z", False),
        ((w_gate, w_up), "y", False),
    )
    out = {}
    for group, axis, direct in plan:
        parts = gather_group(jnp.concatenate(group), axis, sizes[axis], direct)
        start = 0
        for s in group:
            rows = s.shape[0]
            out[id(s)] = absolute([p[start:start + rows] for p in parts], rows)
            start += rows
    return [out[id(s)] for s in shards]


def reduce_group(grads, sizes, direct):
    g = lax.axis_index("xh") * 2 + lax.axis_index("c")

    def shard(w, j):
        rows = w.shape[0] // 4
        return lax.dynamic_slice_in_dim(w, jnp.bitwise_xor(g, j) * rows, rows, axis=0)

    send = jnp.concatenate([shard(w, 1) for w in grads] + [shard(w, 3) for w in grads])
    got = swap_core(send.astype(jnp.bfloat16)).astype(jnp.float32)
    total = got.shape[0] // 2
    own = jnp.concatenate([shard(w, 0) for w in grads]) + got[:total]
    oth = jnp.concatenate([shard(w, 2) for w in grads]) + got[total:]
    pair = jnp.stack([own, oth])
    pair = ring_reduce(pair, "y", sizes["y"], 1, 2, direct)
    pair = ring_reduce(pair, "z", sizes["z"], 1, 2, direct)
    low = pair.astype(jnp.bfloat16)
    mine = (
        pair[0]
        + lax.ppermute(low[0], "xl", [(0, 1), (1, 0)]).astype(jnp.float32)
        + cross(low[1]).astype(jnp.float32)
        + lax.ppermute(low[1], "xh", [(0, 1), (1, 0)]).astype(jnp.float32)
    )
    full = ring_gather(mine.astype(jnp.bfloat16), "z", sizes["z"], 0, direct)
    full = ring_gather(full, "y", sizes["y"], 0, direct)
    out = []
    start = 0
    for w in grads:
        rows = w.shape[0] // 4
        out.append(full[start:start + rows].astype(jnp.float32))
        start += rows
    return out


def to_sequence(x):
    xh = lax.axis_index("xh")
    c = lax.axis_index("c")
    first = lax.ppermute(lax.dynamic_index_in_dim(x, c, 0, False), GRP, [(0, 0), (1, 2), (2, 1), (3, 3)])
    second = lax.ppermute(lax.dynamic_index_in_dim(x, 1 - c, 0, False), GRP, [(0, 2), (1, 0), (2, 3), (3, 1)])
    return jnp.where(xh == 0, jnp.concatenate([first, second]), jnp.concatenate([second, first]))


def from_sequence(x):
    xh = lax.axis_index("xh")
    c = lax.axis_index("c")
    length = x.shape[0] // 2
    first = jnp.where(xh == 0, x[:length], x[length:])
    second = jnp.where(xh == 0, x[length:], x[:length])
    first = lax.ppermute(first, GRP, [(0, 0), (1, 2), (2, 1), (3, 3)])
    second = lax.ppermute(second, GRP, [(2, 0), (0, 1), (3, 2), (1, 3)])
    return jnp.where(c == 0, jnp.stack([first, second]), jnp.stack([second, first]))


def body(
    tokens, segment, piece_start, w_query, w_key, w_value, w_out, w_gate, w_up, w_down, cotangent
):
    sizes = {"y": lax.axis_size("y"), "z": lax.axis_size("z"), "xl": lax.axis_size("xl")}
    width = tokens.shape[2]
    local_length = tokens.shape[1] * 2
    full_length = segment.shape[1]
    head_count = HEADS
    head_size = HDIM
    scale = head_size ** (-0.5)
    xh = lax.axis_index("xh")
    c = lax.axis_index("c")
    first_row = c * local_length
    rows = first_row + jnp.arange(local_length, dtype=jnp.int32)
    columns = jnp.arange(full_length, dtype=jnp.int32)
    inverse = 10000.0 ** (-jnp.arange(0, head_size, 2).astype(jnp.float32) / head_size)
    angles = rows.astype(jnp.float32)[:, None] * inverse[None, :]
    cosine = jnp.cos(angles)[:, None, :]
    sine = jnp.sin(angles)[:, None, :]

    shards = (w_query, w_key, w_value, w_out, w_gate, w_up, w_down)
    query_weight, key_weight, value_weight, out_weight, gate_weight, up_weight, down_weight = (
        gather_weights(shards, sizes)
    )

    hidden = to_sequence(tokens).astype(jnp.float32)
    grad_result = to_sequence(cotangent)
    seg_row = lax.dynamic_index_in_dim(segment, xh, 0, False)
    start_row = lax.dynamic_index_in_dim(piece_start, xh, 0, False)

    def swap_halves(mine):
        other = lax.ppermute(mine, "c", [(0, 1), (1, 0)])
        return jnp.where(c == 0, jnp.concatenate([mine, other]), jnp.concatenate([other, mine]))

    normed, norm_one_back = jax.vjp(layer_norm, hidden)
    normed_low = normed.astype(jnp.bfloat16)
    query_heads = rotate(
        matmul(normed_low, query_weight).reshape(local_length, head_count, head_size),
        cosine,
        sine,
    ).astype(jnp.bfloat16)
    keys = (
        rotate(
            matmul(normed_low, key_weight).reshape(local_length, head_count, head_size),
            cosine,
            sine,
        )
        .reshape(local_length, width)
        .astype(jnp.bfloat16)
    )
    values = matmul(normed_low, value_weight).astype(jnp.bfloat16)
    both = swap_halves(jnp.concatenate([keys, values], axis=1))
    def heads(x, length):
        return x.reshape(length, head_count, head_size).transpose(1, 0, 2)

    def unheads(x):
        return x.transpose(1, 0, 2).reshape(x.shape[1], width)

    key_heads = heads(both[:, :width], full_length)
    value_heads = heads(both[:, width:], full_length)
    query_major = heads(query_heads.reshape(local_length, width), local_length)
    seg_local = lax.dynamic_slice_in_dim(seg_row, first_row, local_length)
    start_local = lax.dynamic_slice_in_dim(start_row, first_row, local_length)
    causal = columns[None, :] <= rows[:, None]
    same_piece = start_local[:, None] == start_row[None, :]
    allowed = (seg_local[:, None] == seg_row[None, :]) & (causal | same_piece)

    def scores_of(heads_in):
        raw = jnp.einsum("hqd,hkd->hqk", heads_in, key_heads, preferred_element_type=jnp.float32)
        return jnp.where(allowed[None], raw * scale, -1e30)

    scores = scores_of(query_major)
    highest = jnp.max(scores, axis=-1, keepdims=True)
    expd = jnp.exp(scores - highest)
    total = jnp.sum(expd, axis=-1, keepdims=True)
    log_total = highest + jnp.log(total)
    probs_low = lax.optimization_barrier((expd / total).astype(jnp.bfloat16))
    mixed = unheads(
        jnp.einsum("hqk,hkd->hqd", probs_low, value_heads, preferred_element_type=jnp.float32)
    )
    mixed_low = mixed.reshape(local_length, width).astype(jnp.bfloat16)
    after = hidden + matmul(mixed_low, out_weight)
    normed_two, norm_two_back = jax.vjp(layer_norm, after)
    normed_two_low = normed_two.astype(jnp.bfloat16)
    gate = matmul(normed_two_low, gate_weight)
    upper = matmul(normed_two_low, up_weight)
    active, gate_back = jax.vjp(gated, gate, upper)
    active_low = active.astype(jnp.bfloat16)
    result = after + matmul(active_low, down_weight)
    output = from_sequence(result.astype(jnp.bfloat16))

    grads = [None] * 7
    grads[6] = contract_rows(active_low, grad_result)
    grad_active = contract_cols(grad_result, down_weight)
    grad_gate, grad_upper = gate_back(grad_active)
    gate_low = grad_gate.astype(jnp.bfloat16)
    upper_low = grad_upper.astype(jnp.bfloat16)
    grads[4] = contract_rows(normed_two_low, gate_low)
    grads[5] = contract_rows(normed_two_low, upper_low)
    grad_normed_two = contract_cols(gate_low, gate_weight) + contract_cols(upper_low, up_weight)
    grad_after = grad_result.astype(jnp.float32) + norm_two_back(grad_normed_two)[0]
    after_low = grad_after.astype(jnp.bfloat16)
    grads[3] = contract_rows(mixed_low, after_low)
    grad_mixed = (
        contract_cols(after_low, out_weight)
        .astype(jnp.bfloat16)
        .reshape(local_length, head_count, head_size)
    )
    mixed_major = heads(grad_mixed.reshape(local_length, width), local_length)
    probs = jnp.exp(scores_of(query_major) - log_total)
    grad_probs = jnp.einsum(
        "hqd,hkd->hqk", mixed_major, value_heads, preferred_element_type=jnp.float32
    )
    inner = jnp.sum(probs * grad_probs, axis=-1, keepdims=True)
    grad_raw = lax.optimization_barrier((probs * (grad_probs - inner) * scale).astype(jnp.bfloat16))
    grad_query = unheads(
        jnp.einsum("hqk,hkd->hqd", grad_raw, key_heads, preferred_element_type=jnp.float32)
    ).reshape(local_length, head_count, head_size)
    grad_keys = unheads(
        jnp.einsum("hqk,hqd->hkd", grad_raw, query_major, preferred_element_type=jnp.float32)
    )
    grad_values = unheads(
        jnp.einsum("hqk,hqd->hkd", probs_low, mixed_major, preferred_element_type=jnp.float32)
    )
    grad_kv = jnp.concatenate([grad_keys, grad_values], axis=1)
    mine_kv = jnp.where(c == 0, grad_kv[:local_length], grad_kv[local_length:])
    theirs_kv = jnp.where(c == 0, grad_kv[local_length:], grad_kv[:local_length])
    own_kv = mine_kv + lax.ppermute(theirs_kv, "c", [(0, 1), (1, 0)])
    own_keys = own_kv[:, :width]
    own_values = own_kv[:, width:]
    query_low = (
        rotate(grad_query, cosine, -sine).reshape(local_length, width).astype(jnp.bfloat16)
    )
    keys_low = (
        rotate(own_keys.reshape(local_length, head_count, head_size), cosine, -sine)
        .reshape(local_length, width)
        .astype(jnp.bfloat16)
    )
    values_low = own_values.astype(jnp.bfloat16)
    grads[0] = contract_rows(normed_low, query_low)
    grads[1] = contract_rows(normed_low, keys_low)
    grads[2] = contract_rows(normed_low, values_low)
    grad_normed = (
        contract_cols(query_low, query_weight)
        + contract_cols(keys_low, key_weight)
        + contract_cols(values_low, value_weight)
    )
    grad_hidden = grad_after + norm_one_back(grad_normed)[0]
    input_grads = from_sequence(grad_hidden.astype(jnp.bfloat16))

    width = grads[6].shape[1]
    gate_rows = grads[4].shape[0]
    early = reduce_group(
        [grads[6], grads[4].reshape(-1, width), grads[5].reshape(-1, width), grads[3]], sizes, False
    )
    late = reduce_group([grads[0], grads[1], grads[2]], sizes, True)
    gate_grad = early[1].reshape(gate_rows // 4, -1)
    up_grad = early[2].reshape(gate_rows // 4, -1)
    owned = [late[0], late[1], late[2], early[3], gate_grad, up_grad, early[0]]
    return (output, input_grads, *owned)


def solution(mesh):
    rep, grp = mesh.devices.shape
    side = int(round((rep // 2) ** 0.5))
    devices = mesh.devices.reshape(side, rep // (2 * side), 2, grp // 2, 2)
    fine = Mesh(devices, ("y", "z", "xl", "xh", "c"))
    seqs = P(REP, GRP, None)
    rows = P(GRP, None)
    placed = (seqs, P(REP, None), P(REP, None), rows, rows, rows, rows, rows, rows, rows, seqs)
    return jax.shard_map(
        body,
        mesh=fine,
        in_specs=placed,
        out_specs=(seqs, seqs, rows, rows, rows, rows, rows, rows, rows),
        check_vma=False,
    )
```

```python
import jax
import jax.numpy as jnp
from jax import lax
from jax.sharding import Mesh
from jax.sharding import PartitionSpec as P

HEADS = 12
HDIM = 64
REP = ("y", "z", "xl")
GRP = ("xh", "c")


def layer_norm(hidden):
    centred = hidden - jnp.mean(hidden, axis=-1, keepdims=True)
    spread = jnp.mean(centred * centred, axis=-1, keepdims=True)
    return centred * lax.rsqrt(spread + 1e-05)


def rotate(heads, cosine, sine):
    half = heads.shape[-1] // 2
    first = heads[..., :half]
    second = heads[..., half:]
    return jnp.concatenate(
        [first * cosine - second * sine, second * cosine + first * sine], axis=-1
    )


def gated(gate, upper):
    return gate / (1.0 + jnp.exp(-gate)) * upper


def matmul(left, right):
    return jnp.dot(left, right, preferred_element_type=jnp.float32)


def contract_rows(left, right):
    return lax.dot_general(
        left, right, (((0,), (0,)), ((), ())), preferred_element_type=jnp.float32
    )


def contract_cols(left, right):
    return lax.dot_general(
        left, right, (((1,), (1,)), ((), ())), preferred_element_type=jnp.float32
    )


def shift(x, axis, n, step):
    return lax.ppermute(x, axis, [(i, (i + step) % n) for i in range(n)])


def place(buf, piece, index, dim):
    start = [0] * buf.ndim
    start[dim] = index * piece.shape[dim]
    return lax.dynamic_update_slice(buf, piece, start)


def ring_gather(piece, axis, n, dim, direct=False):
    if n == 1:
        return piece
    me = lax.axis_index(axis)
    shape = list(piece.shape)
    shape[dim] *= n
    buf = place(jnp.zeros(shape, piece.dtype), piece, me, dim)
    if n == 2 or direct:
        for k in range(1, n):
            buf = place(buf, shift(piece, axis, n, k), (me - k) % n, dim)
        return buf
    back = piece
    ahead = piece
    for step in range(1, n // 2 + 1):
        if step < n - step:
            back = shift(back, axis, n, 1)
            ahead = shift(ahead, axis, n, -1)
            buf = place(buf, back, (me - step) % n, dim)
            buf = place(buf, ahead, (me + step) % n, dim)
        else:
            half = piece.shape[dim] // 2
            first = shift(lax.slice_in_dim(back, 0, half, axis=dim), axis, n, 1)
            second = shift(lax.slice_in_dim(ahead, half, piece.shape[dim], axis=dim), axis, n, -1)
            buf = place(buf, jnp.concatenate([first, second], axis=dim), (me + step) % n, dim)
    return buf


def ring_reduce(x, axis, n, dim, hdim, direct=False):
    if n == 1:
        return x
    me = lax.axis_index(axis)
    size = x.shape[dim] // n

    def chunk(k):
        return lax.dynamic_slice_in_dim(x, (k % n) * size, size, axis=dim)

    def low(v):
        return v.astype(jnp.bfloat16)

    if n == 2 or direct:
        acc = chunk(me)
        for k in range(1, n):
            acc = acc + shift(low(chunk(me + k)), axis, n, k).astype(jnp.float32)
        return acc
    assert n == 4
    half = x.shape[hdim] // 2

    def part(k, which):
        c = chunk(k)
        return lax.slice_in_dim(c, 0, half, axis=hdim) if which == 0 else lax.slice_in_dim(
            c, half, c.shape[hdim], axis=hdim
        )

    from_ahead = shift(low(jnp.stack([part(me - 2, 0), part(me - 1, 1)])), axis, n, -1)
    from_back = shift(low(jnp.stack([part(me + 2, 1), part(me + 1, 0)])), axis, n, 1)
    relay_ahead = shift(low(from_ahead[0].astype(jnp.float32) + part(me - 1, 0)), axis, n, -1)
    relay_back = shift(low(from_back[0].astype(jnp.float32) + part(me + 1, 1)), axis, n, 1)
    first = part(me, 0) + from_back[1].astype(jnp.float32) + relay_ahead.astype(jnp.float32)
    second = part(me, 1) + from_ahead[1].astype(jnp.float32) + relay_back.astype(jnp.float32)
    return jnp.concatenate([first, second], axis=hdim)


def cross(x):
    return lax.ppermute(x, ("xl", "xh"), [(i, 3 - i) for i in range(4)])


def swap_core(x):
    return lax.ppermute(x, "c", [(0, 1), (1, 0)])


def absolute(parts, rows):
    g = lax.axis_index("xh") * 2 + lax.axis_index("c")
    buf = jnp.zeros((4 * rows,) + parts[0].shape[1:], parts[0].dtype)
    for j, part in enumerate(parts):
        buf = place(buf, part, jnp.bitwise_xor(g, j), 0)
    return buf


def gather_group(own, axis, n, direct):
    size = own.shape[0] // n
    me = lax.axis_index(axis)
    mine = lax.dynamic_slice_in_dim(own, me * size, size, axis=0)
    other = ring_gather(cross(mine), axis, n, 0, direct)
    partner = swap_core(jnp.concatenate([own, other]))
    rows = own.shape[0]
    return [own, partner[:rows], other, partner[rows:]]


def gather_weights(group, axis, sizes, direct):
    parts = gather_group(jnp.concatenate(group), axis, sizes[axis], direct)
    out = []
    start = 0
    for s in group:
        rows = s.shape[0]
        out.append(absolute([p[start:start + rows] for p in parts], rows))
        start += rows
    return out


def reduce_group(grads, sizes, direct):
    g = lax.axis_index("xh") * 2 + lax.axis_index("c")

    def shard(w, j):
        rows = w.shape[0] // 4
        return lax.dynamic_slice_in_dim(w, jnp.bitwise_xor(g, j) * rows, rows, axis=0)

    send = jnp.concatenate([shard(w, 1) for w in grads] + [shard(w, 3) for w in grads])
    got = swap_core(send.astype(jnp.bfloat16)).astype(jnp.float32)
    total = got.shape[0] // 2
    own = jnp.concatenate([shard(w, 0) for w in grads]) + got[:total]
    oth = jnp.concatenate([shard(w, 2) for w in grads]) + got[total:]
    pair = jnp.stack([own, oth])
    pair = ring_reduce(pair, "y", sizes["y"], 1, 2, direct)
    pair = ring_reduce(pair, "z", sizes["z"], 1, 2, direct)
    low = pair.astype(jnp.bfloat16)
    mine = (
        pair[0]
        + lax.ppermute(low[0], "xl", [(0, 1), (1, 0)]).astype(jnp.float32)
        + cross(low[1]).astype(jnp.float32)
        + lax.ppermute(low[1], "xh", [(0, 1), (1, 0)]).astype(jnp.float32)
    )
    full = ring_gather(mine.astype(jnp.bfloat16), "z", sizes["z"], 0, direct)
    full = ring_gather(full, "y", sizes["y"], 0, direct)
    out = []
    start = 0
    for w in grads:
        rows = w.shape[0] // 4
        out.append(full[start:start + rows].astype(jnp.float32))
        start += rows
    return out


def to_sequence(x):
    xh = lax.axis_index("xh")
    c = lax.axis_index("c")
    first = lax.ppermute(lax.dynamic_index_in_dim(x, c, 0, False), GRP, [(0, 0), (1, 2), (2, 1), (3, 3)])
    second = lax.ppermute(lax.dynamic_index_in_dim(x, 1 - c, 0, False), GRP, [(0, 2), (1, 0), (2, 3), (3, 1)])
    return jnp.where(xh == 0, jnp.concatenate([first, second]), jnp.concatenate([second, first]))


def from_sequence(x):
    xh = lax.axis_index("xh")
    c = lax.axis_index("c")
    length = x.shape[0] // 2
    first = jnp.where(xh == 0, x[:length], x[length:])
    second = jnp.where(xh == 0, x[length:], x[:length])
    first = lax.ppermute(first, GRP, [(0, 0), (1, 2), (2, 1), (3, 3)])
    second = lax.ppermute(second, GRP, [(2, 0), (0, 1), (3, 2), (1, 3)])
    return jnp.where(c == 0, jnp.stack([first, second]), jnp.stack([second, first]))


def body(
    tokens, segment, piece_start, w_query, w_key, w_value, w_out, w_gate, w_up, w_down, cotangent
):
    sizes = {"y": lax.axis_size("y"), "z": lax.axis_size("z"), "xl": lax.axis_size("xl")}
    width = tokens.shape[2]
    local_length = tokens.shape[1] * 2
    full_length = segment.shape[1]
    head_count = HEADS
    head_size = HDIM
    scale = head_size ** (-0.5)
    xh = lax.axis_index("xh")
    c = lax.axis_index("c")
    first_row = c * local_length
    rows = first_row + jnp.arange(local_length, dtype=jnp.int32)
    columns = jnp.arange(full_length, dtype=jnp.int32)
    inverse = 10000.0 ** (-jnp.arange(0, head_size, 2).astype(jnp.float32) / head_size)
    angles = rows.astype(jnp.float32)[:, None] * inverse[None, :]
    cosine = jnp.cos(angles)[:, None, :]
    sine = jnp.sin(angles)[:, None, :]

    query_weight, key_weight, value_weight = gather_weights(
        (w_query, w_key, w_value), "y", sizes, True
    )

    hidden = to_sequence(tokens).astype(jnp.float32)
    grad_result = to_sequence(cotangent)
    seg_row = lax.dynamic_index_in_dim(segment, xh, 0, False)
    start_row = lax.dynamic_index_in_dim(piece_start, xh, 0, False)

    def swap_halves(mine):
        other = lax.ppermute(mine, "c", [(0, 1), (1, 0)])
        return jnp.where(c == 0, jnp.concatenate([mine, other]), jnp.concatenate([other, mine]))

    normed, norm_one_back = jax.vjp(layer_norm, hidden)
    normed_low = normed.astype(jnp.bfloat16)
    query_heads = rotate(
        matmul(normed_low, query_weight).reshape(local_length, head_count, head_size),
        cosine,
        sine,
    ).astype(jnp.bfloat16)
    keys = (
        rotate(
            matmul(normed_low, key_weight).reshape(local_length, head_count, head_size),
            cosine,
            sine,
        )
        .reshape(local_length, width)
        .astype(jnp.bfloat16)
    )
    values = matmul(normed_low, value_weight).astype(jnp.bfloat16)
    w_out, w_down, w_gate, w_up, values = lax.optimization_barrier((w_out, w_down, w_gate, w_up, values))
    out_weight, down_weight = gather_weights((w_out, w_down), "z", sizes, False)
    gate_weight, up_weight = gather_weights((w_gate, w_up), "y", sizes, False)
    both = swap_halves(jnp.concatenate([keys, values], axis=1))
    def heads(x, length):
        return x.reshape(length, head_count, head_size).transpose(1, 0, 2)

    def unheads(x):
        return x.transpose(1, 0, 2).reshape(x.shape[1], width)

    key_heads = heads(both[:, :width], full_length)
    value_heads = heads(both[:, width:], full_length)
    query_major = heads(query_heads.reshape(local_length, width), local_length)
    seg_local = lax.dynamic_slice_in_dim(seg_row, first_row, local_length)
    start_local = lax.dynamic_slice_in_dim(start_row, first_row, local_length)
    causal = columns[None, :] <= rows[:, None]
    same_piece = start_local[:, None] == start_row[None, :]
    allowed = (seg_local[:, None] == seg_row[None, :]) & (causal | same_piece)

    def scores_of(heads_in):
        raw = jnp.einsum("hqd,hkd->hqk", heads_in, key_heads, preferred_element_type=jnp.float32)
        return jnp.where(allowed[None], raw * scale, -1e30)

    scores = scores_of(query_major)
    highest = jnp.max(scores, axis=-1, keepdims=True)
    expd = jnp.exp(scores - highest)
    total = jnp.sum(expd, axis=-1, keepdims=True)
    log_total = highest + jnp.log(total)
    probs_low = lax.optimization_barrier((expd / total).astype(jnp.bfloat16))
    mixed = unheads(
        jnp.einsum("hqk,hkd->hqd", probs_low, value_heads, preferred_element_type=jnp.float32)
    )
    mixed_low = mixed.reshape(local_length, width).astype(jnp.bfloat16)
    after = hidden + matmul(mixed_low, out_weight)
    normed_two, norm_two_back = jax.vjp(layer_norm, after)
    normed_two_low = normed_two.astype(jnp.bfloat16)
    gate = matmul(normed_two_low, gate_weight)
    upper = matmul(normed_two_low, up_weight)
    active, gate_back = jax.vjp(gated, gate, upper)
    active_low = active.astype(jnp.bfloat16)
    result = after + matmul(active_low, down_weight)
    output = from_sequence(result.astype(jnp.bfloat16))

    grads = [None] * 7
    grads[6] = contract_rows(active_low, grad_result)
    grad_active = contract_cols(grad_result, down_weight)
    grad_gate, grad_upper = gate_back(grad_active)
    gate_low = grad_gate.astype(jnp.bfloat16)
    upper_low = grad_upper.astype(jnp.bfloat16)
    grads[4] = contract_rows(normed_two_low, gate_low)
    grads[5] = contract_rows(normed_two_low, upper_low)
    grad_normed_two = contract_cols(gate_low, gate_weight) + contract_cols(upper_low, up_weight)
    grad_after = grad_result.astype(jnp.float32) + norm_two_back(grad_normed_two)[0]
    after_low = grad_after.astype(jnp.bfloat16)
    grads[3] = contract_rows(mixed_low, after_low)
    grad_mixed = (
        contract_cols(after_low, out_weight)
        .astype(jnp.bfloat16)
        .reshape(local_length, head_count, head_size)
    )
    mixed_major = heads(grad_mixed.reshape(local_length, width), local_length)
    probs = jnp.exp(scores_of(query_major) - log_total)
    grad_probs = jnp.einsum(
        "hqd,hkd->hqk", mixed_major, value_heads, preferred_element_type=jnp.float32
    )
    inner = jnp.sum(probs * grad_probs, axis=-1, keepdims=True)
    grad_raw = lax.optimization_barrier((probs * (grad_probs - inner) * scale).astype(jnp.bfloat16))
    grad_query = unheads(
        jnp.einsum("hqk,hkd->hqd", grad_raw, key_heads, preferred_element_type=jnp.float32)
    ).reshape(local_length, head_count, head_size)
    grad_keys = unheads(
        jnp.einsum("hqk,hqd->hkd", grad_raw, query_major, preferred_element_type=jnp.float32)
    )
    grad_values = unheads(
        jnp.einsum("hqk,hqd->hkd", probs_low, mixed_major, preferred_element_type=jnp.float32)
    )
    grad_kv = jnp.concatenate([grad_keys, grad_values], axis=1)
    early = reduce_group(
        [grads[6], grads[4].reshape(-1, width), grads[5].reshape(-1, width), grads[3]], sizes, False
    )
    early, grad_kv = lax.optimization_barrier((early, grad_kv))
    mine_kv = jnp.where(c == 0, grad_kv[:local_length], grad_kv[local_length:])
    theirs_kv = jnp.where(c == 0, grad_kv[local_length:], grad_kv[:local_length])
    own_kv = mine_kv + lax.ppermute(theirs_kv, "c", [(0, 1), (1, 0)])
    own_keys = own_kv[:, :width]
    own_values = own_kv[:, width:]
    query_low = (
        rotate(grad_query, cosine, -sine).reshape(local_length, width).astype(jnp.bfloat16)
    )
    keys_low = (
        rotate(own_keys.reshape(local_length, head_count, head_size), cosine, -sine)
        .reshape(local_length, width)
        .astype(jnp.bfloat16)
    )
    values_low = own_values.astype(jnp.bfloat16)
    grads[0] = contract_rows(normed_low, query_low)
    grads[1] = contract_rows(normed_low, keys_low)
    grads[2] = contract_rows(normed_low, values_low)
    grad_normed = (
        contract_cols(query_low, query_weight)
        + contract_cols(keys_low, key_weight)
        + contract_cols(values_low, value_weight)
    )
    grad_hidden = grad_after + norm_one_back(grad_normed)[0]
    input_grads = from_sequence(grad_hidden.astype(jnp.bfloat16))
    late = reduce_group([grads[0], grads[1], grads[2]], sizes, True)
    gate_rows = grads[4].shape[0]
    gate_grad = early[1].reshape(gate_rows // 4, -1)
    up_grad = early[2].reshape(gate_rows // 4, -1)
    owned = [late[0], late[1], late[2], early[3], gate_grad, up_grad, early[0]]

    return (output, input_grads, *owned)


def solution(mesh):
    rep, grp = mesh.devices.shape
    side = int(round((rep // 2) ** 0.5))
    devices = mesh.devices.reshape(side, rep // (2 * side), 2, grp // 2, 2)
    fine = Mesh(devices, ("y", "z", "xl", "xh", "c"))
    seqs = P(REP, GRP, None)
    rows = P(GRP, None)
    placed = (seqs, P(REP, None), P(REP, None), rows, rows, rows, rows, rows, rows, rows, seqs)
    return jax.shard_map(
        body,
        mesh=fine,
        in_specs=placed,
        out_specs=(seqs, seqs, rows, rows, rows, rows, rows, rows, rows),
        check_vma=False,
    )
```

```python
import jax
import jax.numpy as jnp
from jax import lax
from jax.sharding import Mesh
from jax.sharding import PartitionSpec as P

HEADS = 12
HDIM = 64
REP = ("y", "z", "xl")
GRP = ("xh", "c")


def layer_norm(hidden):
    centred = hidden - jnp.mean(hidden, axis=-1, keepdims=True)
    spread = jnp.mean(centred * centred, axis=-1, keepdims=True)
    return centred * lax.rsqrt(spread + 1e-05)


def rotate(heads, cosine, sine):
    half = heads.shape[-1] // 2
    first = heads[..., :half]
    second = heads[..., half:]
    return jnp.concatenate(
        [first * cosine - second * sine, second * cosine + first * sine], axis=-1
    )


def gated(gate, upper):
    return gate / (1.0 + jnp.exp(-gate)) * upper


def matmul(left, right):
    return jnp.dot(left, right, preferred_element_type=jnp.float32)


def contract_rows(left, right):
    return lax.dot_general(
        left, right, (((0,), (0,)), ((), ())), preferred_element_type=jnp.float32
    )


def contract_cols(left, right):
    return lax.dot_general(
        left, right, (((1,), (1,)), ((), ())), preferred_element_type=jnp.float32
    )


def shift(x, axis, n, step):
    return lax.ppermute(x, axis, [(i, (i + step) % n) for i in range(n)])


def place(buf, piece, index, dim):
    start = [0] * buf.ndim
    start[dim] = index * piece.shape[dim]
    return lax.dynamic_update_slice(buf, piece, start)


def ring_gather(piece, axis, n, dim, direct=False):
    if n == 1:
        return piece
    me = lax.axis_index(axis)
    shape = list(piece.shape)
    shape[dim] *= n
    buf = place(jnp.zeros(shape, piece.dtype), piece, me, dim)
    if n == 2 or direct:
        for k in range(1, n):
            buf = place(buf, shift(piece, axis, n, k), (me - k) % n, dim)
        return buf
    back = piece
    ahead = piece
    for step in range(1, n // 2 + 1):
        if step < n - step:
            back = shift(back, axis, n, 1)
            ahead = shift(ahead, axis, n, -1)
            buf = place(buf, back, (me - step) % n, dim)
            buf = place(buf, ahead, (me + step) % n, dim)
        else:
            half = piece.shape[dim] // 2
            first = shift(lax.slice_in_dim(back, 0, half, axis=dim), axis, n, 1)
            second = shift(lax.slice_in_dim(ahead, half, piece.shape[dim], axis=dim), axis, n, -1)
            buf = place(buf, jnp.concatenate([first, second], axis=dim), (me + step) % n, dim)
    return buf


def ring_reduce(x, axis, n, dim, hdim, direct=False):
    if n == 1:
        return x
    me = lax.axis_index(axis)
    size = x.shape[dim] // n

    def chunk(k):
        return lax.dynamic_slice_in_dim(x, (k % n) * size, size, axis=dim)

    def low(v):
        return v.astype(jnp.bfloat16)

    if n == 2 or direct:
        acc = chunk(me)
        for k in range(1, n):
            acc = acc + shift(low(chunk(me + k)), axis, n, k).astype(jnp.float32)
        return acc
    assert n == 4
    half = x.shape[hdim] // 2

    def part(k, which):
        c = chunk(k)
        return lax.slice_in_dim(c, 0, half, axis=hdim) if which == 0 else lax.slice_in_dim(
            c, half, c.shape[hdim], axis=hdim
        )

    from_ahead = shift(low(jnp.stack([part(me - 2, 0), part(me - 1, 1)])), axis, n, -1)
    from_back = shift(low(jnp.stack([part(me + 2, 1), part(me + 1, 0)])), axis, n, 1)
    relay_ahead = shift(low(from_ahead[0].astype(jnp.float32) + part(me - 1, 0)), axis, n, -1)
    relay_back = shift(low(from_back[0].astype(jnp.float32) + part(me + 1, 1)), axis, n, 1)
    first = part(me, 0) + from_back[1].astype(jnp.float32) + relay_ahead.astype(jnp.float32)
    second = part(me, 1) + from_ahead[1].astype(jnp.float32) + relay_back.astype(jnp.float32)
    return jnp.concatenate([first, second], axis=hdim)


def cross(x):
    return lax.ppermute(x, ("xl", "xh"), [(i, 3 - i) for i in range(4)])


def swap_core(x):
    return lax.ppermute(x, "c", [(0, 1), (1, 0)])


def absolute(parts, rows):
    g = lax.axis_index("xh") * 2 + lax.axis_index("c")
    buf = jnp.zeros((4 * rows,) + parts[0].shape[1:], parts[0].dtype)
    for j, part in enumerate(parts):
        buf = place(buf, part, jnp.bitwise_xor(g, j), 0)
    return buf


def gather_group(own, axis, n, direct):
    size = own.shape[0] // n
    me = lax.axis_index(axis)
    mine = lax.dynamic_slice_in_dim(own, me * size, size, axis=0)
    other = ring_gather(cross(mine), axis, n, 0, direct)
    partner = swap_core(jnp.concatenate([own, other]))
    rows = own.shape[0]
    return [own, partner[:rows], other, partner[rows:]]


def gather_weights(group, axis, sizes, direct):
    parts = gather_group(jnp.concatenate(group), axis, sizes[axis], direct)
    out = []
    start = 0
    for s in group:
        rows = s.shape[0]
        out.append(absolute([p[start:start + rows] for p in parts], rows))
        start += rows
    return out


def reduce_group(grads, sizes, direct):
    g = lax.axis_index("xh") * 2 + lax.axis_index("c")

    def shard(w, j):
        rows = w.shape[0] // 4
        return lax.dynamic_slice_in_dim(w, jnp.bitwise_xor(g, j) * rows, rows, axis=0)

    send = jnp.concatenate([shard(w, 1) for w in grads] + [shard(w, 3) for w in grads])
    got = swap_core(send.astype(jnp.bfloat16)).astype(jnp.float32)
    total = got.shape[0] // 2
    own = jnp.concatenate([shard(w, 0) for w in grads]) + got[:total]
    oth = jnp.concatenate([shard(w, 2) for w in grads]) + got[total:]
    pair = jnp.stack([own, oth])
    pair = ring_reduce(pair, "y", sizes["y"], 1, 2, direct)
    pair = ring_reduce(pair, "z", sizes["z"], 1, 2, direct)
    low = pair.astype(jnp.bfloat16)
    mine = (
        pair[0]
        + lax.ppermute(low[0], "xl", [(0, 1), (1, 0)]).astype(jnp.float32)
        + cross(low[1]).astype(jnp.float32)
        + lax.ppermute(low[1], "xh", [(0, 1), (1, 0)]).astype(jnp.float32)
    )
    full = ring_gather(mine.astype(jnp.bfloat16), "z", sizes["z"], 0, direct)
    full = ring_gather(full, "y", sizes["y"], 0, direct)
    out = []
    start = 0
    for w in grads:
        rows = w.shape[0] // 4
        out.append(full[start:start + rows].astype(jnp.float32))
        start += rows
    return out


def to_sequence(x):
    xh = lax.axis_index("xh")
    c = lax.axis_index("c")
    first = lax.ppermute(lax.dynamic_index_in_dim(x, c, 0, False), GRP, [(0, 0), (1, 2), (2, 1), (3, 3)])
    second = lax.ppermute(lax.dynamic_index_in_dim(x, 1 - c, 0, False), GRP, [(0, 2), (1, 0), (2, 3), (3, 1)])
    return jnp.where(xh == 0, jnp.concatenate([first, second]), jnp.concatenate([second, first]))


def from_sequence(x):
    xh = lax.axis_index("xh")
    c = lax.axis_index("c")
    length = x.shape[0] // 2
    first = jnp.where(xh == 0, x[:length], x[length:])
    second = jnp.where(xh == 0, x[length:], x[:length])
    first = lax.ppermute(first, GRP, [(0, 0), (1, 2), (2, 1), (3, 3)])
    second = lax.ppermute(second, GRP, [(2, 0), (0, 1), (3, 2), (1, 3)])
    return jnp.where(c == 0, jnp.stack([first, second]), jnp.stack([second, first]))


def body(
    tokens, segment, piece_start, w_query, w_key, w_value, w_out, w_gate, w_up, w_down, cotangent
):
    sizes = {"y": lax.axis_size("y"), "z": lax.axis_size("z"), "xl": lax.axis_size("xl")}
    width = tokens.shape[2]
    local_length = tokens.shape[1] * 2
    full_length = segment.shape[1]
    head_count = HEADS
    head_size = HDIM
    scale = head_size ** (-0.5)
    xh = lax.axis_index("xh")
    c = lax.axis_index("c")
    first_row = c * local_length
    rows = first_row + jnp.arange(local_length, dtype=jnp.int32)
    columns = jnp.arange(full_length, dtype=jnp.int32)
    inverse = 10000.0 ** (-jnp.arange(0, head_size, 2).astype(jnp.float32) / head_size)
    angles = rows.astype(jnp.float32)[:, None] * inverse[None, :]
    cosine = jnp.cos(angles)[:, None, :]
    sine = jnp.sin(angles)[:, None, :]

    query_weight, key_weight, value_weight = gather_weights(
        (w_query, w_key, w_value), "y", {"y": 1}, True
    )

    both_in = to_sequence(jnp.concatenate([tokens, cotangent], axis=2))
    hidden = both_in[:, :width].astype(jnp.float32)
    grad_result = both_in[:, width:]
    seg_row = lax.dynamic_index_in_dim(segment, xh, 0, False)
    start_row = lax.dynamic_index_in_dim(piece_start, xh, 0, False)

    def swap_halves(mine):
        other = lax.ppermute(mine, "c", [(0, 1), (1, 0)])
        return jnp.where(c == 0, jnp.concatenate([mine, other]), jnp.concatenate([other, mine]))

    normed, norm_one_back = jax.vjp(layer_norm, hidden)
    normed_low = normed.astype(jnp.bfloat16)
    query_heads = rotate(
        matmul(normed_low, query_weight).reshape(local_length, head_count, head_size),
        cosine,
        sine,
    ).astype(jnp.bfloat16)
    keys = (
        rotate(
            matmul(normed_low, key_weight).reshape(local_length, head_count, head_size),
            cosine,
            sine,
        )
        .reshape(local_length, width)
        .astype(jnp.bfloat16)
    )
    values = matmul(normed_low, value_weight).astype(jnp.bfloat16)
    w_out, w_down, w_gate, w_up, values = lax.optimization_barrier((w_out, w_down, w_gate, w_up, values))
    width_of_gate = w_gate.shape[1]
    folded = [w.reshape(-1, width) for w in (w_gate, w_up)]
    out_weight, down_weight, gate_weight, up_weight = gather_weights(
        (w_out, w_down, folded[0], folded[1]), "y", sizes, False
    )
    gate_weight = gate_weight.reshape(-1, width_of_gate)
    up_weight = up_weight.reshape(-1, width_of_gate)
    both = swap_halves(jnp.concatenate([keys, values], axis=1))
    def heads(x, length):
        return x.reshape(length, head_count, head_size).transpose(1, 0, 2)

    def unheads(x):
        return x.transpose(1, 0, 2).reshape(x.shape[1], width)

    key_heads = heads(both[:, :width], full_length)
    value_heads = heads(both[:, width:], full_length)
    query_major = heads(query_heads.reshape(local_length, width), local_length)
    seg_local = lax.dynamic_slice_in_dim(seg_row, first_row, local_length)
    start_local = lax.dynamic_slice_in_dim(start_row, first_row, local_length)
    causal = columns[None, :] <= rows[:, None]
    same_piece = start_local[:, None] == start_row[None, :]
    allowed = (seg_local[:, None] == seg_row[None, :]) & (causal | same_piece)

    def scores_of(heads_in):
        raw = jnp.einsum("hqd,hkd->hqk", heads_in, key_heads, preferred_element_type=jnp.float32)
        return jnp.where(allowed[None], raw * scale, -1e30)

    scores = scores_of(query_major)
    highest = jnp.max(scores, axis=-1, keepdims=True)
    expd = jnp.exp(scores - highest)
    total = jnp.sum(expd, axis=-1, keepdims=True)
    log_total = highest + jnp.log(total)
    probs_low = lax.optimization_barrier((expd / total).astype(jnp.bfloat16))
    mixed = unheads(
        jnp.einsum("hqk,hkd->hqd", probs_low, value_heads, preferred_element_type=jnp.float32)
    )
    mixed_low = mixed.reshape(local_length, width).astype(jnp.bfloat16)
    after = hidden + matmul(mixed_low, out_weight)
    normed_two, norm_two_back = jax.vjp(layer_norm, after)
    normed_two_low = normed_two.astype(jnp.bfloat16)
    gate = matmul(normed_two_low, gate_weight)
    upper = matmul(normed_two_low, up_weight)
    active, gate_back = jax.vjp(gated, gate, upper)
    active_low = active.astype(jnp.bfloat16)
    result = after + matmul(active_low, down_weight)
    result_low = result.astype(jnp.bfloat16)

    grads = [None] * 7
    grads[6] = contract_rows(active_low, grad_result)
    grad_active = contract_cols(grad_result, down_weight)
    grad_gate, grad_upper = gate_back(grad_active)
    gate_low = grad_gate.astype(jnp.bfloat16)
    upper_low = grad_upper.astype(jnp.bfloat16)
    def folded_grad(left, right):
        blocks = right.reshape(right.shape[0], -1, width)
        out = jnp.einsum("td,tcf->dcf", left, blocks, preferred_element_type=jnp.float32)
        return out.reshape(-1, width)

    grads[4] = folded_grad(normed_two_low, gate_low)
    grads[5] = folded_grad(normed_two_low, upper_low)
    grad_normed_two = contract_cols(gate_low, gate_weight) + contract_cols(upper_low, up_weight)
    grad_after = grad_result.astype(jnp.float32) + norm_two_back(grad_normed_two)[0]
    after_low = grad_after.astype(jnp.bfloat16)
    grads[3] = contract_rows(mixed_low, after_low)
    grad_mixed = (
        contract_cols(after_low, out_weight)
        .astype(jnp.bfloat16)
        .reshape(local_length, head_count, head_size)
    )
    mixed_major = heads(grad_mixed.reshape(local_length, width), local_length)
    probs = jnp.exp(scores_of(query_major) - log_total)
    grad_probs = jnp.einsum(
        "hqd,hkd->hqk", mixed_major, value_heads, preferred_element_type=jnp.float32
    )
    inner = jnp.sum(probs * grad_probs, axis=-1, keepdims=True)
    grad_raw = lax.optimization_barrier((probs * (grad_probs - inner) * scale).astype(jnp.bfloat16))
    grad_query = unheads(
        jnp.einsum("hqk,hkd->hqd", grad_raw, key_heads, preferred_element_type=jnp.float32)
    ).reshape(local_length, head_count, head_size)
    grad_keys = unheads(
        jnp.einsum("hqk,hqd->hkd", grad_raw, query_major, preferred_element_type=jnp.float32)
    )
    grad_values = unheads(
        jnp.einsum("hqk,hqd->hkd", probs_low, mixed_major, preferred_element_type=jnp.float32)
    )
    grad_kv = jnp.concatenate([grad_keys, grad_values], axis=1)
    mine_kv = jnp.where(c == 0, grad_kv[:local_length], grad_kv[local_length:])
    theirs_kv = jnp.where(c == 0, grad_kv[local_length:], grad_kv[:local_length])
    own_kv = mine_kv + lax.ppermute(theirs_kv, "c", [(0, 1), (1, 0)])
    own_keys = own_kv[:, :width]
    own_values = own_kv[:, width:]
    query_low = (
        rotate(grad_query, cosine, -sine).reshape(local_length, width).astype(jnp.bfloat16)
    )
    keys_low = (
        rotate(own_keys.reshape(local_length, head_count, head_size), cosine, -sine)
        .reshape(local_length, width)
        .astype(jnp.bfloat16)
    )
    values_low = own_values.astype(jnp.bfloat16)
    grads[0] = contract_rows(normed_low, query_low)
    grads[1] = contract_rows(normed_low, keys_low)
    grads[2] = contract_rows(normed_low, values_low)
    grad_normed = (
        contract_cols(query_low, query_weight)
        + contract_cols(keys_low, key_weight)
        + contract_cols(values_low, value_weight)
    )
    grad_hidden = grad_after + norm_one_back(grad_normed)[0]
    both_out = from_sequence(jnp.concatenate([result_low, grad_hidden.astype(jnp.bfloat16)], axis=1))
    output = both_out[..., :width]
    input_grads = both_out[..., width:]
    owned = reduce_group(grads, sizes, False)
    owned[4] = owned[4].reshape(-1, width_of_gate)
    owned[5] = owned[5].reshape(-1, width_of_gate)

    return (output, input_grads, *owned)


def solution(mesh):
    rep, grp = mesh.devices.shape
    side = int(round((rep // 2) ** 0.5))
    devices = mesh.devices.reshape(side, rep // (2 * side), 2, grp // 2, 2)
    fine = Mesh(devices, ("y", "z", "xl", "xh", "c"))
    seqs = P(REP, GRP, None)
    rows = P(GRP, None)
    placed = (seqs, P(REP, None), P(REP, None), rows, rows, rows, rows, rows, rows, rows, seqs)
    return jax.shard_map(
        body,
        mesh=fine,
        in_specs=placed,
        out_specs=(seqs, seqs, rows, rows, rows, rows, rows, rows, rows),
        check_vma=False,
    )
```

```python
import jax
import jax.numpy as jnp
from jax import lax
from jax.sharding import Mesh
from jax.sharding import PartitionSpec as P

HEADS = 12
HDIM = 64
REP = ("y", "z", "xl")
GRP = ("xh", "c")


def layer_norm(hidden):
    centred = hidden - jnp.mean(hidden, axis=-1, keepdims=True)
    spread = jnp.mean(centred * centred, axis=-1, keepdims=True)
    return centred * lax.rsqrt(spread + 1e-05)


def rotate(heads, cosine, sine):
    half = heads.shape[-1] // 2
    first = heads[..., :half]
    second = heads[..., half:]
    return jnp.concatenate(
        [first * cosine - second * sine, second * cosine + first * sine], axis=-1
    )


def gated(gate, upper):
    return gate / (1.0 + jnp.exp(-gate)) * upper


def matmul(left, right):
    return jnp.dot(left, right, preferred_element_type=jnp.float32)


def contract_rows(left, right):
    return lax.dot_general(
        left, right, (((0,), (0,)), ((), ())), preferred_element_type=jnp.float32
    )


def contract_cols(left, right):
    return lax.dot_general(
        left, right, (((1,), (1,)), ((), ())), preferred_element_type=jnp.float32
    )


def shift(x, axis, n, step):
    return lax.ppermute(x, axis, [(i, (i + step) % n) for i in range(n)])


def place(buf, piece, index, dim):
    start = [0] * buf.ndim
    start[dim] = index * piece.shape[dim]
    return lax.dynamic_update_slice(buf, piece, start)


def ring_gather(piece, axis, n, dim, direct=False):
    if n == 1:
        return piece
    me = lax.axis_index(axis)
    shape = list(piece.shape)
    shape[dim] *= n
    buf = place(jnp.zeros(shape, piece.dtype), piece, me, dim)
    if n == 2 or direct:
        for k in range(1, n):
            buf = place(buf, shift(piece, axis, n, k), (me - k) % n, dim)
        return buf
    back = piece
    ahead = piece
    for step in range(1, n // 2 + 1):
        if step < n - step:
            back = shift(back, axis, n, 1)
            ahead = shift(ahead, axis, n, -1)
            buf = place(buf, back, (me - step) % n, dim)
            buf = place(buf, ahead, (me + step) % n, dim)
        else:
            half = piece.shape[dim] // 2
            first = shift(lax.slice_in_dim(back, 0, half, axis=dim), axis, n, 1)
            second = shift(lax.slice_in_dim(ahead, half, piece.shape[dim], axis=dim), axis, n, -1)
            buf = place(buf, jnp.concatenate([first, second], axis=dim), (me + step) % n, dim)
    return buf


def ring_reduce(x, axis, n, dim, hdim, direct=False):
    if n == 1:
        return x
    me = lax.axis_index(axis)
    size = x.shape[dim] // n

    def chunk(k):
        return lax.dynamic_slice_in_dim(x, (k % n) * size, size, axis=dim)

    def low(v):
        return v.astype(jnp.bfloat16)

    if n == 2 or direct:
        acc = chunk(me)
        for k in range(1, n):
            acc = acc + shift(low(chunk(me + k)), axis, n, k).astype(jnp.float32)
        return acc
    assert n == 4
    half = x.shape[hdim] // 2

    def part(k, which):
        c = chunk(k)
        return lax.slice_in_dim(c, 0, half, axis=hdim) if which == 0 else lax.slice_in_dim(
            c, half, c.shape[hdim], axis=hdim
        )

    from_ahead = shift(low(jnp.stack([part(me - 2, 0), part(me - 1, 1)])), axis, n, -1)
    from_back = shift(low(jnp.stack([part(me + 2, 1), part(me + 1, 0)])), axis, n, 1)
    relay_ahead = shift(low(from_ahead[0].astype(jnp.float32) + part(me - 1, 0)), axis, n, -1)
    relay_back = shift(low(from_back[0].astype(jnp.float32) + part(me + 1, 1)), axis, n, 1)
    first = part(me, 0) + from_back[1].astype(jnp.float32) + relay_ahead.astype(jnp.float32)
    second = part(me, 1) + from_ahead[1].astype(jnp.float32) + relay_back.astype(jnp.float32)
    return jnp.concatenate([first, second], axis=hdim)


def cross(x):
    return lax.ppermute(x, ("xl", "xh"), [(i, 3 - i) for i in range(4)])


def swap_core(x):
    return lax.ppermute(x, "c", [(0, 1), (1, 0)])


def absolute(parts, rows):
    g = lax.axis_index("xh") * 2 + lax.axis_index("c")
    buf = jnp.zeros((4 * rows,) + parts[0].shape[1:], parts[0].dtype)
    for j, part in enumerate(parts):
        buf = place(buf, part, jnp.bitwise_xor(g, j), 0)
    return buf


def gather_group(own, axis, n, direct):
    size = own.shape[0] // n
    me = lax.axis_index(axis)
    mine = lax.dynamic_slice_in_dim(own, me * size, size, axis=0)
    other = ring_gather(cross(mine), axis, n, 0, direct)
    partner = swap_core(jnp.concatenate([own, other]))
    rows = own.shape[0]
    return [own, partner[:rows], other, partner[rows:]]


def gather_weights(group, axis, sizes, direct):
    parts = gather_group(jnp.concatenate(group), axis, sizes[axis], direct)
    out = []
    start = 0
    for s in group:
        rows = s.shape[0]
        out.append(absolute([p[start:start + rows] for p in parts], rows))
        start += rows
    return out


def reduce_group(grads, sizes, direct):
    g = lax.axis_index("xh") * 2 + lax.axis_index("c")

    def shard(w, j):
        rows = w.shape[0] // 4
        return lax.dynamic_slice_in_dim(w, jnp.bitwise_xor(g, j) * rows, rows, axis=0)

    send = jnp.concatenate([shard(w, 1) for w in grads] + [shard(w, 3) for w in grads])
    got = swap_core(send.astype(jnp.bfloat16)).astype(jnp.float32)
    total = got.shape[0] // 2
    own = jnp.concatenate([shard(w, 0) for w in grads]) + got[:total]
    oth = jnp.concatenate([shard(w, 2) for w in grads]) + got[total:]
    pair = jnp.stack([own, oth])
    pair = ring_reduce(pair, "y", sizes["y"], 1, 2, direct)
    pair = ring_reduce(pair, "z", sizes["z"], 1, 2, direct)
    low = pair.astype(jnp.bfloat16)
    mine = (
        pair[0]
        + lax.ppermute(low[0], "xl", [(0, 1), (1, 0)]).astype(jnp.float32)
        + cross(low[1]).astype(jnp.float32)
        + lax.ppermute(low[1], "xh", [(0, 1), (1, 0)]).astype(jnp.float32)
    )
    full = ring_gather(mine.astype(jnp.bfloat16), "z", sizes["z"], 0, direct)
    full = ring_gather(full, "y", sizes["y"], 0, direct)
    out = []
    start = 0
    for w in grads:
        rows = w.shape[0] // 4
        out.append(full[start:start + rows].astype(jnp.float32))
        start += rows
    return out


def to_sequence(x):
    xh = lax.axis_index("xh")
    c = lax.axis_index("c")
    first = lax.ppermute(lax.dynamic_index_in_dim(x, c, 0, False), GRP, [(0, 0), (1, 2), (2, 1), (3, 3)])
    second = lax.ppermute(lax.dynamic_index_in_dim(x, 1 - c, 0, False), GRP, [(0, 2), (1, 0), (2, 3), (3, 1)])
    return jnp.where(xh == 0, jnp.concatenate([first, second]), jnp.concatenate([second, first]))


def from_sequence(x):
    xh = lax.axis_index("xh")
    c = lax.axis_index("c")
    length = x.shape[0] // 2
    first = jnp.where(xh == 0, x[:length], x[length:])
    second = jnp.where(xh == 0, x[length:], x[:length])
    first = lax.ppermute(first, GRP, [(0, 0), (1, 2), (2, 1), (3, 3)])
    second = lax.ppermute(second, GRP, [(2, 0), (0, 1), (3, 2), (1, 3)])
    return jnp.where(c == 0, jnp.stack([first, second]), jnp.stack([second, first]))


def body(
    tokens, segment, piece_start, w_query, w_key, w_value, w_out, w_gate, w_up, w_down, cotangent
):
    sizes = {"y": lax.axis_size("y"), "z": lax.axis_size("z"), "xl": lax.axis_size("xl")}
    width = tokens.shape[2]
    local_length = tokens.shape[1] * 2
    full_length = segment.shape[1]
    head_count = HEADS
    head_size = HDIM
    scale = head_size ** (-0.5)
    xh = lax.axis_index("xh")
    c = lax.axis_index("c")
    first_row = c * local_length
    rows = first_row + jnp.arange(local_length, dtype=jnp.int32)
    columns = jnp.arange(full_length, dtype=jnp.int32)
    inverse = 10000.0 ** (-jnp.arange(0, head_size, 2).astype(jnp.float32) / head_size)
    angles = rows.astype(jnp.float32)[:, None] * inverse[None, :]
    cosine = jnp.cos(angles)[:, None, :]
    sine = jnp.sin(angles)[:, None, :]

    query_weight, key_weight, value_weight = gather_weights(
        (w_query, w_key, w_value), "y", sizes, True
    )

    both_in = to_sequence(jnp.concatenate([tokens, cotangent], axis=2))
    hidden = both_in[:, :width].astype(jnp.float32)
    grad_result = both_in[:, width:]
    seg_row = lax.dynamic_index_in_dim(segment, xh, 0, False)
    start_row = lax.dynamic_index_in_dim(piece_start, xh, 0, False)

    def swap_halves(mine):
        other = lax.ppermute(mine, "c", [(0, 1), (1, 0)])
        return jnp.where(c == 0, jnp.concatenate([mine, other]), jnp.concatenate([other, mine]))

    normed, norm_one_back = jax.vjp(layer_norm, hidden)
    normed_low = normed.astype(jnp.bfloat16)
    query_heads = rotate(
        matmul(normed_low, query_weight).reshape(local_length, head_count, head_size),
        cosine,
        sine,
    ).astype(jnp.bfloat16)
    keys = (
        rotate(
            matmul(normed_low, key_weight).reshape(local_length, head_count, head_size),
            cosine,
            sine,
        )
        .reshape(local_length, width)
        .astype(jnp.bfloat16)
    )
    values = matmul(normed_low, value_weight).astype(jnp.bfloat16)
    w_out, w_down, w_gate, w_up, values = lax.optimization_barrier((w_out, w_down, w_gate, w_up, values))
    out_weight, down_weight = gather_weights((w_out, w_down), "z", sizes, False)
    gate_weight, up_weight = gather_weights((w_gate, w_up), "y", sizes, False)
    both = swap_halves(jnp.concatenate([keys, values], axis=1))
    def heads(x, length):
        return x.reshape(length, head_count, head_size).transpose(1, 0, 2)

    def unheads(x):
        return x.transpose(1, 0, 2).reshape(x.shape[1], width)

    key_heads = heads(both[:, :width], full_length)
    value_heads = heads(both[:, width:], full_length)
    query_major = heads(query_heads.reshape(local_length, width), local_length)
    seg_local = lax.dynamic_slice_in_dim(seg_row, first_row, local_length)
    start_local = lax.dynamic_slice_in_dim(start_row, first_row, local_length)
    causal = columns[None, :] <= rows[:, None]
    same_piece = start_local[:, None] == start_row[None, :]
    allowed = (seg_local[:, None] == seg_row[None, :]) & (causal | same_piece)

    def scores_of(heads_in):
        raw = jnp.einsum("hqd,hkd->hqk", heads_in, key_heads, preferred_element_type=jnp.float32)
        return jnp.where(allowed[None], raw * scale, -1e30)

    scores = scores_of(query_major)
    highest = jnp.max(scores, axis=-1, keepdims=True)
    expd = jnp.exp(scores - highest)
    total = jnp.sum(expd, axis=-1, keepdims=True)
    log_total = highest + jnp.log(total)
    probs_low = lax.optimization_barrier((expd / total).astype(jnp.bfloat16))
    mixed = unheads(
        jnp.einsum("hqk,hkd->hqd", probs_low, value_heads, preferred_element_type=jnp.float32)
    )
    mixed_low = mixed.reshape(local_length, width).astype(jnp.bfloat16)
    after = hidden + matmul(mixed_low, out_weight)
    normed_two, norm_two_back = jax.vjp(layer_norm, after)
    normed_two_low = normed_two.astype(jnp.bfloat16)
    gate = matmul(normed_two_low, gate_weight)
    upper = matmul(normed_two_low, up_weight)
    active, gate_back = jax.vjp(gated, gate, upper)
    active_low = active.astype(jnp.bfloat16)
    result = after + matmul(active_low, down_weight)
    result_low = result.astype(jnp.bfloat16)

    grads = [None] * 7
    grads[6] = contract_rows(active_low, grad_result)
    grad_active = contract_cols(grad_result, down_weight)
    grad_gate, grad_upper = gate_back(grad_active)
    gate_low = grad_gate.astype(jnp.bfloat16)
    upper_low = grad_upper.astype(jnp.bfloat16)
    grads[4] = contract_rows(normed_two_low, gate_low)
    grads[5] = contract_rows(normed_two_low, upper_low)
    grad_normed_two = contract_cols(gate_low, gate_weight) + contract_cols(upper_low, up_weight)
    grad_after = grad_result.astype(jnp.float32) + norm_two_back(grad_normed_two)[0]
    after_low = grad_after.astype(jnp.bfloat16)
    grads[3] = contract_rows(mixed_low, after_low)
    grad_mixed = (
        contract_cols(after_low, out_weight)
        .astype(jnp.bfloat16)
        .reshape(local_length, head_count, head_size)
    )
    mixed_major = heads(grad_mixed.reshape(local_length, width), local_length)
    probs = jnp.exp(scores_of(query_major) - log_total)
    grad_probs = jnp.einsum(
        "hqd,hkd->hqk", mixed_major, value_heads, preferred_element_type=jnp.float32
    )
    inner = jnp.sum(probs * grad_probs, axis=-1, keepdims=True)
    grad_raw = lax.optimization_barrier((probs * (grad_probs - inner) * scale).astype(jnp.bfloat16))
    grad_query = unheads(
        jnp.einsum("hqk,hkd->hqd", grad_raw, key_heads, preferred_element_type=jnp.float32)
    ).reshape(local_length, head_count, head_size)
    grad_keys = unheads(
        jnp.einsum("hqk,hqd->hkd", grad_raw, query_major, preferred_element_type=jnp.float32)
    )
    grad_values = unheads(
        jnp.einsum("hqk,hqd->hkd", probs_low, mixed_major, preferred_element_type=jnp.float32)
    )
    grad_kv = jnp.concatenate([grad_keys, grad_values], axis=1)
    early = reduce_group(
        [grads[6], grads[4].reshape(-1, width), grads[5].reshape(-1, width), grads[3]], sizes, False
    )
    early, grad_kv = lax.optimization_barrier((early, grad_kv))
    mine_kv = jnp.where(c == 0, grad_kv[:local_length], grad_kv[local_length:])
    theirs_kv = jnp.where(c == 0, grad_kv[local_length:], grad_kv[:local_length])
    own_kv = mine_kv + lax.ppermute(theirs_kv, "c", [(0, 1), (1, 0)])
    own_keys = own_kv[:, :width]
    own_values = own_kv[:, width:]
    query_low = (
        rotate(grad_query, cosine, -sine).reshape(local_length, width).astype(jnp.bfloat16)
    )
    keys_low = (
        rotate(own_keys.reshape(local_length, head_count, head_size), cosine, -sine)
        .reshape(local_length, width)
        .astype(jnp.bfloat16)
    )
    values_low = own_values.astype(jnp.bfloat16)
    grads[0] = contract_rows(normed_low, query_low)
    grads[1] = contract_rows(normed_low, keys_low)
    grads[2] = contract_rows(normed_low, values_low)
    grad_normed = (
        contract_cols(query_low, query_weight)
        + contract_cols(keys_low, key_weight)
        + contract_cols(values_low, value_weight)
    )
    grad_hidden = grad_after + norm_one_back(grad_normed)[0]
    both_out = from_sequence(jnp.concatenate([result_low, grad_hidden.astype(jnp.bfloat16)], axis=1))
    output = both_out[..., :width]
    input_grads = both_out[..., width:]
    late = reduce_group([grads[0], grads[1], grads[2]], sizes, True)
    gate_rows = grads[4].shape[0]
    gate_grad = early[1].reshape(gate_rows // 4, -1)
    up_grad = early[2].reshape(gate_rows // 4, -1)
    owned = [late[0], late[1], late[2], early[3], gate_grad, up_grad, early[0]]

    return (output, input_grads, *owned)


def solution(mesh):
    rep, grp = mesh.devices.shape
    side = int(round((rep // 2) ** 0.5))
    devices = mesh.devices.reshape(side, rep // (2 * side), 2, grp // 2, 2)
    fine = Mesh(devices, ("y", "z", "xl", "xh", "c"))
    seqs = P(REP, GRP, None)
    rows = P(GRP, None)
    placed = (seqs, P(REP, None), P(REP, None), rows, rows, rows, rows, rows, rows, rows, seqs)
    return jax.shard_map(
        body,
        mesh=fine,
        in_specs=placed,
        out_specs=(seqs, seqs, rows, rows, rows, rows, rows, rows, rows),
        check_vma=False,
    )
```

```python
import jax
import jax.numpy as jnp
from jax import lax
from jax.sharding import Mesh
from jax.sharding import PartitionSpec as P
from jax.experimental import pallas as pl
from jax.experimental.pallas import tpu as pltpu

HEADS = 12
HDIM = 64
REP = ("y", "z", "xl")
GRP = ("xh", "c")


def layer_norm(hidden):
    centred = hidden - jnp.mean(hidden, axis=-1, keepdims=True)
    spread = jnp.mean(centred * centred, axis=-1, keepdims=True)
    return centred * lax.rsqrt(spread + 1e-05)


def rotate(heads, cosine, sine):
    half = heads.shape[-1] // 2
    first = heads[..., :half]
    second = heads[..., half:]
    return jnp.concatenate(
        [first * cosine - second * sine, second * cosine + first * sine], axis=-1
    )


def gated(gate, upper):
    return gate / (1.0 + jnp.exp(-gate)) * upper


def matmul(left, right):
    return jnp.dot(left, right, preferred_element_type=jnp.float32)


def contract_rows(left, right):
    return lax.dot_general(
        left, right, (((0,), (0,)), ((), ())), preferred_element_type=jnp.float32
    )


def contract_cols(left, right):
    return lax.dot_general(
        left, right, (((1,), (1,)), ((), ())), preferred_element_type=jnp.float32
    )


def allowed_mask(rq_ref, sq_ref, pq_ref, sk_ref, pk_ref, shape):
    cols = lax.broadcasted_iota(jnp.int32, shape, 1)
    return (sq_ref[...] == sk_ref[...]) & ((cols <= rq_ref[...]) | (pq_ref[...] == pk_ref[...]))


def attention_forward_kernel(q_ref, k_ref, v_ref, rq_ref, sq_ref, pq_ref, sk_ref, pk_ref, o_ref, lse_ref):
    queries = q_ref.shape[0]
    keys = k_ref.shape[0]
    allowed = allowed_mask(rq_ref, sq_ref, pq_ref, sk_ref, pk_ref, (queries, keys))
    scale = HDIM ** (-0.5)
    for h in range(q_ref.shape[1] // HDIM):
        cols = slice(h * HDIM, (h + 1) * HDIM)
        raw = lax.dot_general(
            q_ref[:, cols], k_ref[:, cols], (((1,), (1,)), ((), ())),
            preferred_element_type=jnp.float32,
        )
        scores = jnp.where(allowed, raw * scale, -1e30)
        highest = jnp.max(scores, axis=1, keepdims=True)
        expd = jnp.exp(scores - highest)
        total = jnp.sum(expd, axis=1, keepdims=True)
        probs_low = (expd / total).astype(jnp.bfloat16)
        o_ref[:, cols] = jnp.dot(probs_low, v_ref[:, cols], preferred_element_type=jnp.float32)
        lse_ref[:, h:h + 1] = highest + jnp.log(total)


def attention_backward_kernel(
    q_ref, k_ref, v_ref, do_ref, lse_ref, rq_ref, sq_ref, pq_ref, sk_ref, pk_ref, dq_ref, dk_ref, dv_ref
):
    queries = q_ref.shape[0]
    keys = k_ref.shape[0]
    allowed = allowed_mask(rq_ref, sq_ref, pq_ref, sk_ref, pk_ref, (queries, keys))
    scale = HDIM ** (-0.5)
    for h in range(q_ref.shape[1] // HDIM):
        cols = slice(h * HDIM, (h + 1) * HDIM)
        q = q_ref[:, cols]
        k = k_ref[:, cols]
        v = v_ref[:, cols]
        do = do_ref[:, cols]
        raw = lax.dot_general(q, k, (((1,), (1,)), ((), ())), preferred_element_type=jnp.float32)
        scores = jnp.where(allowed, raw * scale, -1e30)
        probs = jnp.exp(scores - lse_ref[:, h:h + 1])
        grad_probs = lax.dot_general(do, v, (((1,), (1,)), ((), ())), preferred_element_type=jnp.float32)
        inner = jnp.sum(probs * grad_probs, axis=1, keepdims=True)
        grad_raw = (probs * (grad_probs - inner) * scale).astype(jnp.bfloat16)
        dq_ref[:, cols] = jnp.dot(grad_raw, k, preferred_element_type=jnp.float32)
        dk_ref[:, cols] = lax.dot_general(
            grad_raw, q, (((0,), (0,)), ((), ())), preferred_element_type=jnp.float32
        )
        dv_ref[:, cols] = lax.dot_general(
            probs.astype(jnp.bfloat16), do, (((0,), (0,)), ((), ())), preferred_element_type=jnp.float32
        )


def mask_specs(queries, keys):
    column = pl.BlockSpec((queries, 1), lambda i: (0, 0))
    row = pl.BlockSpec((1, keys), lambda i: (0, 0))
    return [column, column, column, row, row]


def attention_forward(q, kv, masks):
    queries, width = q.shape
    keys = kv.shape[0]
    block = 2 * HDIM
    pairs = width // block
    return pl.pallas_call(
        attention_forward_kernel,
        grid=(pairs,),
        in_specs=[
            pl.BlockSpec((queries, block), lambda i: (0, i)),
            pl.BlockSpec((keys, block), lambda i: (0, i)),
            pl.BlockSpec((keys, block), lambda i, p=pairs: (0, i + p)),
        ] + mask_specs(queries, keys),
        out_specs=[
            pl.BlockSpec((queries, block), lambda i: (0, i)),
            pl.BlockSpec((None, queries, 2), lambda i: (i, 0, 0)),
        ],
        out_shape=[
            jax.ShapeDtypeStruct((queries, width), jnp.float32),
            jax.ShapeDtypeStruct((pairs, queries, 2), jnp.float32),
        ],
        compiler_params=pltpu.CompilerParams(dimension_semantics=("arbitrary",)),
        cost_estimate=pl.CostEstimate(
            flops=4 * queries * keys * width, transcendentals=queries * keys * HEADS,
            bytes_accessed=2 * (queries + 2 * keys) * width + 4 * queries * width,
        ),
    )(q, kv, kv, *masks)


def attention_backward(q, kv, do, lse, masks):
    queries, width = q.shape
    keys = kv.shape[0]
    block = 2 * HDIM
    pairs = width // block
    return pl.pallas_call(
        attention_backward_kernel,
        grid=(pairs,),
        in_specs=[
            pl.BlockSpec((queries, block), lambda i: (0, i)),
            pl.BlockSpec((keys, block), lambda i: (0, i)),
            pl.BlockSpec((keys, block), lambda i, p=pairs: (0, i + p)),
            pl.BlockSpec((queries, block), lambda i: (0, i)),
            pl.BlockSpec((None, queries, 2), lambda i: (i, 0, 0)),
        ] + mask_specs(queries, keys),
        out_specs=[
            pl.BlockSpec((queries, block), lambda i: (0, i)),
            pl.BlockSpec((keys, block), lambda i: (0, i)),
            pl.BlockSpec((keys, block), lambda i: (0, i)),
        ],
        out_shape=[
            jax.ShapeDtypeStruct((queries, width), jnp.float32),
            jax.ShapeDtypeStruct((keys, width), jnp.float32),
            jax.ShapeDtypeStruct((keys, width), jnp.float32),
        ],
        compiler_params=pltpu.CompilerParams(dimension_semantics=("arbitrary",)),
        cost_estimate=pl.CostEstimate(
            flops=10 * queries * keys * width, transcendentals=queries * keys * HEADS,
            bytes_accessed=2 * (2 * queries + 2 * keys) * width + 4 * (queries + 2 * keys) * width,
        ),
    )(q, kv, kv, do, lse, *masks)


def shift(x, axis, n, step):
    return lax.ppermute(x, axis, [(i, (i + step) % n) for i in range(n)])


def place(buf, piece, index, dim):
    start = [0] * buf.ndim
    start[dim] = index * piece.shape[dim]
    return lax.dynamic_update_slice(buf, piece, start)


def ring_gather(piece, axis, n, dim, direct=False):
    if n == 1:
        return piece
    me = lax.axis_index(axis)
    shape = list(piece.shape)
    shape[dim] *= n
    buf = place(jnp.zeros(shape, piece.dtype), piece, me, dim)
    if n == 2 or direct:
        for k in range(1, n):
            buf = place(buf, shift(piece, axis, n, k), (me - k) % n, dim)
        return buf
    back = piece
    ahead = piece
    for step in range(1, n // 2 + 1):
        if step < n - step:
            back = shift(back, axis, n, 1)
            ahead = shift(ahead, axis, n, -1)
            buf = place(buf, back, (me - step) % n, dim)
            buf = place(buf, ahead, (me + step) % n, dim)
        else:
            half = piece.shape[dim] // 2
            first = shift(lax.slice_in_dim(back, 0, half, axis=dim), axis, n, 1)
            second = shift(lax.slice_in_dim(ahead, half, piece.shape[dim], axis=dim), axis, n, -1)
            buf = place(buf, jnp.concatenate([first, second], axis=dim), (me + step) % n, dim)
    return buf


def ring_reduce(x, axis, n, dim, hdim, direct=False):
    if n == 1:
        return x
    me = lax.axis_index(axis)
    size = x.shape[dim] // n

    def chunk(k):
        return lax.dynamic_slice_in_dim(x, (k % n) * size, size, axis=dim)

    def low(v):
        return v.astype(jnp.bfloat16)

    if n == 2 or direct:
        acc = chunk(me)
        for k in range(1, n):
            acc = acc + shift(low(chunk(me + k)), axis, n, k).astype(jnp.float32)
        return acc
    assert n == 4
    half = x.shape[hdim] // 2

    def part(k, which):
        c = chunk(k)
        return lax.slice_in_dim(c, 0, half, axis=hdim) if which == 0 else lax.slice_in_dim(
            c, half, c.shape[hdim], axis=hdim
        )

    from_ahead = shift(low(jnp.stack([part(me - 2, 0), part(me - 1, 1)])), axis, n, -1)
    from_back = shift(low(jnp.stack([part(me + 2, 1), part(me + 1, 0)])), axis, n, 1)
    relay_ahead = shift(low(from_ahead[0].astype(jnp.float32) + part(me - 1, 0)), axis, n, -1)
    relay_back = shift(low(from_back[0].astype(jnp.float32) + part(me + 1, 1)), axis, n, 1)
    first = part(me, 0) + from_back[1].astype(jnp.float32) + relay_ahead.astype(jnp.float32)
    second = part(me, 1) + from_ahead[1].astype(jnp.float32) + relay_back.astype(jnp.float32)
    return jnp.concatenate([first, second], axis=hdim)


def cross(x):
    return lax.ppermute(x, ("xl", "xh"), [(i, 3 - i) for i in range(4)])


def swap_core(x):
    return lax.ppermute(x, "c", [(0, 1), (1, 0)])


def absolute(parts, rows):
    g = lax.axis_index("xh") * 2 + lax.axis_index("c")
    buf = jnp.zeros((4 * rows,) + parts[0].shape[1:], parts[0].dtype)
    for j, part in enumerate(parts):
        buf = place(buf, part, jnp.bitwise_xor(g, j), 0)
    return buf


def gather_group(own, axis, n, direct):
    size = own.shape[0] // n
    me = lax.axis_index(axis)
    mine = lax.dynamic_slice_in_dim(own, me * size, size, axis=0)
    other = ring_gather(cross(mine), axis, n, 0, direct)
    partner = swap_core(jnp.concatenate([own, other]))
    rows = own.shape[0]
    return [own, partner[:rows], other, partner[rows:]]


def gather_weights(group, axis, sizes, direct):
    parts = gather_group(jnp.concatenate(group), axis, sizes[axis], direct)
    out = []
    start = 0
    for s in group:
        rows = s.shape[0]
        out.append(absolute([p[start:start + rows] for p in parts], rows))
        start += rows
    return out


def reduce_group(grads, sizes, direct):
    g = lax.axis_index("xh") * 2 + lax.axis_index("c")

    def shard(w, j):
        rows = w.shape[0] // 4
        return lax.dynamic_slice_in_dim(w, jnp.bitwise_xor(g, j) * rows, rows, axis=0)

    send = jnp.concatenate([shard(w, 1) for w in grads] + [shard(w, 3) for w in grads])
    got = swap_core(send.astype(jnp.bfloat16)).astype(jnp.float32)
    total = got.shape[0] // 2
    own = jnp.concatenate([shard(w, 0) for w in grads]) + got[:total]
    oth = jnp.concatenate([shard(w, 2) for w in grads]) + got[total:]
    pair = jnp.stack([own, oth])
    pair = ring_reduce(pair, "y", sizes["y"], 1, 2, direct)
    pair = ring_reduce(pair, "z", sizes["z"], 1, 2, direct)
    low = pair.astype(jnp.bfloat16)
    mine = (
        pair[0]
        + lax.ppermute(low[0], "xl", [(0, 1), (1, 0)]).astype(jnp.float32)
        + cross(low[1]).astype(jnp.float32)
        + lax.ppermute(low[1], "xh", [(0, 1), (1, 0)]).astype(jnp.float32)
    )
    full = ring_gather(mine.astype(jnp.bfloat16), "z", sizes["z"], 0, direct)
    full = ring_gather(full, "y", sizes["y"], 0, direct)
    out = []
    start = 0
    for w in grads:
        rows = w.shape[0] // 4
        out.append(full[start:start + rows].astype(jnp.float32))
        start += rows
    return out


def to_sequence(x):
    xh = lax.axis_index("xh")
    c = lax.axis_index("c")
    first = lax.ppermute(lax.dynamic_index_in_dim(x, c, 0, False), GRP, [(0, 0), (1, 2), (2, 1), (3, 3)])
    second = lax.ppermute(lax.dynamic_index_in_dim(x, 1 - c, 0, False), GRP, [(0, 2), (1, 0), (2, 3), (3, 1)])
    return jnp.where(xh == 0, jnp.concatenate([first, second]), jnp.concatenate([second, first]))


def from_sequence(x):
    xh = lax.axis_index("xh")
    c = lax.axis_index("c")
    length = x.shape[0] // 2
    first = jnp.where(xh == 0, x[:length], x[length:])
    second = jnp.where(xh == 0, x[length:], x[:length])
    first = lax.ppermute(first, GRP, [(0, 0), (1, 2), (2, 1), (3, 3)])
    second = lax.ppermute(second, GRP, [(2, 0), (0, 1), (3, 2), (1, 3)])
    return jnp.where(c == 0, jnp.stack([first, second]), jnp.stack([second, first]))


def body(
    tokens, segment, piece_start, w_query, w_key, w_value, w_out, w_gate, w_up, w_down, cotangent
):
    sizes = {"y": lax.axis_size("y"), "z": lax.axis_size("z"), "xl": lax.axis_size("xl")}
    width = tokens.shape[2]
    local_length = tokens.shape[1] * 2
    full_length = segment.shape[1]
    head_count = HEADS
    head_size = HDIM
    scale = head_size ** (-0.5)
    xh = lax.axis_index("xh")
    c = lax.axis_index("c")
    first_row = c * local_length
    rows = first_row + jnp.arange(local_length, dtype=jnp.int32)
    columns = jnp.arange(full_length, dtype=jnp.int32)
    inverse = 10000.0 ** (-jnp.arange(0, head_size, 2).astype(jnp.float32) / head_size)
    angles = rows.astype(jnp.float32)[:, None] * inverse[None, :]
    cosine = jnp.cos(angles)[:, None, :]
    sine = jnp.sin(angles)[:, None, :]

    query_weight, key_weight, value_weight = gather_weights(
        (w_query, w_key, w_value), "y", sizes, True
    )

    both_in = to_sequence(jnp.concatenate([tokens, cotangent], axis=2))
    hidden = both_in[:, :width].astype(jnp.float32)
    grad_result = both_in[:, width:]
    seg_row = lax.dynamic_index_in_dim(segment, xh, 0, False)
    start_row = lax.dynamic_index_in_dim(piece_start, xh, 0, False)

    def swap_halves(mine):
        other = lax.ppermute(mine, "c", [(0, 1), (1, 0)])
        return jnp.where(c == 0, jnp.concatenate([mine, other]), jnp.concatenate([other, mine]))

    normed, norm_one_back = jax.vjp(layer_norm, hidden)
    normed_low = normed.astype(jnp.bfloat16)
    query_heads = rotate(
        matmul(normed_low, query_weight).reshape(local_length, head_count, head_size),
        cosine,
        sine,
    ).astype(jnp.bfloat16)
    keys = (
        rotate(
            matmul(normed_low, key_weight).reshape(local_length, head_count, head_size),
            cosine,
            sine,
        )
        .reshape(local_length, width)
        .astype(jnp.bfloat16)
    )
    values = matmul(normed_low, value_weight).astype(jnp.bfloat16)
    w_out, w_down, w_gate, w_up, values = lax.optimization_barrier((w_out, w_down, w_gate, w_up, values))
    out_weight, down_weight = gather_weights((w_out, w_down), "z", sizes, False)
    gate_weight, up_weight = gather_weights((w_gate, w_up), "y", sizes, False)
    both = swap_halves(jnp.concatenate([keys, values], axis=1))
    seg_local = lax.dynamic_slice_in_dim(seg_row, first_row, local_length)
    start_local = lax.dynamic_slice_in_dim(start_row, first_row, local_length)
    masks = (
        rows[:, None],
        seg_local[:, None],
        start_local[:, None],
        seg_row[None, :],
        start_row[None, :],
    )
    query_flat = query_heads.reshape(local_length, width)
    mixed, log_total = attention_forward(query_flat, both, masks)
    mixed_low = mixed.reshape(local_length, width).astype(jnp.bfloat16)
    after = hidden + matmul(mixed_low, out_weight)
    normed_two, norm_two_back = jax.vjp(layer_norm, after)
    normed_two_low = normed_two.astype(jnp.bfloat16)
    gate = matmul(normed_two_low, gate_weight)
    upper = matmul(normed_two_low, up_weight)
    active, gate_back = jax.vjp(gated, gate, upper)
    active_low = active.astype(jnp.bfloat16)
    result = after + matmul(active_low, down_weight)
    result_low = result.astype(jnp.bfloat16)

    grads = [None] * 7
    grads[6] = contract_rows(active_low, grad_result)
    grad_active = contract_cols(grad_result, down_weight)
    grad_gate, grad_upper = gate_back(grad_active)
    gate_low = grad_gate.astype(jnp.bfloat16)
    upper_low = grad_upper.astype(jnp.bfloat16)
    grads[4] = contract_rows(normed_two_low, gate_low)
    grads[5] = contract_rows(normed_two_low, upper_low)
    grad_normed_two = contract_cols(gate_low, gate_weight) + contract_cols(upper_low, up_weight)
    grad_after = grad_result.astype(jnp.float32) + norm_two_back(grad_normed_two)[0]
    after_low = grad_after.astype(jnp.bfloat16)
    grads[3] = contract_rows(mixed_low, after_low)
    grad_mixed = (
        contract_cols(after_low, out_weight)
        .astype(jnp.bfloat16)
        .reshape(local_length, head_count, head_size)
    )
    grad_query, grad_keys, grad_values = attention_backward(
        query_flat, both, grad_mixed.reshape(local_length, width), log_total, masks
    )
    grad_query = grad_query.reshape(local_length, head_count, head_size)
    grad_kv = jnp.concatenate([grad_keys, grad_values], axis=1)
    early = reduce_group(
        [grads[6], grads[4].reshape(-1, width), grads[5].reshape(-1, width), grads[3]], sizes, False
    )
    early, grad_kv = lax.optimization_barrier((early, grad_kv))
    mine_kv = jnp.where(c == 0, grad_kv[:local_length], grad_kv[local_length:])
    theirs_kv = jnp.where(c == 0, grad_kv[local_length:], grad_kv[:local_length])
    own_kv = mine_kv + lax.ppermute(theirs_kv, "c", [(0, 1), (1, 0)])
    own_keys = own_kv[:, :width]
    own_values = own_kv[:, width:]
    query_low = (
        rotate(grad_query, cosine, -sine).reshape(local_length, width).astype(jnp.bfloat16)
    )
    keys_low = (
        rotate(own_keys.reshape(local_length, head_count, head_size), cosine, -sine)
        .reshape(local_length, width)
        .astype(jnp.bfloat16)
    )
    values_low = own_values.astype(jnp.bfloat16)
    grads[0] = contract_rows(normed_low, query_low)
    grads[1] = contract_rows(normed_low, keys_low)
    grads[2] = contract_rows(normed_low, values_low)
    grad_normed = (
        contract_cols(query_low, query_weight)
        + contract_cols(keys_low, key_weight)
        + contract_cols(values_low, value_weight)
    )
    grad_hidden = grad_after + norm_one_back(grad_normed)[0]
    both_out = from_sequence(jnp.concatenate([result_low, grad_hidden.astype(jnp.bfloat16)], axis=1))
    output = both_out[..., :width]
    input_grads = both_out[..., width:]
    late = reduce_group([grads[0], grads[1], grads[2]], sizes, True)
    gate_rows = grads[4].shape[0]
    gate_grad = early[1].reshape(gate_rows // 4, -1)
    up_grad = early[2].reshape(gate_rows // 4, -1)
    owned = [late[0], late[1], late[2], early[3], gate_grad, up_grad, early[0]]

    return (output, input_grads, *owned)


def solution(mesh):
    rep, grp = mesh.devices.shape
    side = int(round((rep // 2) ** 0.5))
    devices = mesh.devices.reshape(side, rep // (2 * side), 2, grp // 2, 2)
    fine = Mesh(devices, ("y", "z", "xl", "xh", "c"))
    seqs = P(REP, GRP, None)
    rows = P(GRP, None)
    placed = (seqs, P(REP, None), P(REP, None), rows, rows, rows, rows, rows, rows, rows, seqs)
    return jax.shard_map(
        body,
        mesh=fine,
        in_specs=placed,
        out_specs=(seqs, seqs, rows, rows, rows, rows, rows, rows, rows),
        check_vma=False,
    )
```

```python
import jax
import jax.numpy as jnp
from jax import lax
from jax.sharding import Mesh
from jax.sharding import PartitionSpec as P
from jax.experimental import pallas as pl
from jax.experimental.pallas import tpu as pltpu

HEADS = 12
HDIM = 64
REP = ("y", "z", "xl")
GRP = ("xh", "c")


def layer_norm(hidden):
    centred = hidden - jnp.mean(hidden, axis=-1, keepdims=True)
    spread = jnp.mean(centred * centred, axis=-1, keepdims=True)
    return centred * lax.rsqrt(spread + 1e-05)


def rotate(heads, cosine, sine):
    half = heads.shape[-1] // 2
    first = heads[..., :half]
    second = heads[..., half:]
    return jnp.concatenate(
        [first * cosine - second * sine, second * cosine + first * sine], axis=-1
    )


def gated(gate, upper):
    return gate / (1.0 + jnp.exp(-gate)) * upper


def matmul(left, right):
    return jnp.dot(left, right, preferred_element_type=jnp.float32)


def contract_rows(left, right):
    return lax.dot_general(
        left, right, (((0,), (0,)), ((), ())), preferred_element_type=jnp.float32
    )


def contract_cols(left, right):
    return lax.dot_general(
        left, right, (((1,), (1,)), ((), ())), preferred_element_type=jnp.float32
    )


def allowed_mask(rq_ref, sq_ref, pq_ref, sk_ref, pk_ref, rk_ref):
    return (sq_ref[...] == sk_ref[...]) & (
        (rk_ref[...] <= rq_ref[...]) | (pq_ref[...] == pk_ref[...])
    )


def attention_forward_kernel(
    q_ref, k_ref, v_ref, rq_ref, sq_ref, pq_ref, sk_ref, pk_ref, rk_ref, o_ref, lse_ref
):
    queries = q_ref.shape[0]
    keys = k_ref.shape[0]
    allowed = allowed_mask(rq_ref, sq_ref, pq_ref, sk_ref, pk_ref, rk_ref)
    scale = HDIM ** (-0.5)
    for h in range(q_ref.shape[1] // HDIM):
        cols = slice(h * HDIM, (h + 1) * HDIM)
        raw = lax.dot_general(
            q_ref[:, cols], k_ref[:, cols], (((1,), (1,)), ((), ())),
            preferred_element_type=jnp.float32,
        )
        scores = jnp.where(allowed, raw * scale, -1e30)
        highest = jnp.max(scores, axis=1, keepdims=True)
        expd = jnp.exp(scores - highest)
        total = jnp.sum(expd, axis=1, keepdims=True)
        probs_low = (expd / total).astype(jnp.bfloat16)
        o_ref[:, cols] = jnp.dot(probs_low, v_ref[:, cols], preferred_element_type=jnp.float32)
        lse_ref[:, h:h + 1] = highest + jnp.log(total)


def attention_backward_kernel(
    q_ref, k_ref, v_ref, do_ref, lse_ref, rq_ref, sq_ref, pq_ref, sk_ref, pk_ref, rk_ref,
    dq_ref, dk_ref, dv_ref,
):
    queries = q_ref.shape[0]
    keys = k_ref.shape[0]
    allowed = allowed_mask(rq_ref, sq_ref, pq_ref, sk_ref, pk_ref, rk_ref)
    scale = HDIM ** (-0.5)
    for h in range(q_ref.shape[1] // HDIM):
        cols = slice(h * HDIM, (h + 1) * HDIM)
        q = q_ref[:, cols]
        k = k_ref[:, cols]
        v = v_ref[:, cols]
        do = do_ref[:, cols]
        raw = lax.dot_general(q, k, (((1,), (1,)), ((), ())), preferred_element_type=jnp.float32)
        scores = jnp.where(allowed, raw * scale, -1e30)
        probs = jnp.exp(scores - lse_ref[:, h:h + 1])
        grad_probs = lax.dot_general(do, v, (((1,), (1,)), ((), ())), preferred_element_type=jnp.float32)
        inner = jnp.sum(probs * grad_probs, axis=1, keepdims=True)
        grad_raw = (probs * (grad_probs - inner) * scale).astype(jnp.bfloat16)
        dq_ref[:, cols] = jnp.dot(grad_raw, k, preferred_element_type=jnp.float32)
        dk_ref[:, cols] = lax.dot_general(
            grad_raw, q, (((0,), (0,)), ((), ())), preferred_element_type=jnp.float32
        )
        dv_ref[:, cols] = lax.dot_general(
            probs.astype(jnp.bfloat16), do, (((0,), (0,)), ((), ())), preferred_element_type=jnp.float32
        )


def mask_specs(queries, keys):
    column = pl.BlockSpec((queries, 1), lambda i: (0, 0))
    row = pl.BlockSpec((1, keys), lambda i: (0, 0))
    return [column, column, column, row, row, row]


def attention_forward(q, kv, masks):
    queries, width = q.shape
    keys = kv.shape[0]
    block = 2 * HDIM
    pairs = width // block
    return pl.pallas_call(
        attention_forward_kernel,
        grid=(pairs,),
        in_specs=[
            pl.BlockSpec((queries, block), lambda i: (0, i)),
            pl.BlockSpec((keys, block), lambda i: (0, i)),
            pl.BlockSpec((keys, block), lambda i, p=pairs: (0, i + p)),
        ] + mask_specs(queries, keys),
        out_specs=[
            pl.BlockSpec((queries, block), lambda i: (0, i)),
            pl.BlockSpec((None, queries, 2), lambda i: (i, 0, 0)),
        ],
        out_shape=[
            jax.ShapeDtypeStruct((queries, width), jnp.float32),
            jax.ShapeDtypeStruct((pairs, queries, 2), jnp.float32),
        ],
        compiler_params=pltpu.CompilerParams(dimension_semantics=("arbitrary",)),
        cost_estimate=pl.CostEstimate(
            flops=4 * queries * keys * width, transcendentals=queries * keys * HEADS,
            bytes_accessed=2 * (queries + 2 * keys) * width + 4 * queries * width,
        ),
    )(q, kv, kv, *masks)


def attention_backward(q, kv, do, lse, masks):
    queries, width = q.shape
    keys = kv.shape[0]
    block = 2 * HDIM
    pairs = width // block
    return pl.pallas_call(
        attention_backward_kernel,
        grid=(pairs,),
        in_specs=[
            pl.BlockSpec((queries, block), lambda i: (0, i)),
            pl.BlockSpec((keys, block), lambda i: (0, i)),
            pl.BlockSpec((keys, block), lambda i, p=pairs: (0, i + p)),
            pl.BlockSpec((queries, block), lambda i: (0, i)),
            pl.BlockSpec((None, queries, 2), lambda i: (i, 0, 0)),
        ] + mask_specs(queries, keys),
        out_specs=[
            pl.BlockSpec((queries, block), lambda i: (0, i)),
            pl.BlockSpec((keys, block), lambda i: (0, i)),
            pl.BlockSpec((keys, block), lambda i: (0, i)),
        ],
        out_shape=[
            jax.ShapeDtypeStruct((queries, width), jnp.float32),
            jax.ShapeDtypeStruct((keys, width), jnp.float32),
            jax.ShapeDtypeStruct((keys, width), jnp.float32),
        ],
        compiler_params=pltpu.CompilerParams(dimension_semantics=("arbitrary",)),
        cost_estimate=pl.CostEstimate(
            flops=10 * queries * keys * width, transcendentals=queries * keys * HEADS,
            bytes_accessed=2 * (2 * queries + 2 * keys) * width + 4 * (queries + 2 * keys) * width,
        ),
    )(q, kv, kv, do, lse, *masks)


def shift(x, axis, n, step):
    return lax.ppermute(x, axis, [(i, (i + step) % n) for i in range(n)])


def place(buf, piece, index, dim):
    start = [0] * buf.ndim
    start[dim] = index * piece.shape[dim]
    return lax.dynamic_update_slice(buf, piece, start)


def ring_gather(piece, axis, n, dim, direct=False):
    if n == 1:
        return piece
    me = lax.axis_index(axis)
    shape = list(piece.shape)
    shape[dim] *= n
    buf = place(jnp.zeros(shape, piece.dtype), piece, me, dim)
    if n == 2 or direct:
        for k in range(1, n):
            buf = place(buf, shift(piece, axis, n, k), (me - k) % n, dim)
        return buf
    back = piece
    ahead = piece
    for step in range(1, n // 2 + 1):
        if step < n - step:
            back = shift(back, axis, n, 1)
            ahead = shift(ahead, axis, n, -1)
            buf = place(buf, back, (me - step) % n, dim)
            buf = place(buf, ahead, (me + step) % n, dim)
        else:
            half = piece.shape[dim] // 2
            first = shift(lax.slice_in_dim(back, 0, half, axis=dim), axis, n, 1)
            second = shift(lax.slice_in_dim(ahead, half, piece.shape[dim], axis=dim), axis, n, -1)
            buf = place(buf, jnp.concatenate([first, second], axis=dim), (me + step) % n, dim)
    return buf


def ring_reduce(x, axis, n, dim, hdim, direct=False):
    if n == 1:
        return x
    me = lax.axis_index(axis)
    size = x.shape[dim] // n

    def chunk(k):
        return lax.dynamic_slice_in_dim(x, (k % n) * size, size, axis=dim)

    def low(v):
        return v.astype(jnp.bfloat16)

    if n == 2 or direct:
        acc = chunk(me)
        for k in range(1, n):
            acc = acc + shift(low(chunk(me + k)), axis, n, k).astype(jnp.float32)
        return acc
    assert n == 4
    half = x.shape[hdim] // 2

    def part(k, which):
        c = chunk(k)
        return lax.slice_in_dim(c, 0, half, axis=hdim) if which == 0 else lax.slice_in_dim(
            c, half, c.shape[hdim], axis=hdim
        )

    from_ahead = shift(low(jnp.stack([part(me - 2, 0), part(me - 1, 1)])), axis, n, -1)
    from_back = shift(low(jnp.stack([part(me + 2, 1), part(me + 1, 0)])), axis, n, 1)
    relay_ahead = shift(low(from_ahead[0].astype(jnp.float32) + part(me - 1, 0)), axis, n, -1)
    relay_back = shift(low(from_back[0].astype(jnp.float32) + part(me + 1, 1)), axis, n, 1)
    first = part(me, 0) + from_back[1].astype(jnp.float32) + relay_ahead.astype(jnp.float32)
    second = part(me, 1) + from_ahead[1].astype(jnp.float32) + relay_back.astype(jnp.float32)
    return jnp.concatenate([first, second], axis=hdim)


def cross(x):
    return lax.ppermute(x, ("xl", "xh"), [(i, 3 - i) for i in range(4)])


def swap_core(x):
    return lax.ppermute(x, "c", [(0, 1), (1, 0)])


def absolute(parts, rows):
    g = lax.axis_index("xh") * 2 + lax.axis_index("c")
    buf = jnp.zeros((4 * rows,) + parts[0].shape[1:], parts[0].dtype)
    for j, part in enumerate(parts):
        buf = place(buf, part, jnp.bitwise_xor(g, j), 0)
    return buf


def gather_group(own, axis, n, direct):
    size = own.shape[0] // n
    me = lax.axis_index(axis)
    mine = lax.dynamic_slice_in_dim(own, me * size, size, axis=0)
    other = ring_gather(cross(mine), axis, n, 0, direct)
    partner = swap_core(jnp.concatenate([own, other]))
    rows = own.shape[0]
    return [own, partner[:rows], other, partner[rows:]]


def gather_weights(group, axis, sizes, direct):
    parts = gather_group(jnp.concatenate(group), axis, sizes[axis], direct)
    out = []
    start = 0
    for s in group:
        rows = s.shape[0]
        out.append(absolute([p[start:start + rows] for p in parts], rows))
        start += rows
    return out


def reduce_group(grads, sizes, direct):
    g = lax.axis_index("xh") * 2 + lax.axis_index("c")

    def shard(w, j):
        rows = w.shape[0] // 4
        return lax.dynamic_slice_in_dim(w, jnp.bitwise_xor(g, j) * rows, rows, axis=0)

    send = jnp.concatenate([shard(w, 1) for w in grads] + [shard(w, 3) for w in grads])
    got = swap_core(send.astype(jnp.bfloat16))
    total = got.shape[0] // 2
    kept = jnp.stack(
        [jnp.concatenate([shard(w, 0) for w in grads]), jnp.concatenate([shard(w, 2) for w in grads])]
    )
    pair = kept.astype(jnp.float32) + got.reshape(2, total, -1).astype(jnp.float32)
    pair = ring_reduce(pair, "y", sizes["y"], 1, 2, direct)
    pair = ring_reduce(pair, "z", sizes["z"], 1, 2, direct)
    low = pair.astype(jnp.bfloat16)
    mine = (
        pair[0]
        + lax.ppermute(low[0], "xl", [(0, 1), (1, 0)]).astype(jnp.float32)
        + cross(low[1]).astype(jnp.float32)
        + lax.ppermute(low[1], "xh", [(0, 1), (1, 0)]).astype(jnp.float32)
    )
    full = ring_gather(mine.astype(jnp.bfloat16), "z", sizes["z"], 0, direct)
    full = ring_gather(full, "y", sizes["y"], 0, direct)
    out = []
    start = 0
    for w in grads:
        rows = w.shape[0] // 4
        out.append(full[start:start + rows].astype(jnp.float32))
        start += rows
    return out


def to_sequence(x):
    xh = lax.axis_index("xh")
    c = lax.axis_index("c")
    first = lax.ppermute(lax.dynamic_index_in_dim(x, c, 0, False), GRP, [(0, 0), (1, 2), (2, 1), (3, 3)])
    second = lax.ppermute(lax.dynamic_index_in_dim(x, 1 - c, 0, False), GRP, [(0, 2), (1, 0), (2, 3), (3, 1)])
    return jnp.where(xh == 0, jnp.concatenate([first, second]), jnp.concatenate([second, first]))


def from_sequence(x):
    xh = lax.axis_index("xh")
    c = lax.axis_index("c")
    length = x.shape[0] // 2
    first = jnp.where(xh == 0, x[:length], x[length:])
    second = jnp.where(xh == 0, x[length:], x[:length])
    first = lax.ppermute(first, GRP, [(0, 0), (1, 2), (2, 1), (3, 3)])
    second = lax.ppermute(second, GRP, [(2, 0), (0, 1), (3, 2), (1, 3)])
    return jnp.where(c == 0, jnp.stack([first, second]), jnp.stack([second, first]))


def body(
    tokens, segment, piece_start, w_query, w_key, w_value, w_out, w_gate, w_up, w_down, cotangent
):
    sizes = {"y": lax.axis_size("y"), "z": lax.axis_size("z"), "xl": lax.axis_size("xl")}
    width = tokens.shape[2]
    local_length = tokens.shape[1] * 2
    full_length = segment.shape[1]
    head_count = HEADS
    head_size = HDIM
    scale = head_size ** (-0.5)
    xh = lax.axis_index("xh")
    c = lax.axis_index("c")
    first_row = c * local_length
    rows = first_row + jnp.arange(local_length, dtype=jnp.int32)
    columns = jnp.arange(full_length, dtype=jnp.int32)
    inverse = 10000.0 ** (-jnp.arange(0, head_size, 2).astype(jnp.float32) / head_size)
    angles = rows.astype(jnp.float32)[:, None] * inverse[None, :]
    cosine = jnp.cos(angles)[:, None, :]
    sine = jnp.sin(angles)[:, None, :]

    query_weight, key_weight, value_weight = gather_weights(
        (w_query, w_key, w_value), "y", sizes, True
    )

    both_in = to_sequence(jnp.concatenate([tokens, cotangent], axis=2))
    hidden = both_in[:, :width].astype(jnp.float32)
    grad_result = both_in[:, width:]
    seg_row = lax.dynamic_index_in_dim(segment, xh, 0, False)
    start_row = lax.dynamic_index_in_dim(piece_start, xh, 0, False)

    normed, norm_one_back = jax.vjp(layer_norm, hidden)
    normed_low = normed.astype(jnp.bfloat16)
    query_heads = rotate(
        matmul(normed_low, query_weight).reshape(local_length, head_count, head_size),
        cosine,
        sine,
    ).astype(jnp.bfloat16)
    keys = (
        rotate(
            matmul(normed_low, key_weight).reshape(local_length, head_count, head_size),
            cosine,
            sine,
        )
        .reshape(local_length, width)
        .astype(jnp.bfloat16)
    )
    values = matmul(normed_low, value_weight).astype(jnp.bfloat16)
    w_out, w_down, w_gate, w_up, values = lax.optimization_barrier((w_out, w_down, w_gate, w_up, values))
    out_weight, down_weight = gather_weights((w_out, w_down), "z", sizes, False)
    gate_weight, up_weight = gather_weights((w_gate, w_up), "y", sizes, False)
    mine_kv = jnp.concatenate([keys, values], axis=1)
    both = jnp.concatenate([mine_kv, swap_core(mine_kv)])
    other_row = (1 - c) * local_length
    seg_local = lax.dynamic_slice_in_dim(seg_row, first_row, local_length)
    start_local = lax.dynamic_slice_in_dim(start_row, first_row, local_length)
    key_rows = jnp.concatenate([rows, other_row + jnp.arange(local_length, dtype=jnp.int32)])
    seg_keys = jnp.concatenate([seg_local, lax.dynamic_slice_in_dim(seg_row, other_row, local_length)])
    start_keys = jnp.concatenate(
        [start_local, lax.dynamic_slice_in_dim(start_row, other_row, local_length)]
    )
    masks = (
        rows[:, None],
        seg_local[:, None],
        start_local[:, None],
        seg_keys[None, :],
        start_keys[None, :],
        key_rows[None, :],
    )
    query_flat = query_heads.reshape(local_length, width)
    mixed, log_total = attention_forward(query_flat, both, masks)
    mixed_low = mixed.reshape(local_length, width).astype(jnp.bfloat16)
    after = hidden + matmul(mixed_low, out_weight)
    normed_two, norm_two_back = jax.vjp(layer_norm, after)
    normed_two_low = normed_two.astype(jnp.bfloat16)
    gate = matmul(normed_two_low, gate_weight)
    upper = matmul(normed_two_low, up_weight)
    active, gate_back = jax.vjp(gated, gate, upper)
    active_low = active.astype(jnp.bfloat16)
    result = after + matmul(active_low, down_weight)
    result_low = result.astype(jnp.bfloat16)

    grads = [None] * 7
    grads[6] = contract_rows(active_low, grad_result)
    grad_active = contract_cols(grad_result, down_weight)
    grad_gate, grad_upper = gate_back(grad_active)
    gate_low = grad_gate.astype(jnp.bfloat16)
    upper_low = grad_upper.astype(jnp.bfloat16)
    grads[4] = contract_rows(normed_two_low, gate_low)
    grads[5] = contract_rows(normed_two_low, upper_low)
    grad_normed_two = contract_cols(gate_low, gate_weight) + contract_cols(upper_low, up_weight)
    grad_after = grad_result.astype(jnp.float32) + norm_two_back(grad_normed_two)[0]
    after_low = grad_after.astype(jnp.bfloat16)
    grads[3] = contract_rows(mixed_low, after_low)
    grad_mixed = (
        contract_cols(after_low, out_weight)
        .astype(jnp.bfloat16)
        .reshape(local_length, head_count, head_size)
    )
    grad_query, grad_keys, grad_values = attention_backward(
        query_flat, both, grad_mixed.reshape(local_length, width), log_total, masks
    )
    grad_query = grad_query.reshape(local_length, head_count, head_size)
    grad_kv = jnp.concatenate([grad_keys, grad_values], axis=1)
    own_kv = grad_kv[:local_length] + swap_core(grad_kv[local_length:])
    own_keys = own_kv[:, :width]
    own_values = own_kv[:, width:]
    query_low = (
        rotate(grad_query, cosine, -sine).reshape(local_length, width).astype(jnp.bfloat16)
    )
    keys_low = (
        rotate(own_keys.reshape(local_length, head_count, head_size), cosine, -sine)
        .reshape(local_length, width)
        .astype(jnp.bfloat16)
    )
    values_low = own_values.astype(jnp.bfloat16)
    grads[0] = contract_rows(normed_low, query_low)
    grads[1] = contract_rows(normed_low, keys_low)
    grads[2] = contract_rows(normed_low, values_low)
    grad_normed = (
        contract_cols(query_low, query_weight)
        + contract_cols(keys_low, key_weight)
        + contract_cols(values_low, value_weight)
    )
    grad_hidden = grad_after + norm_one_back(grad_normed)[0]
    both_out = from_sequence(jnp.concatenate([result_low, grad_hidden.astype(jnp.bfloat16)], axis=1))
    output = both_out[..., :width]
    input_grads = both_out[..., width:]
    gate_rows = grads[4].shape[0]
    low = [w.astype(jnp.bfloat16) for w in grads]
    owned = reduce_group(
        [low[0], low[1], low[2], low[3], low[4].reshape(-1, width), low[5].reshape(-1, width), low[6]],
        sizes,
        False,
    )
    owned[4] = owned[4].reshape(gate_rows // 4, -1)
    owned[5] = owned[5].reshape(gate_rows // 4, -1)

    return (output, input_grads, *owned)


def solution(mesh):
    rep, grp = mesh.devices.shape
    side = int(round((rep // 2) ** 0.5))
    devices = mesh.devices.reshape(side, rep // (2 * side), 2, grp // 2, 2)
    fine = Mesh(devices, ("y", "z", "xl", "xh", "c"))
    seqs = P(REP, GRP, None)
    rows = P(GRP, None)
    placed = (seqs, P(REP, None), P(REP, None), rows, rows, rows, rows, rows, rows, rows, seqs)
    return jax.shard_map(
        body,
        mesh=fine,
        in_specs=placed,
        out_specs=(seqs, seqs, rows, rows, rows, rows, rows, rows, rows),
        check_vma=False,
    )
```

```python
import jax
import jax.numpy as jnp
from jax import lax
from jax.sharding import Mesh
from jax.sharding import PartitionSpec as P
from jax.experimental import pallas as pl
from jax.experimental.pallas import tpu as pltpu

HEADS = 12
HDIM = 64
REP = ("y", "z", "xl")
GRP = ("xh", "c")


def layer_norm(hidden):
    centred = hidden - jnp.mean(hidden, axis=-1, keepdims=True)
    spread = jnp.mean(centred * centred, axis=-1, keepdims=True)
    return centred * lax.rsqrt(spread + 1e-05)


def rotate(heads, cosine, sine):
    half = heads.shape[-1] // 2
    first = heads[..., :half]
    second = heads[..., half:]
    return jnp.concatenate(
        [first * cosine - second * sine, second * cosine + first * sine], axis=-1
    )


def gated(gate, upper):
    return gate / (1.0 + jnp.exp(-gate)) * upper


def matmul(left, right):
    return jnp.dot(left, right, preferred_element_type=jnp.float32)


def contract_rows(left, right):
    return lax.dot_general(
        left, right, (((0,), (0,)), ((), ())), preferred_element_type=jnp.float32
    )


def contract_cols(left, right):
    return lax.dot_general(
        left, right, (((1,), (1,)), ((), ())), preferred_element_type=jnp.float32
    )


def allowed_mask(rq_ref, sq_ref, pq_ref, sk_ref, pk_ref, rk_ref):
    return (sq_ref[...] == sk_ref[...]) & (
        (rk_ref[...] <= rq_ref[...]) | (pq_ref[...] == pk_ref[...])
    )


def attention_forward_kernel(
    q_ref, k_ref, v_ref, rq_ref, sq_ref, pq_ref, sk_ref, pk_ref, rk_ref, o_ref, lse_ref
):
    queries = q_ref.shape[0]
    keys = k_ref.shape[0]
    allowed = allowed_mask(rq_ref, sq_ref, pq_ref, sk_ref, pk_ref, rk_ref)
    scale = HDIM ** (-0.5)
    for h in range(q_ref.shape[1] // HDIM):
        cols = slice(h * HDIM, (h + 1) * HDIM)
        raw = lax.dot_general(
            q_ref[:, cols], k_ref[:, cols], (((1,), (1,)), ((), ())),
            preferred_element_type=jnp.float32,
        )
        scores = jnp.where(allowed, raw * scale, -1e30)
        highest = jnp.max(scores, axis=1, keepdims=True)
        expd = jnp.exp(scores - highest)
        total = jnp.sum(expd, axis=1, keepdims=True)
        probs_low = (expd / total).astype(jnp.bfloat16)
        o_ref[:, cols] = jnp.dot(probs_low, v_ref[:, cols], preferred_element_type=jnp.float32)
        lse_ref[:, h:h + 1] = highest + jnp.log(total)


def attention_backward_kernel(
    q_ref, k_ref, v_ref, do_ref, lse_ref, rq_ref, sq_ref, pq_ref, sk_ref, pk_ref, rk_ref,
    dq_ref, dk_ref, dv_ref,
):
    queries = q_ref.shape[0]
    keys = k_ref.shape[0]
    allowed = allowed_mask(rq_ref, sq_ref, pq_ref, sk_ref, pk_ref, rk_ref)
    scale = HDIM ** (-0.5)
    for h in range(q_ref.shape[1] // HDIM):
        cols = slice(h * HDIM, (h + 1) * HDIM)
        q = q_ref[:, cols]
        k = k_ref[:, cols]
        v = v_ref[:, cols]
        do = do_ref[:, cols]
        raw = lax.dot_general(q, k, (((1,), (1,)), ((), ())), preferred_element_type=jnp.float32)
        scores = jnp.where(allowed, raw * scale, -1e30)
        probs = jnp.exp(scores - lse_ref[:, h:h + 1])
        grad_probs = lax.dot_general(do, v, (((1,), (1,)), ((), ())), preferred_element_type=jnp.float32)
        inner = jnp.sum(probs * grad_probs, axis=1, keepdims=True)
        grad_raw = (probs * (grad_probs - inner) * scale).astype(jnp.bfloat16)
        dq_ref[:, cols] = jnp.dot(grad_raw, k, preferred_element_type=jnp.float32)
        dk_ref[:, cols] = lax.dot_general(
            grad_raw, q, (((0,), (0,)), ((), ())), preferred_element_type=jnp.float32
        )
        dv_ref[:, cols] = lax.dot_general(
            probs.astype(jnp.bfloat16), do, (((0,), (0,)), ((), ())), preferred_element_type=jnp.float32
        )


def mask_specs(queries, keys):
    column = pl.BlockSpec((queries, 1), lambda i: (0, 0))
    row = pl.BlockSpec((1, keys), lambda i: (0, 0))
    return [column, column, column, row, row, row]


def attention_forward(q, kv, masks):
    queries, width = q.shape
    keys = kv.shape[0]
    block = 2 * HDIM
    pairs = width // block
    return pl.pallas_call(
        attention_forward_kernel,
        grid=(pairs,),
        in_specs=[
            pl.BlockSpec((queries, block), lambda i: (0, i)),
            pl.BlockSpec((keys, block), lambda i: (0, i)),
            pl.BlockSpec((keys, block), lambda i, p=pairs: (0, i + p)),
        ] + mask_specs(queries, keys),
        out_specs=[
            pl.BlockSpec((queries, block), lambda i: (0, i)),
            pl.BlockSpec((None, queries, 2), lambda i: (i, 0, 0)),
        ],
        out_shape=[
            jax.ShapeDtypeStruct((queries, width), jnp.float32),
            jax.ShapeDtypeStruct((pairs, queries, 2), jnp.float32),
        ],
        compiler_params=pltpu.CompilerParams(dimension_semantics=("arbitrary",)),
        cost_estimate=pl.CostEstimate(
            flops=4 * queries * keys * width, transcendentals=queries * keys * HEADS,
            bytes_accessed=2 * (queries + 2 * keys) * width + 4 * queries * width,
        ),
    )(q, kv, kv, *masks)


def attention_backward(q, kv, do, lse, masks):
    queries, width = q.shape
    keys = kv.shape[0]
    block = 2 * HDIM
    pairs = width // block
    return pl.pallas_call(
        attention_backward_kernel,
        grid=(pairs,),
        in_specs=[
            pl.BlockSpec((queries, block), lambda i: (0, i)),
            pl.BlockSpec((keys, block), lambda i: (0, i)),
            pl.BlockSpec((keys, block), lambda i, p=pairs: (0, i + p)),
            pl.BlockSpec((queries, block), lambda i: (0, i)),
            pl.BlockSpec((None, queries, 2), lambda i: (i, 0, 0)),
        ] + mask_specs(queries, keys),
        out_specs=[
            pl.BlockSpec((queries, block), lambda i: (0, i)),
            pl.BlockSpec((keys, block), lambda i: (0, i)),
            pl.BlockSpec((keys, block), lambda i: (0, i)),
        ],
        out_shape=[
            jax.ShapeDtypeStruct((queries, width), jnp.float32),
            jax.ShapeDtypeStruct((keys, width), jnp.float32),
            jax.ShapeDtypeStruct((keys, width), jnp.float32),
        ],
        compiler_params=pltpu.CompilerParams(dimension_semantics=("arbitrary",)),
        cost_estimate=pl.CostEstimate(
            flops=10 * queries * keys * width, transcendentals=queries * keys * HEADS,
            bytes_accessed=2 * (2 * queries + 2 * keys) * width + 4 * (queries + 2 * keys) * width,
        ),
    )(q, kv, kv, do, lse, *masks)


def shift(x, axis, n, step):
    return lax.ppermute(x, axis, [(i, (i + step) % n) for i in range(n)])


def place(buf, piece, index, dim):
    start = [0] * buf.ndim
    start[dim] = index * piece.shape[dim]
    return lax.dynamic_update_slice(buf, piece, start)


def ring_gather(piece, axis, n, dim, direct=False):
    if n == 1:
        return piece
    me = lax.axis_index(axis)
    shape = list(piece.shape)
    shape[dim] *= n
    buf = place(jnp.zeros(shape, piece.dtype), piece, me, dim)
    if n == 2 or direct:
        for k in range(1, n):
            buf = place(buf, shift(piece, axis, n, k), (me - k) % n, dim)
        return buf
    back = piece
    ahead = piece
    for step in range(1, n // 2 + 1):
        if step < n - step:
            back = shift(back, axis, n, 1)
            ahead = shift(ahead, axis, n, -1)
            buf = place(buf, back, (me - step) % n, dim)
            buf = place(buf, ahead, (me + step) % n, dim)
        else:
            half = piece.shape[dim] // 2
            first = shift(lax.slice_in_dim(back, 0, half, axis=dim), axis, n, 1)
            second = shift(lax.slice_in_dim(ahead, half, piece.shape[dim], axis=dim), axis, n, -1)
            buf = place(buf, jnp.concatenate([first, second], axis=dim), (me + step) % n, dim)
    return buf


def ring_reduce(x, axis, n, dim, hdim, direct=False):
    if n == 1:
        return x
    me = lax.axis_index(axis)
    size = x.shape[dim] // n

    def chunk(k):
        return lax.dynamic_slice_in_dim(x, (k % n) * size, size, axis=dim)

    def low(v):
        return v.astype(jnp.bfloat16)

    if n == 2 or direct:
        acc = chunk(me)
        for k in range(1, n):
            acc = acc + shift(low(chunk(me + k)), axis, n, k).astype(jnp.float32)
        return acc
    assert n == 4
    half = x.shape[hdim] // 2

    def part(k, which):
        c = chunk(k)
        return lax.slice_in_dim(c, 0, half, axis=hdim) if which == 0 else lax.slice_in_dim(
            c, half, c.shape[hdim], axis=hdim
        )

    from_ahead = shift(low(jnp.stack([part(me - 2, 0), part(me - 1, 1)])), axis, n, -1)
    from_back = shift(low(jnp.stack([part(me + 2, 1), part(me + 1, 0)])), axis, n, 1)
    relay_ahead = shift(low(from_ahead[0].astype(jnp.float32) + part(me - 1, 0)), axis, n, -1)
    relay_back = shift(low(from_back[0].astype(jnp.float32) + part(me + 1, 1)), axis, n, 1)
    first = part(me, 0) + from_back[1].astype(jnp.float32) + relay_ahead.astype(jnp.float32)
    second = part(me, 1) + from_ahead[1].astype(jnp.float32) + relay_back.astype(jnp.float32)
    return jnp.concatenate([first, second], axis=hdim)


def cross(x):
    return lax.ppermute(x, ("xl", "xh"), [(i, 3 - i) for i in range(4)])


def swap_core(x):
    return lax.ppermute(x, "c", [(0, 1), (1, 0)])


def absolute(parts, rows):
    g = lax.axis_index("xh") * 2 + lax.axis_index("c")
    buf = jnp.zeros((4 * rows,) + parts[0].shape[1:], parts[0].dtype)
    for j, part in enumerate(parts):
        buf = place(buf, part, jnp.bitwise_xor(g, j), 0)
    return buf


def gather_group(own, axis, n, direct):
    size = own.shape[0] // n
    me = lax.axis_index(axis)
    mine = lax.dynamic_slice_in_dim(own, me * size, size, axis=0)
    other = ring_gather(cross(mine), axis, n, 0, direct)
    partner = swap_core(jnp.concatenate([own, other]))
    rows = own.shape[0]
    return [own, partner[:rows], other, partner[rows:]]


def gather_weights(group, axis, sizes, direct):
    parts = gather_group(jnp.concatenate(group), axis, sizes[axis], direct)
    out = []
    start = 0
    for s in group:
        rows = s.shape[0]
        out.append(absolute([p[start:start + rows] for p in parts], rows))
        start += rows
    return out


def reduce_group(grads, sizes, direct):
    g = lax.axis_index("xh") * 2 + lax.axis_index("c")

    def shard(w, j):
        rows = w.shape[0] // 4
        return lax.dynamic_slice_in_dim(w, jnp.bitwise_xor(g, j) * rows, rows, axis=0)

    send = jnp.concatenate([shard(w, 1) for w in grads] + [shard(w, 3) for w in grads])
    got = swap_core(send.astype(jnp.bfloat16))
    total = got.shape[0] // 2
    kept = jnp.stack(
        [jnp.concatenate([shard(w, 0) for w in grads]), jnp.concatenate([shard(w, 2) for w in grads])]
    )
    pair = kept.astype(jnp.float32) + got.reshape(2, total, -1).astype(jnp.float32)
    ny, nz = sizes["y"], sizes["z"]
    rows = pair.shape[1]
    own = ring_reduce(pair[0], "y", ny, 0, 1, direct)
    own = ring_reduce(own, "z", nz, 0, 1, direct)
    oth = ring_reduce(pair[1].reshape(ny, rows // ny, -1), "z", nz, 1, 2, direct)
    oth = ring_reduce(oth, "y", ny, 0, 2, direct).reshape(own.shape)
    low_own = own.astype(jnp.bfloat16)
    low_oth = oth.astype(jnp.bfloat16)
    mine = (
        own
        + lax.ppermute(low_own, "xl", [(0, 1), (1, 0)]).astype(jnp.float32)
        + cross(low_oth).astype(jnp.float32)
        + lax.ppermute(low_oth, "xh", [(0, 1), (1, 0)]).astype(jnp.float32)
    )
    full = ring_gather(mine.astype(jnp.bfloat16), "z", sizes["z"], 0, direct)
    full = ring_gather(full, "y", sizes["y"], 0, direct)
    out = []
    start = 0
    for w in grads:
        rows = w.shape[0] // 4
        out.append(full[start:start + rows].astype(jnp.float32))
        start += rows
    return out


def to_sequence(x):
    xh = lax.axis_index("xh")
    c = lax.axis_index("c")
    first = lax.ppermute(lax.dynamic_index_in_dim(x, c, 0, False), GRP, [(0, 0), (1, 2), (2, 1), (3, 3)])
    second = lax.ppermute(lax.dynamic_index_in_dim(x, 1 - c, 0, False), GRP, [(0, 2), (1, 0), (2, 3), (3, 1)])
    return jnp.where(xh == 0, jnp.concatenate([first, second]), jnp.concatenate([second, first]))


def from_sequence(x):
    xh = lax.axis_index("xh")
    c = lax.axis_index("c")
    length = x.shape[0] // 2
    first = jnp.where(xh == 0, x[:length], x[length:])
    second = jnp.where(xh == 0, x[length:], x[:length])
    first = lax.ppermute(first, GRP, [(0, 0), (1, 2), (2, 1), (3, 3)])
    second = lax.ppermute(second, GRP, [(2, 0), (0, 1), (3, 2), (1, 3)])
    return jnp.where(c == 0, jnp.stack([first, second]), jnp.stack([second, first]))


def body(
    tokens, segment, piece_start, w_query, w_key, w_value, w_out, w_gate, w_up, w_down, cotangent
):
    sizes = {"y": lax.axis_size("y"), "z": lax.axis_size("z"), "xl": lax.axis_size("xl")}
    width = tokens.shape[2]
    local_length = tokens.shape[1] * 2
    full_length = segment.shape[1]
    head_count = HEADS
    head_size = HDIM
    scale = head_size ** (-0.5)
    xh = lax.axis_index("xh")
    c = lax.axis_index("c")
    first_row = c * local_length
    rows = first_row + jnp.arange(local_length, dtype=jnp.int32)
    columns = jnp.arange(full_length, dtype=jnp.int32)
    inverse = 10000.0 ** (-jnp.arange(0, head_size, 2).astype(jnp.float32) / head_size)
    angles = rows.astype(jnp.float32)[:, None] * inverse[None, :]
    cosine = jnp.cos(angles)[:, None, :]
    sine = jnp.sin(angles)[:, None, :]

    query_weight, key_weight, value_weight = gather_weights(
        (w_query, w_key, w_value), "y", sizes, True
    )

    both_in = to_sequence(jnp.concatenate([tokens, cotangent], axis=2))
    hidden = both_in[:, :width].astype(jnp.float32)
    grad_result = both_in[:, width:]
    seg_row = lax.dynamic_index_in_dim(segment, xh, 0, False)
    start_row = lax.dynamic_index_in_dim(piece_start, xh, 0, False)

    normed, norm_one_back = jax.vjp(layer_norm, hidden)
    normed_low = normed.astype(jnp.bfloat16)
    query_heads = rotate(
        matmul(normed_low, query_weight).reshape(local_length, head_count, head_size),
        cosine,
        sine,
    ).astype(jnp.bfloat16)
    keys = (
        rotate(
            matmul(normed_low, key_weight).reshape(local_length, head_count, head_size),
            cosine,
            sine,
        )
        .reshape(local_length, width)
        .astype(jnp.bfloat16)
    )
    values = matmul(normed_low, value_weight).astype(jnp.bfloat16)
    w_out, w_down, w_gate, w_up, values = lax.optimization_barrier((w_out, w_down, w_gate, w_up, values))
    out_weight, down_weight = gather_weights((w_out, w_down), "z", sizes, False)
    gate_weight, up_weight = gather_weights((w_gate, w_up), "y", sizes, False)
    mine_kv = jnp.concatenate([keys, values], axis=1)
    both = jnp.concatenate([mine_kv, swap_core(mine_kv)])
    other_row = (1 - c) * local_length
    seg_local = lax.dynamic_slice_in_dim(seg_row, first_row, local_length)
    start_local = lax.dynamic_slice_in_dim(start_row, first_row, local_length)
    key_rows = jnp.concatenate([rows, other_row + jnp.arange(local_length, dtype=jnp.int32)])
    seg_keys = jnp.concatenate([seg_local, lax.dynamic_slice_in_dim(seg_row, other_row, local_length)])
    start_keys = jnp.concatenate(
        [start_local, lax.dynamic_slice_in_dim(start_row, other_row, local_length)]
    )
    masks = (
        rows[:, None],
        seg_local[:, None],
        start_local[:, None],
        seg_keys[None, :],
        start_keys[None, :],
        key_rows[None, :],
    )
    query_flat = query_heads.reshape(local_length, width)
    mixed, log_total = attention_forward(query_flat, both, masks)
    mixed_low = mixed.reshape(local_length, width).astype(jnp.bfloat16)
    after = hidden + matmul(mixed_low, out_weight)
    normed_two, norm_two_back = jax.vjp(layer_norm, after)
    normed_two_low = normed_two.astype(jnp.bfloat16)
    gate = matmul(normed_two_low, gate_weight)
    upper = matmul(normed_two_low, up_weight)
    active, gate_back = jax.vjp(gated, gate, upper)
    active_low = active.astype(jnp.bfloat16)
    result = after + matmul(active_low, down_weight)
    result_low = result.astype(jnp.bfloat16)

    grads = [None] * 7
    grads[6] = contract_rows(active_low, grad_result)
    grad_active = contract_cols(grad_result, down_weight)
    grad_gate, grad_upper = gate_back(grad_active)
    gate_low = grad_gate.astype(jnp.bfloat16)
    upper_low = grad_upper.astype(jnp.bfloat16)
    grads[4] = contract_rows(normed_two_low, gate_low)
    grads[5] = contract_rows(normed_two_low, upper_low)
    grad_normed_two = contract_cols(gate_low, gate_weight) + contract_cols(upper_low, up_weight)
    grad_after = grad_result.astype(jnp.float32) + norm_two_back(grad_normed_two)[0]
    after_low = grad_after.astype(jnp.bfloat16)
    grads[3] = contract_rows(mixed_low, after_low)
    grad_mixed = (
        contract_cols(after_low, out_weight)
        .astype(jnp.bfloat16)
        .reshape(local_length, head_count, head_size)
    )
    grad_query, grad_keys, grad_values = attention_backward(
        query_flat, both, grad_mixed.reshape(local_length, width), log_total, masks
    )
    grad_query = grad_query.reshape(local_length, head_count, head_size)
    grad_kv = jnp.concatenate([grad_keys, grad_values], axis=1)
    own_kv = grad_kv[:local_length] + swap_core(grad_kv[local_length:])
    own_keys = own_kv[:, :width]
    own_values = own_kv[:, width:]
    query_low = (
        rotate(grad_query, cosine, -sine).reshape(local_length, width).astype(jnp.bfloat16)
    )
    keys_low = (
        rotate(own_keys.reshape(local_length, head_count, head_size), cosine, -sine)
        .reshape(local_length, width)
        .astype(jnp.bfloat16)
    )
    values_low = own_values.astype(jnp.bfloat16)
    grads[0] = contract_rows(normed_low, query_low)
    grads[1] = contract_rows(normed_low, keys_low)
    grads[2] = contract_rows(normed_low, values_low)
    grad_normed = (
        contract_cols(query_low, query_weight)
        + contract_cols(keys_low, key_weight)
        + contract_cols(values_low, value_weight)
    )
    grad_hidden = grad_after + norm_one_back(grad_normed)[0]
    both_out = from_sequence(jnp.concatenate([result_low, grad_hidden.astype(jnp.bfloat16)], axis=1))
    output = both_out[..., :width]
    input_grads = both_out[..., width:]
    gate_rows = grads[4].shape[0]
    low = [w.astype(jnp.bfloat16) for w in grads]
    owned = reduce_group(
        [low[0], low[1], low[2], low[3], low[4].reshape(-1, width), low[5].reshape(-1, width), low[6]],
        sizes,
        False,
    )
    owned[4] = owned[4].reshape(gate_rows // 4, -1)
    owned[5] = owned[5].reshape(gate_rows // 4, -1)

    return (output, input_grads, *owned)


def solution(mesh):
    rep, grp = mesh.devices.shape
    side = int(round((rep // 2) ** 0.5))
    devices = mesh.devices.reshape(side, rep // (2 * side), 2, grp // 2, 2)
    fine = Mesh(devices, ("y", "z", "xl", "xh", "c"))
    seqs = P(REP, GRP, None)
    rows = P(GRP, None)
    placed = (seqs, P(REP, None), P(REP, None), rows, rows, rows, rows, rows, rows, rows, seqs)
    return jax.shard_map(
        body,
        mesh=fine,
        in_specs=placed,
        out_specs=(seqs, seqs, rows, rows, rows, rows, rows, rows, rows),
        check_vma=False,
    )
```

```python
import jax
import jax.numpy as jnp
from jax import lax
from jax.sharding import Mesh
from jax.sharding import PartitionSpec as P
from jax.experimental import pallas as pl
from jax.experimental.pallas import tpu as pltpu

HEADS = 12
HDIM = 64
REP = ("y", "z", "xl")
GRP = ("xh", "c")


def layer_norm(hidden):
    centred = hidden - jnp.mean(hidden, axis=-1, keepdims=True)
    spread = jnp.mean(centred * centred, axis=-1, keepdims=True)
    return centred * lax.rsqrt(spread + 1e-05)


def rotate(heads, cosine, sine):
    half = heads.shape[-1] // 2
    first = heads[..., :half]
    second = heads[..., half:]
    return jnp.concatenate(
        [first * cosine - second * sine, second * cosine + first * sine], axis=-1
    )


def gated(gate, upper):
    return gate / (1.0 + jnp.exp(-gate)) * upper


def matmul(left, right):
    return jnp.dot(left, right, preferred_element_type=jnp.float32)


def contract_rows(left, right):
    return lax.dot_general(
        left, right, (((0,), (0,)), ((), ())), preferred_element_type=jnp.float32
    )


def contract_cols(left, right):
    return lax.dot_general(
        left, right, (((1,), (1,)), ((), ())), preferred_element_type=jnp.float32
    )


def allowed_mask(rq_ref, sq_ref, pq_ref, sk_ref, pk_ref, rk_ref):
    return (sq_ref[...] == sk_ref[...]) & (
        (rk_ref[...] <= rq_ref[...]) | (pq_ref[...] == pk_ref[...])
    )


def attention_forward_kernel(
    q_ref, k_ref, v_ref, rq_ref, sq_ref, pq_ref, sk_ref, pk_ref, rk_ref, o_ref, lse_ref
):
    queries = q_ref.shape[0]
    keys = k_ref.shape[0]
    allowed = allowed_mask(rq_ref, sq_ref, pq_ref, sk_ref, pk_ref, rk_ref)
    scale = HDIM ** (-0.5)
    for h in range(q_ref.shape[1] // HDIM):
        cols = slice(h * HDIM, (h + 1) * HDIM)
        raw = lax.dot_general(
            q_ref[:, cols], k_ref[:, cols], (((1,), (1,)), ((), ())),
            preferred_element_type=jnp.float32,
        )
        scores = jnp.where(allowed, raw * scale, -1e30)
        highest = jnp.max(scores, axis=1, keepdims=True)
        expd = jnp.exp(scores - highest)
        total = jnp.sum(expd, axis=1, keepdims=True)
        probs_low = (expd / total).astype(jnp.bfloat16)
        o_ref[:, cols] = jnp.dot(probs_low, v_ref[:, cols], preferred_element_type=jnp.float32)
        lse_ref[:, h:h + 1] = highest + jnp.log(total)


def attention_backward_kernel(
    q_ref, k_ref, v_ref, do_ref, lse_ref, rq_ref, sq_ref, pq_ref, sk_ref, pk_ref, rk_ref,
    dq_ref, dk_ref, dv_ref,
):
    queries = q_ref.shape[0]
    keys = k_ref.shape[0]
    allowed = allowed_mask(rq_ref, sq_ref, pq_ref, sk_ref, pk_ref, rk_ref)
    scale = HDIM ** (-0.5)
    for h in range(q_ref.shape[1] // HDIM):
        cols = slice(h * HDIM, (h + 1) * HDIM)
        q = q_ref[:, cols]
        k = k_ref[:, cols]
        v = v_ref[:, cols]
        do = do_ref[:, cols]
        raw = lax.dot_general(q, k, (((1,), (1,)), ((), ())), preferred_element_type=jnp.float32)
        scores = jnp.where(allowed, raw * scale, -1e30)
        probs = jnp.exp(scores - lse_ref[:, h:h + 1])
        grad_probs = lax.dot_general(do, v, (((1,), (1,)), ((), ())), preferred_element_type=jnp.float32)
        inner = jnp.sum(probs * grad_probs, axis=1, keepdims=True)
        grad_raw = (probs * (grad_probs - inner) * scale).astype(jnp.bfloat16)
        dq_ref[:, cols] = jnp.dot(grad_raw, k, preferred_element_type=jnp.float32)
        dk_ref[:, cols] = lax.dot_general(
            grad_raw, q, (((0,), (0,)), ((), ())), preferred_element_type=jnp.float32
        )
        dv_ref[:, cols] = lax.dot_general(
            probs.astype(jnp.bfloat16), do, (((0,), (0,)), ((), ())), preferred_element_type=jnp.float32
        )


def mask_specs(queries, keys):
    column = pl.BlockSpec((queries, 1), lambda i: (0, 0))
    row = pl.BlockSpec((1, keys), lambda i: (0, 0))
    return [column, column, column, row, row, row]


def attention_forward(q, kv, masks):
    queries, width = q.shape
    keys = kv.shape[0]
    block = 2 * HDIM
    pairs = width // block
    return pl.pallas_call(
        attention_forward_kernel,
        grid=(pairs,),
        in_specs=[
            pl.BlockSpec((queries, block), lambda i: (0, i)),
            pl.BlockSpec((keys, block), lambda i: (0, i)),
            pl.BlockSpec((keys, block), lambda i, p=pairs: (0, i + p)),
        ] + mask_specs(queries, keys),
        out_specs=[
            pl.BlockSpec((queries, block), lambda i: (0, i)),
            pl.BlockSpec((None, queries, 2), lambda i: (i, 0, 0)),
        ],
        out_shape=[
            jax.ShapeDtypeStruct((queries, width), jnp.float32),
            jax.ShapeDtypeStruct((pairs, queries, 2), jnp.float32),
        ],
        compiler_params=pltpu.CompilerParams(dimension_semantics=("arbitrary",)),
        cost_estimate=pl.CostEstimate(
            flops=4 * queries * keys * width, transcendentals=queries * keys * HEADS,
            bytes_accessed=2 * (queries + 2 * keys) * width + 4 * queries * width,
        ),
    )(q, kv, kv, *masks)


def attention_backward(q, kv, do, lse, masks):
    queries, width = q.shape
    keys = kv.shape[0]
    block = 2 * HDIM
    pairs = width // block
    return pl.pallas_call(
        attention_backward_kernel,
        grid=(pairs,),
        in_specs=[
            pl.BlockSpec((queries, block), lambda i: (0, i)),
            pl.BlockSpec((keys, block), lambda i: (0, i)),
            pl.BlockSpec((keys, block), lambda i, p=pairs: (0, i + p)),
            pl.BlockSpec((queries, block), lambda i: (0, i)),
            pl.BlockSpec((None, queries, 2), lambda i: (i, 0, 0)),
        ] + mask_specs(queries, keys),
        out_specs=[
            pl.BlockSpec((queries, block), lambda i: (0, i)),
            pl.BlockSpec((keys, block), lambda i: (0, i)),
            pl.BlockSpec((keys, block), lambda i: (0, i)),
        ],
        out_shape=[
            jax.ShapeDtypeStruct((queries, width), jnp.float32),
            jax.ShapeDtypeStruct((keys, width), jnp.float32),
            jax.ShapeDtypeStruct((keys, width), jnp.float32),
        ],
        compiler_params=pltpu.CompilerParams(dimension_semantics=("arbitrary",)),
        cost_estimate=pl.CostEstimate(
            flops=10 * queries * keys * width, transcendentals=queries * keys * HEADS,
            bytes_accessed=2 * (2 * queries + 2 * keys) * width + 4 * (queries + 2 * keys) * width,
        ),
    )(q, kv, kv, do, lse, *masks)


def shift(x, axis, n, step):
    return lax.ppermute(x, axis, [(i, (i + step) % n) for i in range(n)])


def place(buf, piece, index, dim):
    start = [0] * buf.ndim
    start[dim] = index * piece.shape[dim]
    return lax.dynamic_update_slice(buf, piece, start)


def ring_gather(piece, axis, n, dim, direct=False):
    if n == 1:
        return piece
    me = lax.axis_index(axis)
    shape = list(piece.shape)
    shape[dim] *= n
    buf = place(jnp.zeros(shape, piece.dtype), piece, me, dim)
    if n == 2 or direct:
        for k in range(1, n):
            buf = place(buf, shift(piece, axis, n, k), (me - k) % n, dim)
        return buf
    back = piece
    ahead = piece
    for step in range(1, n // 2 + 1):
        if step < n - step:
            back = shift(back, axis, n, 1)
            ahead = shift(ahead, axis, n, -1)
            buf = place(buf, back, (me - step) % n, dim)
            buf = place(buf, ahead, (me + step) % n, dim)
        else:
            half = piece.shape[dim] // 2
            first = shift(lax.slice_in_dim(back, 0, half, axis=dim), axis, n, 1)
            second = shift(lax.slice_in_dim(ahead, half, piece.shape[dim], axis=dim), axis, n, -1)
            buf = place(buf, jnp.concatenate([first, second], axis=dim), (me + step) % n, dim)
    return buf


def ring_reduce(x, axis, n, dim, hdim, direct=False):
    if n == 1:
        return x
    me = lax.axis_index(axis)
    size = x.shape[dim] // n

    def chunk(k):
        return lax.dynamic_slice_in_dim(x, (k % n) * size, size, axis=dim)

    def low(v):
        return v.astype(jnp.bfloat16)

    if n == 2 or direct:
        acc = chunk(me)
        for k in range(1, n):
            acc = acc + shift(low(chunk(me + k)), axis, n, k).astype(jnp.float32)
        return acc
    assert n == 4
    half = x.shape[hdim] // 2

    def part(k, which):
        c = chunk(k)
        return lax.slice_in_dim(c, 0, half, axis=hdim) if which == 0 else lax.slice_in_dim(
            c, half, c.shape[hdim], axis=hdim
        )

    from_ahead = shift(low(jnp.stack([part(me - 2, 0), part(me - 1, 1)])), axis, n, -1)
    from_back = shift(low(jnp.stack([part(me + 2, 1), part(me + 1, 0)])), axis, n, 1)
    relay_ahead = shift(low(from_ahead[0].astype(jnp.float32) + part(me - 1, 0)), axis, n, -1)
    relay_back = shift(low(from_back[0].astype(jnp.float32) + part(me + 1, 1)), axis, n, 1)
    first = part(me, 0) + from_back[1].astype(jnp.float32) + relay_ahead.astype(jnp.float32)
    second = part(me, 1) + from_ahead[1].astype(jnp.float32) + relay_back.astype(jnp.float32)
    return jnp.concatenate([first, second], axis=hdim)


def cross(x):
    return lax.ppermute(x, ("xl", "xh"), [(i, 3 - i) for i in range(4)])


def swap_core(x):
    return lax.ppermute(x, "c", [(0, 1), (1, 0)])


def absolute(parts, rows):
    g = lax.axis_index("xh") * 2 + lax.axis_index("c")
    buf = jnp.zeros((4 * rows,) + parts[0].shape[1:], parts[0].dtype)
    for j, part in enumerate(parts):
        buf = place(buf, part, jnp.bitwise_xor(g, j), 0)
    return buf


def gather_group(own, axis, n, direct):
    size = own.shape[0] // n
    me = lax.axis_index(axis)
    mine = lax.dynamic_slice_in_dim(own, me * size, size, axis=0)
    other = ring_gather(cross(mine), axis, n, 0, direct)
    partner = swap_core(jnp.concatenate([own, other]))
    rows = own.shape[0]
    return [own, partner[:rows], other, partner[rows:]]


def gather_weights(group, axis, sizes, direct):
    parts = gather_group(jnp.concatenate(group), axis, sizes[axis], direct)
    out = []
    start = 0
    for s in group:
        rows = s.shape[0]
        out.append(absolute([p[start:start + rows] for p in parts], rows))
        start += rows
    return out


def reduce_group(grads, sizes, direct):
    g = lax.axis_index("xh") * 2 + lax.axis_index("c")

    def shard(w, j):
        rows = w.shape[0] // 4
        return lax.dynamic_slice_in_dim(w, jnp.bitwise_xor(g, j) * rows, rows, axis=0)

    send = jnp.concatenate([shard(w, 1) for w in grads] + [shard(w, 3) for w in grads])
    got = swap_core(send.astype(jnp.bfloat16))
    total = got.shape[0] // 2
    kept = jnp.stack(
        [jnp.concatenate([shard(w, 0) for w in grads]), jnp.concatenate([shard(w, 2) for w in grads])]
    )
    pair = kept.astype(jnp.float32) + got.reshape(2, total, -1).astype(jnp.float32)
    ny, nz = sizes["y"], sizes["z"]
    rows = pair.shape[1]
    own = ring_reduce(pair[0], "y", ny, 0, 1, direct)
    own = ring_reduce(own, "z", nz, 0, 1, True)
    oth = ring_reduce(pair[1].reshape(ny, rows // ny, -1), "z", nz, 1, 2, direct)
    oth = ring_reduce(oth, "y", ny, 0, 2, True).reshape(own.shape)
    low_own = own.astype(jnp.bfloat16)
    low_oth = oth.astype(jnp.bfloat16)
    mine = (
        own
        + lax.ppermute(low_own, "xl", [(0, 1), (1, 0)]).astype(jnp.float32)
        + cross(low_oth).astype(jnp.float32)
        + lax.ppermute(low_oth, "xh", [(0, 1), (1, 0)]).astype(jnp.float32)
    )
    full = ring_gather(mine.astype(jnp.bfloat16), "z", sizes["z"], 0, True)
    full = ring_gather(full, "y", sizes["y"], 0, direct)
    out = []
    start = 0
    for w in grads:
        rows = w.shape[0] // 4
        out.append(full[start:start + rows].astype(jnp.float32))
        start += rows
    return out


def to_sequence(x):
    xh = lax.axis_index("xh")
    c = lax.axis_index("c")
    first = lax.ppermute(lax.dynamic_index_in_dim(x, c, 0, False), GRP, [(0, 0), (1, 2), (2, 1), (3, 3)])
    second = lax.ppermute(lax.dynamic_index_in_dim(x, 1 - c, 0, False), GRP, [(0, 2), (1, 0), (2, 3), (3, 1)])
    return jnp.where(xh == 0, jnp.concatenate([first, second]), jnp.concatenate([second, first]))


def from_sequence(x):
    xh = lax.axis_index("xh")
    c = lax.axis_index("c")
    length = x.shape[0] // 2
    first = jnp.where(xh == 0, x[:length], x[length:])
    second = jnp.where(xh == 0, x[length:], x[:length])
    first = lax.ppermute(first, GRP, [(0, 0), (1, 2), (2, 1), (3, 3)])
    second = lax.ppermute(second, GRP, [(2, 0), (0, 1), (3, 2), (1, 3)])
    return jnp.where(c == 0, jnp.stack([first, second]), jnp.stack([second, first]))


def body(
    tokens, segment, piece_start, w_query, w_key, w_value, w_out, w_gate, w_up, w_down, cotangent
):
    sizes = {"y": lax.axis_size("y"), "z": lax.axis_size("z"), "xl": lax.axis_size("xl")}
    width = tokens.shape[2]
    local_length = tokens.shape[1] * 2
    full_length = segment.shape[1]
    head_count = HEADS
    head_size = HDIM
    scale = head_size ** (-0.5)
    xh = lax.axis_index("xh")
    c = lax.axis_index("c")
    first_row = c * local_length
    rows = first_row + jnp.arange(local_length, dtype=jnp.int32)
    columns = jnp.arange(full_length, dtype=jnp.int32)
    inverse = 10000.0 ** (-jnp.arange(0, head_size, 2).astype(jnp.float32) / head_size)
    angles = rows.astype(jnp.float32)[:, None] * inverse[None, :]
    cosine = jnp.cos(angles)[:, None, :]
    sine = jnp.sin(angles)[:, None, :]

    query_weight, key_weight, value_weight = gather_weights(
        (w_query, w_key, w_value), "y", sizes, True
    )

    both_in = to_sequence(jnp.concatenate([tokens, cotangent], axis=2))
    hidden = both_in[:, :width].astype(jnp.float32)
    grad_result = both_in[:, width:]
    seg_row = lax.dynamic_index_in_dim(segment, xh, 0, False)
    start_row = lax.dynamic_index_in_dim(piece_start, xh, 0, False)

    normed, norm_one_back = jax.vjp(layer_norm, hidden)
    normed_low = normed.astype(jnp.bfloat16)
    query_heads = rotate(
        matmul(normed_low, query_weight).reshape(local_length, head_count, head_size),
        cosine,
        sine,
    ).astype(jnp.bfloat16)
    keys = (
        rotate(
            matmul(normed_low, key_weight).reshape(local_length, head_count, head_size),
            cosine,
            sine,
        )
        .reshape(local_length, width)
        .astype(jnp.bfloat16)
    )
    values = matmul(normed_low, value_weight).astype(jnp.bfloat16)
    w_out, w_down, w_gate, w_up, values = lax.optimization_barrier((w_out, w_down, w_gate, w_up, values))
    out_weight, down_weight = gather_weights((w_out, w_down), "z", sizes, False)
    gate_weight, up_weight = gather_weights((w_gate, w_up), "y", sizes, False)
    mine_kv = jnp.concatenate([keys, values], axis=1)
    both = jnp.concatenate([mine_kv, swap_core(mine_kv)])
    other_row = (1 - c) * local_length
    seg_local = lax.dynamic_slice_in_dim(seg_row, first_row, local_length)
    start_local = lax.dynamic_slice_in_dim(start_row, first_row, local_length)
    key_rows = jnp.concatenate([rows, other_row + jnp.arange(local_length, dtype=jnp.int32)])
    seg_keys = jnp.concatenate([seg_local, lax.dynamic_slice_in_dim(seg_row, other_row, local_length)])
    start_keys = jnp.concatenate(
        [start_local, lax.dynamic_slice_in_dim(start_row, other_row, local_length)]
    )
    masks = (
        rows[:, None],
        seg_local[:, None],
        start_local[:, None],
        seg_keys[None, :],
        start_keys[None, :],
        key_rows[None, :],
    )
    query_flat = query_heads.reshape(local_length, width)
    mixed, log_total = attention_forward(query_flat, both, masks)
    mixed_low = mixed.reshape(local_length, width).astype(jnp.bfloat16)
    after = hidden + matmul(mixed_low, out_weight)
    normed_two, norm_two_back = jax.vjp(layer_norm, after)
    normed_two_low = normed_two.astype(jnp.bfloat16)
    gate = matmul(normed_two_low, gate_weight)
    upper = matmul(normed_two_low, up_weight)
    active, gate_back = jax.vjp(gated, gate, upper)
    active_low = active.astype(jnp.bfloat16)
    result = after + matmul(active_low, down_weight)
    result_low = result.astype(jnp.bfloat16)

    grads = [None] * 7
    grads[6] = contract_rows(active_low, grad_result)
    grad_active = contract_cols(grad_result, down_weight)
    grad_gate, grad_upper = gate_back(grad_active)
    gate_low = grad_gate.astype(jnp.bfloat16)
    upper_low = grad_upper.astype(jnp.bfloat16)
    grads[4] = contract_rows(normed_two_low, gate_low)
    grads[5] = contract_rows(normed_two_low, upper_low)
    grad_normed_two = contract_cols(gate_low, gate_weight) + contract_cols(upper_low, up_weight)
    grad_after = grad_result.astype(jnp.float32) + norm_two_back(grad_normed_two)[0]
    after_low = grad_after.astype(jnp.bfloat16)
    grads[3] = contract_rows(mixed_low, after_low)
    grad_mixed = (
        contract_cols(after_low, out_weight)
        .astype(jnp.bfloat16)
        .reshape(local_length, head_count, head_size)
    )
    grad_query, grad_keys, grad_values = attention_backward(
        query_flat, both, grad_mixed.reshape(local_length, width), log_total, masks
    )
    grad_query = grad_query.reshape(local_length, head_count, head_size)
    grad_kv = jnp.concatenate([grad_keys, grad_values], axis=1)
    own_kv = grad_kv[:local_length] + swap_core(grad_kv[local_length:])
    own_keys = own_kv[:, :width]
    own_values = own_kv[:, width:]
    query_low = (
        rotate(grad_query, cosine, -sine).reshape(local_length, width).astype(jnp.bfloat16)
    )
    keys_low = (
        rotate(own_keys.reshape(local_length, head_count, head_size), cosine, -sine)
        .reshape(local_length, width)
        .astype(jnp.bfloat16)
    )
    values_low = own_values.astype(jnp.bfloat16)
    grads[0] = contract_rows(normed_low, query_low)
    grads[1] = contract_rows(normed_low, keys_low)
    grads[2] = contract_rows(normed_low, values_low)
    grad_normed = (
        contract_cols(query_low, query_weight)
        + contract_cols(keys_low, key_weight)
        + contract_cols(values_low, value_weight)
    )
    grad_hidden = grad_after + norm_one_back(grad_normed)[0]
    both_out = from_sequence(jnp.concatenate([result_low, grad_hidden.astype(jnp.bfloat16)], axis=1))
    output = both_out[..., :width]
    input_grads = both_out[..., width:]
    gate_rows = grads[4].shape[0]
    low = [w.astype(jnp.bfloat16) for w in grads]
    owned = reduce_group(
        [low[0], low[1], low[2], low[3], low[4].reshape(-1, width), low[5].reshape(-1, width), low[6]],
        sizes,
        False,
    )
    owned[4] = owned[4].reshape(gate_rows // 4, -1)
    owned[5] = owned[5].reshape(gate_rows // 4, -1)

    return (output, input_grads, *owned)


def solution(mesh):
    rep, grp = mesh.devices.shape
    side = int(round((rep // 2) ** 0.5))
    devices = mesh.devices.reshape(side, rep // (2 * side), 2, grp // 2, 2)
    fine = Mesh(devices, ("y", "z", "xl", "xh", "c"))
    seqs = P(REP, GRP, None)
    rows = P(GRP, None)
    placed = (seqs, P(REP, None), P(REP, None), rows, rows, rows, rows, rows, rows, rows, seqs)
    return jax.shard_map(
        body,
        mesh=fine,
        in_specs=placed,
        out_specs=(seqs, seqs, rows, rows, rows, rows, rows, rows, rows),
        check_vma=False,
    )
```

```python
import jax
import jax.numpy as jnp
from jax import lax
from jax.sharding import Mesh
from jax.sharding import PartitionSpec as P
from jax.experimental import pallas as pl
from jax.experimental.pallas import tpu as pltpu

HEADS = 12
HDIM = 64
REP = ("y", "z", "xl")
GRP = ("xh", "c")


def layer_norm(hidden):
    centred = hidden - jnp.mean(hidden, axis=-1, keepdims=True)
    spread = jnp.mean(centred * centred, axis=-1, keepdims=True)
    return centred * lax.rsqrt(spread + 1e-05)


def rotate(heads, cosine, sine):
    half = heads.shape[-1] // 2
    first = heads[..., :half]
    second = heads[..., half:]
    return jnp.concatenate(
        [first * cosine - second * sine, second * cosine + first * sine], axis=-1
    )


def gated(gate, upper):
    return gate / (1.0 + jnp.exp(-gate)) * upper


def matmul(left, right):
    return jnp.dot(left, right, preferred_element_type=jnp.float32)


def contract_rows(left, right):
    return lax.dot_general(
        left, right, (((0,), (0,)), ((), ())), preferred_element_type=jnp.float32
    )


def contract_cols(left, right):
    return lax.dot_general(
        left, right, (((1,), (1,)), ((), ())), preferred_element_type=jnp.float32
    )


def allowed_mask(rq_ref, sq_ref, pq_ref, sk_ref, pk_ref, rk_ref):
    return (sq_ref[...] == sk_ref[...]) & (
        (rk_ref[...] <= rq_ref[...]) | (pq_ref[...] == pk_ref[...])
    )


def attention_forward_kernel(
    q_ref, k_ref, v_ref, rq_ref, sq_ref, pq_ref, sk_ref, pk_ref, rk_ref, o_ref, lse_ref
):
    queries = q_ref.shape[0]
    keys = k_ref.shape[0]
    allowed = allowed_mask(rq_ref, sq_ref, pq_ref, sk_ref, pk_ref, rk_ref)
    scale = HDIM ** (-0.5)
    for h in range(q_ref.shape[1] // HDIM):
        cols = slice(h * HDIM, (h + 1) * HDIM)
        raw = lax.dot_general(
            q_ref[:, cols], k_ref[:, cols], (((1,), (1,)), ((), ())),
            preferred_element_type=jnp.float32,
        )
        scores = jnp.where(allowed, raw * scale, -1e30)
        highest = jnp.max(scores, axis=1, keepdims=True)
        expd = jnp.exp(scores - highest)
        total = jnp.sum(expd, axis=1, keepdims=True)
        probs_low = (expd / total).astype(jnp.bfloat16)
        o_ref[:, cols] = jnp.dot(probs_low, v_ref[:, cols], preferred_element_type=jnp.float32)
        lse_ref[:, h:h + 1] = highest + jnp.log(total)


def attention_backward_kernel(
    q_ref, k_ref, v_ref, do_ref, lse_ref, rq_ref, sq_ref, pq_ref, sk_ref, pk_ref, rk_ref,
    dq_ref, dk_ref, dv_ref,
):
    queries = q_ref.shape[0]
    keys = k_ref.shape[0]
    allowed = allowed_mask(rq_ref, sq_ref, pq_ref, sk_ref, pk_ref, rk_ref)
    scale = HDIM ** (-0.5)
    for h in range(q_ref.shape[1] // HDIM):
        cols = slice(h * HDIM, (h + 1) * HDIM)
        q = q_ref[:, cols]
        k = k_ref[:, cols]
        v = v_ref[:, cols]
        do = do_ref[:, cols]
        raw = lax.dot_general(q, k, (((1,), (1,)), ((), ())), preferred_element_type=jnp.float32)
        scores = jnp.where(allowed, raw * scale, -1e30)
        probs = jnp.exp(scores - lse_ref[:, h:h + 1])
        grad_probs = lax.dot_general(do, v, (((1,), (1,)), ((), ())), preferred_element_type=jnp.float32)
        inner = jnp.sum(probs * grad_probs, axis=1, keepdims=True)
        grad_raw = (probs * (grad_probs - inner) * scale).astype(jnp.bfloat16)
        dq_ref[:, cols] = jnp.dot(grad_raw, k, preferred_element_type=jnp.float32)
        dk_ref[:, cols] = lax.dot_general(
            grad_raw, q, (((0,), (0,)), ((), ())), preferred_element_type=jnp.float32
        )
        dv_ref[:, cols] = lax.dot_general(
            probs.astype(jnp.bfloat16), do, (((0,), (0,)), ((), ())), preferred_element_type=jnp.float32
        )


def mask_specs(queries, keys):
    column = pl.BlockSpec((queries, 1), lambda i: (0, 0))
    row = pl.BlockSpec((1, keys), lambda i: (0, 0))
    return [column, column, column, row, row, row]


def attention_forward(q, kv, masks):
    queries, width = q.shape
    keys = kv.shape[0]
    block = 2 * HDIM
    pairs = width // block
    return pl.pallas_call(
        attention_forward_kernel,
        grid=(pairs,),
        in_specs=[
            pl.BlockSpec((queries, block), lambda i: (0, i)),
            pl.BlockSpec((keys, block), lambda i: (0, i)),
            pl.BlockSpec((keys, block), lambda i, p=pairs: (0, i + p)),
        ] + mask_specs(queries, keys),
        out_specs=[
            pl.BlockSpec((queries, block), lambda i: (0, i)),
            pl.BlockSpec((None, queries, 2), lambda i: (i, 0, 0)),
        ],
        out_shape=[
            jax.ShapeDtypeStruct((queries, width), jnp.float32),
            jax.ShapeDtypeStruct((pairs, queries, 2), jnp.float32),
        ],
        compiler_params=pltpu.CompilerParams(dimension_semantics=("arbitrary",)),
        cost_estimate=pl.CostEstimate(
            flops=4 * queries * keys * width, transcendentals=queries * keys * HEADS,
            bytes_accessed=2 * (queries + 2 * keys) * width + 4 * queries * width,
        ),
    )(q, kv, kv, *masks)


def attention_backward(q, kv, do, lse, masks):
    queries, width = q.shape
    keys = kv.shape[0]
    block = 2 * HDIM
    pairs = width // block
    return pl.pallas_call(
        attention_backward_kernel,
        grid=(pairs,),
        in_specs=[
            pl.BlockSpec((queries, block), lambda i: (0, i)),
            pl.BlockSpec((keys, block), lambda i: (0, i)),
            pl.BlockSpec((keys, block), lambda i, p=pairs: (0, i + p)),
            pl.BlockSpec((queries, block), lambda i: (0, i)),
            pl.BlockSpec((None, queries, 2), lambda i: (i, 0, 0)),
        ] + mask_specs(queries, keys),
        out_specs=[
            pl.BlockSpec((queries, block), lambda i: (0, i)),
            pl.BlockSpec((keys, block), lambda i: (0, i)),
            pl.BlockSpec((keys, block), lambda i: (0, i)),
        ],
        out_shape=[
            jax.ShapeDtypeStruct((queries, width), jnp.float32),
            jax.ShapeDtypeStruct((keys, width), jnp.float32),
            jax.ShapeDtypeStruct((keys, width), jnp.float32),
        ],
        compiler_params=pltpu.CompilerParams(dimension_semantics=("arbitrary",)),
        cost_estimate=pl.CostEstimate(
            flops=10 * queries * keys * width, transcendentals=queries * keys * HEADS,
            bytes_accessed=2 * (2 * queries + 2 * keys) * width + 4 * (queries + 2 * keys) * width,
        ),
    )(q, kv, kv, do, lse, *masks)


def shift(x, axis, n, step):
    return lax.ppermute(x, axis, [(i, (i + step) % n) for i in range(n)])


def place(buf, piece, index, dim):
    start = [0] * buf.ndim
    start[dim] = index * piece.shape[dim]
    return lax.dynamic_update_slice(buf, piece, start)


def ring_gather(piece, axis, n, dim, direct=False):
    if n == 1:
        return piece
    me = lax.axis_index(axis)
    shape = list(piece.shape)
    shape[dim] *= n
    buf = place(jnp.zeros(shape, piece.dtype), piece, me, dim)
    if n == 2 or direct:
        for k in range(1, n):
            buf = place(buf, shift(piece, axis, n, k), (me - k) % n, dim)
        return buf
    back = piece
    ahead = piece
    for step in range(1, n // 2 + 1):
        if step < n - step:
            back = shift(back, axis, n, 1)
            ahead = shift(ahead, axis, n, -1)
            buf = place(buf, back, (me - step) % n, dim)
            buf = place(buf, ahead, (me + step) % n, dim)
        else:
            half = piece.shape[dim] // 2
            first = shift(lax.slice_in_dim(back, 0, half, axis=dim), axis, n, 1)
            second = shift(lax.slice_in_dim(ahead, half, piece.shape[dim], axis=dim), axis, n, -1)
            buf = place(buf, jnp.concatenate([first, second], axis=dim), (me + step) % n, dim)
    return buf


def ring_reduce(x, axis, n, dim, hdim, direct=False):
    if n == 1:
        return x
    me = lax.axis_index(axis)
    size = x.shape[dim] // n

    def chunk(k):
        return lax.dynamic_slice_in_dim(x, (k % n) * size, size, axis=dim)

    def low(v):
        return v.astype(jnp.bfloat16)

    if n == 2 or direct:
        acc = chunk(me)
        for k in range(1, n):
            acc = acc + shift(low(chunk(me + k)), axis, n, k).astype(jnp.float32)
        return acc
    assert n == 4
    half = x.shape[hdim] // 2

    def part(k, which):
        c = chunk(k)
        return lax.slice_in_dim(c, 0, half, axis=hdim) if which == 0 else lax.slice_in_dim(
            c, half, c.shape[hdim], axis=hdim
        )

    from_ahead = shift(low(jnp.stack([part(me - 2, 0), part(me - 1, 1)])), axis, n, -1)
    from_back = shift(low(jnp.stack([part(me + 2, 1), part(me + 1, 0)])), axis, n, 1)
    relay_ahead = shift(low(from_ahead[0].astype(jnp.float32) + part(me - 1, 0)), axis, n, -1)
    relay_back = shift(low(from_back[0].astype(jnp.float32) + part(me + 1, 1)), axis, n, 1)
    first = part(me, 0) + from_back[1].astype(jnp.float32) + relay_ahead.astype(jnp.float32)
    second = part(me, 1) + from_ahead[1].astype(jnp.float32) + relay_back.astype(jnp.float32)
    return jnp.concatenate([first, second], axis=hdim)


def cross(x):
    return lax.ppermute(x, ("xl", "xh"), [(i, 3 - i) for i in range(4)])


def swap_core(x):
    return lax.ppermute(x, "c", [(0, 1), (1, 0)])


def absolute(parts, rows):
    g = lax.axis_index("xh") * 2 + lax.axis_index("c")
    buf = jnp.zeros((4 * rows,) + parts[0].shape[1:], parts[0].dtype)
    for j, part in enumerate(parts):
        buf = place(buf, part, jnp.bitwise_xor(g, j), 0)
    return buf


def gather_group(own, axis, n, direct):
    size = own.shape[0] // n
    me = lax.axis_index(axis)
    mine = lax.dynamic_slice_in_dim(own, me * size, size, axis=0)
    other = ring_gather(cross(mine), axis, n, 0, direct)
    partner = swap_core(jnp.concatenate([own, other]))
    rows = own.shape[0]
    return [own, partner[:rows], other, partner[rows:]]


def gather_weights(group, axis, sizes, direct):
    parts = gather_group(jnp.concatenate(group), axis, sizes[axis], direct)
    out = []
    start = 0
    for s in group:
        rows = s.shape[0]
        out.append(absolute([p[start:start + rows] for p in parts], rows))
        start += rows
    return out


def reduce_group(grads, sizes, direct):
    g = lax.axis_index("xh") * 2 + lax.axis_index("c")

    def shard(w, j):
        rows = w.shape[0] // 4
        return lax.dynamic_slice_in_dim(w, jnp.bitwise_xor(g, j) * rows, rows, axis=0)

    send = jnp.concatenate([shard(w, 1) for w in grads] + [shard(w, 3) for w in grads])
    got = swap_core(send.astype(jnp.bfloat16))
    total = got.shape[0] // 2
    kept = jnp.stack(
        [jnp.concatenate([shard(w, 0) for w in grads]), jnp.concatenate([shard(w, 2) for w in grads])]
    )
    pair = kept.astype(jnp.float32) + got.reshape(2, total, -1).astype(jnp.float32)
    ny, nz = sizes["y"], sizes["z"]
    rows = pair.shape[1]
    own = ring_reduce(pair[0], "y", ny, 0, 1, direct)
    own = ring_reduce(own, "z", nz, 0, 1, True)
    oth = ring_reduce(pair[1].reshape(ny, rows // ny, -1), "z", nz, 1, 2, direct)
    oth = ring_reduce(oth, "y", ny, 0, 2, True).reshape(own.shape)
    low_own = own.astype(jnp.bfloat16)
    low_oth = oth.astype(jnp.bfloat16)
    mine = (
        own
        + lax.ppermute(low_own, "xl", [(0, 1), (1, 0)]).astype(jnp.float32)
        + cross(low_oth).astype(jnp.float32)
        + lax.ppermute(low_oth, "xh", [(0, 1), (1, 0)]).astype(jnp.float32)
    )
    low_mine = mine.astype(jnp.bfloat16)
    half = low_mine.shape[1] // 2
    first = ring_gather(low_mine[:, :half], "z", nz, 0, True)
    first = ring_gather(first, "y", ny, 0, direct)
    second = ring_gather(low_mine[None, :, half:], "y", ny, 0, True)
    second = ring_gather(second, "z", nz, 1, direct).reshape(first.shape)
    full = jnp.concatenate([first, second], axis=1)
    out = []
    start = 0
    for w in grads:
        rows = w.shape[0] // 4
        out.append(full[start:start + rows].astype(jnp.float32))
        start += rows
    return out


def to_sequence(x):
    xh = lax.axis_index("xh")
    c = lax.axis_index("c")
    first = lax.ppermute(lax.dynamic_index_in_dim(x, c, 0, False), GRP, [(0, 0), (1, 2), (2, 1), (3, 3)])
    second = lax.ppermute(lax.dynamic_index_in_dim(x, 1 - c, 0, False), GRP, [(0, 2), (1, 0), (2, 3), (3, 1)])
    return jnp.where(xh == 0, jnp.concatenate([first, second]), jnp.concatenate([second, first]))


def from_sequence(x):
    xh = lax.axis_index("xh")
    c = lax.axis_index("c")
    length = x.shape[0] // 2
    first = jnp.where(xh == 0, x[:length], x[length:])
    second = jnp.where(xh == 0, x[length:], x[:length])
    first = lax.ppermute(first, GRP, [(0, 0), (1, 2), (2, 1), (3, 3)])
    second = lax.ppermute(second, GRP, [(2, 0), (0, 1), (3, 2), (1, 3)])
    return jnp.where(c == 0, jnp.stack([first, second]), jnp.stack([second, first]))


def body(
    tokens, segment, piece_start, w_query, w_key, w_value, w_out, w_gate, w_up, w_down, cotangent
):
    sizes = {"y": lax.axis_size("y"), "z": lax.axis_size("z"), "xl": lax.axis_size("xl")}
    width = tokens.shape[2]
    local_length = tokens.shape[1] * 2
    full_length = segment.shape[1]
    head_count = HEADS
    head_size = HDIM
    scale = head_size ** (-0.5)
    xh = lax.axis_index("xh")
    c = lax.axis_index("c")
    first_row = c * local_length
    rows = first_row + jnp.arange(local_length, dtype=jnp.int32)
    columns = jnp.arange(full_length, dtype=jnp.int32)
    inverse = 10000.0 ** (-jnp.arange(0, head_size, 2).astype(jnp.float32) / head_size)
    angles = rows.astype(jnp.float32)[:, None] * inverse[None, :]
    cosine = jnp.cos(angles)[:, None, :]
    sine = jnp.sin(angles)[:, None, :]

    query_weight, key_weight, value_weight = gather_weights(
        (w_query, w_key, w_value), "y", sizes, True
    )

    both_in = to_sequence(jnp.concatenate([tokens, cotangent], axis=2))
    hidden = both_in[:, :width].astype(jnp.float32)
    grad_result = both_in[:, width:]
    seg_row = lax.dynamic_index_in_dim(segment, xh, 0, False)
    start_row = lax.dynamic_index_in_dim(piece_start, xh, 0, False)

    normed, norm_one_back = jax.vjp(layer_norm, hidden)
    normed_low = normed.astype(jnp.bfloat16)
    query_heads = rotate(
        matmul(normed_low, query_weight).reshape(local_length, head_count, head_size),
        cosine,
        sine,
    ).astype(jnp.bfloat16)
    keys = (
        rotate(
            matmul(normed_low, key_weight).reshape(local_length, head_count, head_size),
            cosine,
            sine,
        )
        .reshape(local_length, width)
        .astype(jnp.bfloat16)
    )
    values = matmul(normed_low, value_weight).astype(jnp.bfloat16)
    w_out, w_down, w_gate, w_up, values = lax.optimization_barrier((w_out, w_down, w_gate, w_up, values))
    out_weight, down_weight = gather_weights((w_out, w_down), "z", sizes, False)
    gate_weight, up_weight = gather_weights((w_gate, w_up), "y", sizes, False)
    mine_kv = jnp.concatenate([keys, values], axis=1)
    both = jnp.concatenate([mine_kv, swap_core(mine_kv)])
    other_row = (1 - c) * local_length
    seg_local = lax.dynamic_slice_in_dim(seg_row, first_row, local_length)
    start_local = lax.dynamic_slice_in_dim(start_row, first_row, local_length)
    key_rows = jnp.concatenate([rows, other_row + jnp.arange(local_length, dtype=jnp.int32)])
    seg_keys = jnp.concatenate([seg_local, lax.dynamic_slice_in_dim(seg_row, other_row, local_length)])
    start_keys = jnp.concatenate(
        [start_local, lax.dynamic_slice_in_dim(start_row, other_row, local_length)]
    )
    masks = (
        rows[:, None],
        seg_local[:, None],
        start_local[:, None],
        seg_keys[None, :],
        start_keys[None, :],
        key_rows[None, :],
    )
    query_flat = query_heads.reshape(local_length, width)
    mixed, log_total = attention_forward(query_flat, both, masks)
    mixed_low = mixed.reshape(local_length, width).astype(jnp.bfloat16)
    after = hidden + matmul(mixed_low, out_weight)
    normed_two, norm_two_back = jax.vjp(layer_norm, after)
    normed_two_low = normed_two.astype(jnp.bfloat16)
    gate = matmul(normed_two_low, gate_weight)
    upper = matmul(normed_two_low, up_weight)
    active, gate_back = jax.vjp(gated, gate, upper)
    active_low = active.astype(jnp.bfloat16)
    result = after + matmul(active_low, down_weight)
    result_low = result.astype(jnp.bfloat16)

    grads = [None] * 7
    grads[6] = contract_rows(active_low, grad_result)
    grad_active = contract_cols(grad_result, down_weight)
    grad_gate, grad_upper = gate_back(grad_active)
    gate_low = grad_gate.astype(jnp.bfloat16)
    upper_low = grad_upper.astype(jnp.bfloat16)
    grads[4] = contract_rows(normed_two_low, gate_low)
    grads[5] = contract_rows(normed_two_low, upper_low)
    grad_normed_two = contract_cols(gate_low, gate_weight) + contract_cols(upper_low, up_weight)
    grad_after = grad_result.astype(jnp.float32) + norm_two_back(grad_normed_two)[0]
    after_low = grad_after.astype(jnp.bfloat16)
    grads[3] = contract_rows(mixed_low, after_low)
    grad_mixed = (
        contract_cols(after_low, out_weight)
        .astype(jnp.bfloat16)
        .reshape(local_length, head_count, head_size)
    )
    grad_query, grad_keys, grad_values = attention_backward(
        query_flat, both, grad_mixed.reshape(local_length, width), log_total, masks
    )
    grad_query = grad_query.reshape(local_length, head_count, head_size)
    grad_kv = jnp.concatenate([grad_keys, grad_values], axis=1)
    own_kv = grad_kv[:local_length] + swap_core(grad_kv[local_length:])
    own_keys = own_kv[:, :width]
    own_values = own_kv[:, width:]
    query_low = (
        rotate(grad_query, cosine, -sine).reshape(local_length, width).astype(jnp.bfloat16)
    )
    keys_low = (
        rotate(own_keys.reshape(local_length, head_count, head_size), cosine, -sine)
        .reshape(local_length, width)
        .astype(jnp.bfloat16)
    )
    values_low = own_values.astype(jnp.bfloat16)
    grads[0] = contract_rows(normed_low, query_low)
    grads[1] = contract_rows(normed_low, keys_low)
    grads[2] = contract_rows(normed_low, values_low)
    grad_normed = (
        contract_cols(query_low, query_weight)
        + contract_cols(keys_low, key_weight)
        + contract_cols(values_low, value_weight)
    )
    grad_hidden = grad_after + norm_one_back(grad_normed)[0]
    both_out = from_sequence(jnp.concatenate([result_low, grad_hidden.astype(jnp.bfloat16)], axis=1))
    output = both_out[..., :width]
    input_grads = both_out[..., width:]
    gate_rows = grads[4].shape[0]
    low = [w.astype(jnp.bfloat16) for w in grads]
    owned = reduce_group(
        [low[0], low[1], low[2], low[3], low[4].reshape(-1, width), low[5].reshape(-1, width), low[6]],
        sizes,
        False,
    )
    owned[4] = owned[4].reshape(gate_rows // 4, -1)
    owned[5] = owned[5].reshape(gate_rows // 4, -1)

    return (output, input_grads, *owned)


def solution(mesh):
    rep, grp = mesh.devices.shape
    side = int(round((rep // 2) ** 0.5))
    devices = mesh.devices.reshape(side, rep // (2 * side), 2, grp // 2, 2)
    fine = Mesh(devices, ("y", "z", "xl", "xh", "c"))
    seqs = P(REP, GRP, None)
    rows = P(GRP, None)
    placed = (seqs, P(REP, None), P(REP, None), rows, rows, rows, rows, rows, rows, rows, seqs)
    return jax.shard_map(
        body,
        mesh=fine,
        in_specs=placed,
        out_specs=(seqs, seqs, rows, rows, rows, rows, rows, rows, rows),
        check_vma=False,
    )
```

```python
import jax
import jax.numpy as jnp
from jax import lax
from jax.sharding import Mesh
from jax.sharding import PartitionSpec as P
from jax.experimental import pallas as pl
from jax.experimental.pallas import tpu as pltpu

HEADS = 12
HDIM = 64
REP = ("y", "z", "xl")
GRP = ("xh", "c")


def layer_norm(hidden):
    centred = hidden - jnp.mean(hidden, axis=-1, keepdims=True)
    spread = jnp.mean(centred * centred, axis=-1, keepdims=True)
    return centred * lax.rsqrt(spread + 1e-05)


def rotate(heads, cosine, sine):
    half = heads.shape[-1] // 2
    first = heads[..., :half]
    second = heads[..., half:]
    return jnp.concatenate(
        [first * cosine - second * sine, second * cosine + first * sine], axis=-1
    )


def gated(gate, upper):
    return gate / (1.0 + jnp.exp(-gate)) * upper


def matmul(left, right):
    return jnp.dot(left, right, preferred_element_type=jnp.float32)


def contract_rows(left, right):
    return lax.dot_general(
        left, right, (((0,), (0,)), ((), ())), preferred_element_type=jnp.float32
    )


def contract_cols(left, right):
    return lax.dot_general(
        left, right, (((1,), (1,)), ((), ())), preferred_element_type=jnp.float32
    )


def allowed_mask(rq_ref, sq_ref, pq_ref, sk_ref, pk_ref, rk_ref):
    return (sq_ref[...] == sk_ref[...]) & (
        (rk_ref[...] <= rq_ref[...]) | (pq_ref[...] == pk_ref[...])
    )


def attention_forward_kernel(
    q_ref, k_ref, v_ref, rq_ref, sq_ref, pq_ref, sk_ref, pk_ref, rk_ref, o_ref, lse_ref
):
    queries = q_ref.shape[0]
    keys = k_ref.shape[0]
    allowed = allowed_mask(rq_ref, sq_ref, pq_ref, sk_ref, pk_ref, rk_ref)
    scale = HDIM ** (-0.5)
    for h in range(q_ref.shape[1] // HDIM):
        cols = slice(h * HDIM, (h + 1) * HDIM)
        raw = lax.dot_general(
            q_ref[:, cols], k_ref[:, cols], (((1,), (1,)), ((), ())),
            preferred_element_type=jnp.float32,
        )
        scores = jnp.where(allowed, raw * scale, -1e30)
        highest = jnp.max(scores, axis=1, keepdims=True)
        expd = jnp.exp(scores - highest)
        total = jnp.sum(expd, axis=1, keepdims=True)
        probs_low = (expd / total).astype(jnp.bfloat16)
        o_ref[:, cols] = jnp.dot(probs_low, v_ref[:, cols], preferred_element_type=jnp.float32)
        lse_ref[:, h:h + 1] = highest + jnp.log(total)


def attention_backward_kernel(
    q_ref, k_ref, v_ref, do_ref, lse_ref, rq_ref, sq_ref, pq_ref, sk_ref, pk_ref, rk_ref,
    dq_ref, dk_ref, dv_ref,
):
    queries = q_ref.shape[0]
    keys = k_ref.shape[0]
    allowed = allowed_mask(rq_ref, sq_ref, pq_ref, sk_ref, pk_ref, rk_ref)
    scale = HDIM ** (-0.5)
    for h in range(q_ref.shape[1] // HDIM):
        cols = slice(h * HDIM, (h + 1) * HDIM)
        q = q_ref[:, cols]
        k = k_ref[:, cols]
        v = v_ref[:, cols]
        do = do_ref[:, cols]
        raw = lax.dot_general(q, k, (((1,), (1,)), ((), ())), preferred_element_type=jnp.float32)
        scores = jnp.where(allowed, raw * scale, -1e30)
        probs = jnp.exp(scores - lse_ref[:, h:h + 1])
        grad_probs = lax.dot_general(do, v, (((1,), (1,)), ((), ())), preferred_element_type=jnp.float32)
        inner = jnp.sum(probs * grad_probs, axis=1, keepdims=True)
        grad_raw = (probs * (grad_probs - inner) * scale).astype(jnp.bfloat16)
        dq_ref[:, cols] = jnp.dot(grad_raw, k, preferred_element_type=jnp.float32)
        dk_ref[:, cols] = lax.dot_general(
            grad_raw, q, (((0,), (0,)), ((), ())), preferred_element_type=jnp.float32
        )
        dv_ref[:, cols] = lax.dot_general(
            probs.astype(jnp.bfloat16), do, (((0,), (0,)), ((), ())), preferred_element_type=jnp.float32
        )


def mask_specs(queries, keys):
    column = pl.BlockSpec((queries, 1), lambda i: (0, 0))
    row = pl.BlockSpec((1, keys), lambda i: (0, 0))
    return [column, column, column, row, row, row]


def attention_forward(q, kv, masks):
    queries, width = q.shape
    keys = kv.shape[0]
    block = 2 * HDIM
    pairs = width // block
    return pl.pallas_call(
        attention_forward_kernel,
        grid=(pairs,),
        in_specs=[
            pl.BlockSpec((queries, block), lambda i: (0, i)),
            pl.BlockSpec((keys, block), lambda i: (0, i)),
            pl.BlockSpec((keys, block), lambda i, p=pairs: (0, i + p)),
        ] + mask_specs(queries, keys),
        out_specs=[
            pl.BlockSpec((queries, block), lambda i: (0, i)),
            pl.BlockSpec((None, queries, 2), lambda i: (i, 0, 0)),
        ],
        out_shape=[
            jax.ShapeDtypeStruct((queries, width), jnp.float32),
            jax.ShapeDtypeStruct((pairs, queries, 2), jnp.float32),
        ],
        compiler_params=pltpu.CompilerParams(dimension_semantics=("arbitrary",)),
        cost_estimate=pl.CostEstimate(
            flops=4 * queries * keys * width, transcendentals=queries * keys * HEADS,
            bytes_accessed=2 * (queries + 2 * keys) * width + 4 * queries * width,
        ),
    )(q, kv, kv, *masks)


def attention_backward(q, kv, do, lse, masks):
    queries, width = q.shape
    keys = kv.shape[0]
    block = 2 * HDIM
    pairs = width // block
    return pl.pallas_call(
        attention_backward_kernel,
        grid=(pairs,),
        in_specs=[
            pl.BlockSpec((queries, block), lambda i: (0, i)),
            pl.BlockSpec((keys, block), lambda i: (0, i)),
            pl.BlockSpec((keys, block), lambda i, p=pairs: (0, i + p)),
            pl.BlockSpec((queries, block), lambda i: (0, i)),
            pl.BlockSpec((None, queries, 2), lambda i: (i, 0, 0)),
        ] + mask_specs(queries, keys),
        out_specs=[
            pl.BlockSpec((queries, block), lambda i: (0, i)),
            pl.BlockSpec((keys, block), lambda i: (0, i)),
            pl.BlockSpec((keys, block), lambda i: (0, i)),
        ],
        out_shape=[
            jax.ShapeDtypeStruct((queries, width), jnp.float32),
            jax.ShapeDtypeStruct((keys, width), jnp.float32),
            jax.ShapeDtypeStruct((keys, width), jnp.float32),
        ],
        compiler_params=pltpu.CompilerParams(dimension_semantics=("arbitrary",)),
        cost_estimate=pl.CostEstimate(
            flops=10 * queries * keys * width, transcendentals=queries * keys * HEADS,
            bytes_accessed=2 * (2 * queries + 2 * keys) * width + 4 * (queries + 2 * keys) * width,
        ),
    )(q, kv, kv, do, lse, *masks)


def shift(x, axis, n, step):
    return lax.ppermute(x, axis, [(i, (i + step) % n) for i in range(n)])


def place(buf, piece, index, dim):
    start = [0] * buf.ndim
    start[dim] = index * piece.shape[dim]
    return lax.dynamic_update_slice(buf, piece, start)


def ring_gather(piece, axis, n, dim, direct=False):
    if n == 1:
        return piece
    me = lax.axis_index(axis)
    shape = list(piece.shape)
    shape[dim] *= n
    buf = place(jnp.zeros(shape, piece.dtype), piece, me, dim)
    if n == 2 or direct:
        for k in range(1, n):
            buf = place(buf, shift(piece, axis, n, k), (me - k) % n, dim)
        return buf
    back = piece
    ahead = piece
    for step in range(1, n // 2 + 1):
        if step < n - step:
            back = shift(back, axis, n, 1)
            ahead = shift(ahead, axis, n, -1)
            buf = place(buf, back, (me - step) % n, dim)
            buf = place(buf, ahead, (me + step) % n, dim)
        else:
            half = piece.shape[dim] // 2
            first = shift(lax.slice_in_dim(back, 0, half, axis=dim), axis, n, 1)
            second = shift(lax.slice_in_dim(ahead, half, piece.shape[dim], axis=dim), axis, n, -1)
            buf = place(buf, jnp.concatenate([first, second], axis=dim), (me + step) % n, dim)
    return buf


def ring_reduce(x, axis, n, dim, hdim, direct=False):
    if n == 1:
        return x
    me = lax.axis_index(axis)
    size = x.shape[dim] // n

    def chunk(k):
        return lax.dynamic_slice_in_dim(x, (k % n) * size, size, axis=dim)

    def low(v):
        return v.astype(jnp.bfloat16)

    if n == 2 or direct:
        acc = chunk(me)
        for k in range(1, n):
            acc = acc + shift(low(chunk(me + k)), axis, n, k).astype(jnp.float32)
        return acc
    assert n == 4
    half = x.shape[hdim] // 2

    def part(k, which):
        c = chunk(k)
        return lax.slice_in_dim(c, 0, half, axis=hdim) if which == 0 else lax.slice_in_dim(
            c, half, c.shape[hdim], axis=hdim
        )

    from_ahead = shift(low(jnp.stack([part(me - 2, 0), part(me - 1, 1)])), axis, n, -1)
    from_back = shift(low(jnp.stack([part(me + 2, 1), part(me + 1, 0)])), axis, n, 1)
    relay_ahead = shift(low(from_ahead[0].astype(jnp.float32) + part(me - 1, 0)), axis, n, -1)
    relay_back = shift(low(from_back[0].astype(jnp.float32) + part(me + 1, 1)), axis, n, 1)
    first = part(me, 0) + from_back[1].astype(jnp.float32) + relay_ahead.astype(jnp.float32)
    second = part(me, 1) + from_ahead[1].astype(jnp.float32) + relay_back.astype(jnp.float32)
    return jnp.concatenate([first, second], axis=hdim)


def cross(x):
    return lax.ppermute(x, ("xl", "xh"), [(i, 3 - i) for i in range(4)])


def swap_core(x):
    return lax.ppermute(x, "c", [(0, 1), (1, 0)])


def absolute(parts, rows):
    g = lax.axis_index("xh") * 2 + lax.axis_index("c")
    buf = jnp.zeros((4 * rows,) + parts[0].shape[1:], parts[0].dtype)
    for j, part in enumerate(parts):
        buf = place(buf, part, jnp.bitwise_xor(g, j), 0)
    return buf


def gather_group(own, axis, n, direct):
    size = own.shape[0] // n
    me = lax.axis_index(axis)
    mine = lax.dynamic_slice_in_dim(own, me * size, size, axis=0)
    other = ring_gather(cross(mine), axis, n, 0, direct)
    partner = swap_core(jnp.concatenate([own, other]))
    rows = own.shape[0]
    return [own, partner[:rows], other, partner[rows:]]


def gather_weights(group, axis, sizes, direct):
    parts = gather_group(jnp.concatenate(group), axis, sizes[axis], direct)
    out = []
    start = 0
    for s in group:
        rows = s.shape[0]
        out.append(absolute([p[start:start + rows] for p in parts], rows))
        start += rows
    return out


def reduce_group(grads, sizes, direct):
    g = lax.axis_index("xh") * 2 + lax.axis_index("c")

    def shard(w, j):
        rows = w.shape[-2] // 4
        part = lax.dynamic_slice_in_dim(w, jnp.bitwise_xor(g, j) * rows, rows, axis=w.ndim - 2)
        return part.reshape(-1, w.shape[-1])

    send = jnp.concatenate([shard(w, 1) for w in grads] + [shard(w, 3) for w in grads])
    got = swap_core(send.astype(jnp.bfloat16))
    total = got.shape[0] // 2
    kept = jnp.stack(
        [jnp.concatenate([shard(w, 0) for w in grads]), jnp.concatenate([shard(w, 2) for w in grads])]
    )
    pair = kept.astype(jnp.float32) + got.reshape(2, total, -1).astype(jnp.float32)
    ny, nz = sizes["y"], sizes["z"]
    rows = pair.shape[1]
    own = ring_reduce(pair[0], "y", ny, 0, 1, direct)
    own = ring_reduce(own, "z", nz, 0, 1, True)
    oth = ring_reduce(pair[1].reshape(ny, rows // ny, -1), "z", nz, 1, 2, direct)
    oth = ring_reduce(oth, "y", ny, 0, 2, True).reshape(own.shape)
    low_own = own.astype(jnp.bfloat16)
    low_oth = oth.astype(jnp.bfloat16)
    mine = (
        own
        + lax.ppermute(low_own, "xl", [(0, 1), (1, 0)]).astype(jnp.float32)
        + cross(low_oth).astype(jnp.float32)
        + lax.ppermute(low_oth, "xh", [(0, 1), (1, 0)]).astype(jnp.float32)
    )
    full = ring_gather(mine.astype(jnp.bfloat16), "z", sizes["z"], 0, True)
    full = ring_gather(full, "y", sizes["y"], 0, direct)
    out = []
    start = 0
    for w in grads:
        rows = w.size // (4 * w.shape[-1])
        out.append(full[start:start + rows].astype(jnp.float32))
        start += rows
    return out


def to_sequence(x):
    xh = lax.axis_index("xh")
    c = lax.axis_index("c")
    first = lax.ppermute(lax.dynamic_index_in_dim(x, c, 0, False), GRP, [(0, 0), (1, 2), (2, 1), (3, 3)])
    second = lax.ppermute(lax.dynamic_index_in_dim(x, 1 - c, 0, False), GRP, [(0, 2), (1, 0), (2, 3), (3, 1)])
    return jnp.where(xh == 0, jnp.concatenate([first, second]), jnp.concatenate([second, first]))


def from_sequence(x):
    xh = lax.axis_index("xh")
    c = lax.axis_index("c")
    length = x.shape[0] // 2
    first = jnp.where(xh == 0, x[:length], x[length:])
    second = jnp.where(xh == 0, x[length:], x[:length])
    first = lax.ppermute(first, GRP, [(0, 0), (1, 2), (2, 1), (3, 3)])
    second = lax.ppermute(second, GRP, [(2, 0), (0, 1), (3, 2), (1, 3)])
    return jnp.where(c == 0, jnp.stack([first, second]), jnp.stack([second, first]))


def body(
    tokens, segment, piece_start, w_query, w_key, w_value, w_out, w_gate, w_up, w_down, cotangent
):
    sizes = {"y": lax.axis_size("y"), "z": lax.axis_size("z"), "xl": lax.axis_size("xl")}
    width = tokens.shape[2]
    local_length = tokens.shape[1] * 2
    full_length = segment.shape[1]
    head_count = HEADS
    head_size = HDIM
    scale = head_size ** (-0.5)
    xh = lax.axis_index("xh")
    c = lax.axis_index("c")
    first_row = c * local_length
    rows = first_row + jnp.arange(local_length, dtype=jnp.int32)
    columns = jnp.arange(full_length, dtype=jnp.int32)
    inverse = 10000.0 ** (-jnp.arange(0, head_size, 2).astype(jnp.float32) / head_size)
    angles = rows.astype(jnp.float32)[:, None] * inverse[None, :]
    cosine = jnp.cos(angles)[:, None, :]
    sine = jnp.sin(angles)[:, None, :]

    query_weight, key_weight, value_weight = gather_weights(
        (w_query, w_key, w_value), "y", sizes, True
    )

    both_in = to_sequence(jnp.concatenate([tokens, cotangent], axis=2))
    hidden = both_in[:, :width].astype(jnp.float32)
    grad_result = both_in[:, width:]
    seg_row = lax.dynamic_index_in_dim(segment, xh, 0, False)
    start_row = lax.dynamic_index_in_dim(piece_start, xh, 0, False)

    normed, norm_one_back = jax.vjp(layer_norm, hidden)
    normed_low = normed.astype(jnp.bfloat16)
    query_heads = rotate(
        matmul(normed_low, query_weight).reshape(local_length, head_count, head_size),
        cosine,
        sine,
    ).astype(jnp.bfloat16)
    keys = (
        rotate(
            matmul(normed_low, key_weight).reshape(local_length, head_count, head_size),
            cosine,
            sine,
        )
        .reshape(local_length, width)
        .astype(jnp.bfloat16)
    )
    values = matmul(normed_low, value_weight).astype(jnp.bfloat16)
    w_out, w_down, w_gate, w_up, values = lax.optimization_barrier((w_out, w_down, w_gate, w_up, values))
    out_weight, down_weight = gather_weights((w_out, w_down), "z", sizes, False)
    gate_weight, up_weight = gather_weights((w_gate, w_up), "y", sizes, False)
    mine_kv = jnp.concatenate([keys, values], axis=1)
    both = jnp.concatenate([mine_kv, swap_core(mine_kv)])
    other_row = (1 - c) * local_length
    seg_local = lax.dynamic_slice_in_dim(seg_row, first_row, local_length)
    start_local = lax.dynamic_slice_in_dim(start_row, first_row, local_length)
    key_rows = jnp.concatenate([rows, other_row + jnp.arange(local_length, dtype=jnp.int32)])
    seg_keys = jnp.concatenate([seg_local, lax.dynamic_slice_in_dim(seg_row, other_row, local_length)])
    start_keys = jnp.concatenate(
        [start_local, lax.dynamic_slice_in_dim(start_row, other_row, local_length)]
    )
    masks = (
        rows[:, None],
        seg_local[:, None],
        start_local[:, None],
        seg_keys[None, :],
        start_keys[None, :],
        key_rows[None, :],
    )
    query_flat = query_heads.reshape(local_length, width)
    mixed, log_total = attention_forward(query_flat, both, masks)
    mixed_low = mixed.reshape(local_length, width).astype(jnp.bfloat16)
    after = hidden + matmul(mixed_low, out_weight)
    normed_two, norm_two_back = jax.vjp(layer_norm, after)
    normed_two_low = normed_two.astype(jnp.bfloat16)
    gate = matmul(normed_two_low, gate_weight)
    upper = matmul(normed_two_low, up_weight)
    active, gate_back = jax.vjp(gated, gate, upper)
    active_low = active.astype(jnp.bfloat16)
    result = after + matmul(active_low, down_weight)
    result_low = result.astype(jnp.bfloat16)

    grads = [None] * 7
    grads[6] = contract_rows(active_low, grad_result)
    grad_active = contract_cols(grad_result, down_weight)
    grad_gate, grad_upper = gate_back(grad_active)
    gate_low = grad_gate.astype(jnp.bfloat16)
    upper_low = grad_upper.astype(jnp.bfloat16)
    def blocked_grad(left, right):
        count = right.shape[1] // width
        return jnp.stack(
            [contract_rows(left, right[:, i * width:(i + 1) * width]) for i in range(count)]
        )

    grads[4] = blocked_grad(normed_two_low, gate_low)
    grads[5] = blocked_grad(normed_two_low, upper_low)
    grad_normed_two = contract_cols(gate_low, gate_weight) + contract_cols(upper_low, up_weight)
    grad_after = grad_result.astype(jnp.float32) + norm_two_back(grad_normed_two)[0]
    after_low = grad_after.astype(jnp.bfloat16)
    grads[3] = contract_rows(mixed_low, after_low)
    grad_mixed = (
        contract_cols(after_low, out_weight)
        .astype(jnp.bfloat16)
        .reshape(local_length, head_count, head_size)
    )
    grad_query, grad_keys, grad_values = attention_backward(
        query_flat, both, grad_mixed.reshape(local_length, width), log_total, masks
    )
    grad_query = grad_query.reshape(local_length, head_count, head_size)
    grad_kv = jnp.concatenate([grad_keys, grad_values], axis=1)
    own_kv = grad_kv[:local_length] + swap_core(grad_kv[local_length:])
    own_keys = own_kv[:, :width]
    own_values = own_kv[:, width:]
    query_low = (
        rotate(grad_query, cosine, -sine).reshape(local_length, width).astype(jnp.bfloat16)
    )
    keys_low = (
        rotate(own_keys.reshape(local_length, head_count, head_size), cosine, -sine)
        .reshape(local_length, width)
        .astype(jnp.bfloat16)
    )
    values_low = own_values.astype(jnp.bfloat16)
    grads[0] = contract_rows(normed_low, query_low)
    grads[1] = contract_rows(normed_low, keys_low)
    grads[2] = contract_rows(normed_low, values_low)
    grad_normed = (
        contract_cols(query_low, query_weight)
        + contract_cols(keys_low, key_weight)
        + contract_cols(values_low, value_weight)
    )
    grad_hidden = grad_after + norm_one_back(grad_normed)[0]
    both_out = from_sequence(jnp.concatenate([result_low, grad_hidden.astype(jnp.bfloat16)], axis=1))
    output = both_out[..., :width]
    input_grads = both_out[..., width:]
    blocks, gate_rows = grads[4].shape[0], grads[4].shape[1]
    low = [w.astype(jnp.bfloat16) for w in grads]
    owned = reduce_group(low, sizes, False)
    for i in (4, 5):
        owned[i] = owned[i].reshape(blocks, gate_rows // 4, width).transpose(1, 0, 2).reshape(
            gate_rows // 4, blocks * width
        )

    return (output, input_grads, *owned)


def solution(mesh):
    rep, grp = mesh.devices.shape
    side = int(round((rep // 2) ** 0.5))
    devices = mesh.devices.reshape(side, rep // (2 * side), 2, grp // 2, 2)
    fine = Mesh(devices, ("y", "z", "xl", "xh", "c"))
    seqs = P(REP, GRP, None)
    rows = P(GRP, None)
    placed = (seqs, P(REP, None), P(REP, None), rows, rows, rows, rows, rows, rows, rows, seqs)
    return jax.shard_map(
        body,
        mesh=fine,
        in_specs=placed,
        out_specs=(seqs, seqs, rows, rows, rows, rows, rows, rows, rows),
        check_vma=False,
    )
```

```python
import jax
import jax.numpy as jnp
from jax import lax
from jax.sharding import Mesh
from jax.sharding import PartitionSpec as P
from jax.experimental import pallas as pl
from jax.experimental.pallas import tpu as pltpu

HEADS = 12
HDIM = 64
REP = ("y", "z", "xl")
GRP = ("xh", "c")


def layer_norm(hidden):
    centred = hidden - jnp.mean(hidden, axis=-1, keepdims=True)
    spread = jnp.mean(centred * centred, axis=-1, keepdims=True)
    return centred * lax.rsqrt(spread + 1e-05)


def rotate(heads, cosine, sine):
    half = heads.shape[-1] // 2
    first = heads[..., :half]
    second = heads[..., half:]
    return jnp.concatenate(
        [first * cosine - second * sine, second * cosine + first * sine], axis=-1
    )


def gated(gate, upper):
    return gate / (1.0 + jnp.exp(-gate)) * upper


def matmul(left, right):
    return jnp.dot(left, right, preferred_element_type=jnp.float32)


def contract_rows(left, right):
    return lax.dot_general(
        left, right, (((0,), (0,)), ((), ())), preferred_element_type=jnp.float32
    )


def contract_cols(left, right):
    return lax.dot_general(
        left, right, (((1,), (1,)), ((), ())), preferred_element_type=jnp.float32
    )


def allowed_mask(rq_ref, sq_ref, pq_ref, sk_ref, pk_ref, rk_ref):
    return (sq_ref[...] == sk_ref[...]) & (
        (rk_ref[...] <= rq_ref[...]) | (pq_ref[...] == pk_ref[...])
    )


def attention_forward_kernel(
    q_ref, k_ref, v_ref, rq_ref, sq_ref, pq_ref, sk_ref, pk_ref, rk_ref, o_ref, lse_ref
):
    queries = q_ref.shape[0]
    keys = k_ref.shape[0]
    allowed = allowed_mask(rq_ref, sq_ref, pq_ref, sk_ref, pk_ref, rk_ref)
    scale = HDIM ** (-0.5)
    for h in range(q_ref.shape[1] // HDIM):
        cols = slice(h * HDIM, (h + 1) * HDIM)
        raw = lax.dot_general(
            q_ref[:, cols], k_ref[:, cols], (((1,), (1,)), ((), ())),
            preferred_element_type=jnp.float32,
        )
        scores = jnp.where(allowed, raw * scale, -1e30)
        highest = jnp.max(scores, axis=1, keepdims=True)
        expd = jnp.exp(scores - highest)
        total = jnp.sum(expd, axis=1, keepdims=True)
        probs_low = (expd / total).astype(jnp.bfloat16)
        o_ref[:, cols] = jnp.dot(probs_low, v_ref[:, cols], preferred_element_type=jnp.float32)
        lse_ref[:, h:h + 1] = highest + jnp.log(total)


def attention_backward_kernel(
    q_ref, k_ref, v_ref, do_ref, lse_ref, rq_ref, sq_ref, pq_ref, sk_ref, pk_ref, rk_ref,
    dq_ref, dk_ref, dv_ref,
):
    queries = q_ref.shape[0]
    keys = k_ref.shape[0]
    allowed = allowed_mask(rq_ref, sq_ref, pq_ref, sk_ref, pk_ref, rk_ref)
    scale = HDIM ** (-0.5)
    for h in range(q_ref.shape[1] // HDIM):
        cols = slice(h * HDIM, (h + 1) * HDIM)
        q = q_ref[:, cols]
        k = k_ref[:, cols]
        v = v_ref[:, cols]
        do = do_ref[:, cols]
        raw = lax.dot_general(q, k, (((1,), (1,)), ((), ())), preferred_element_type=jnp.float32)
        scores = jnp.where(allowed, raw * scale, -1e30)
        probs = jnp.exp(scores - lse_ref[:, h:h + 1])
        grad_probs = lax.dot_general(do, v, (((1,), (1,)), ((), ())), preferred_element_type=jnp.float32)
        inner = jnp.sum(probs * grad_probs, axis=1, keepdims=True)
        grad_raw = (probs * (grad_probs - inner) * scale).astype(jnp.bfloat16)
        dq_ref[:, cols] = jnp.dot(grad_raw, k, preferred_element_type=jnp.float32)
        dk_ref[:, cols] = lax.dot_general(
            grad_raw, q, (((0,), (0,)), ((), ())), preferred_element_type=jnp.float32
        )
        dv_ref[:, cols] = lax.dot_general(
            probs.astype(jnp.bfloat16), do, (((0,), (0,)), ((), ())), preferred_element_type=jnp.float32
        )


def mask_specs(queries, keys):
    column = pl.BlockSpec((queries, 1), lambda i: (0, 0))
    row = pl.BlockSpec((1, keys), lambda i: (0, 0))
    return [column, column, column, row, row, row]


def attention_forward(q, kv, masks):
    queries, width = q.shape
    keys = kv.shape[0]
    block = 2 * HDIM
    pairs = width // block
    return pl.pallas_call(
        attention_forward_kernel,
        grid=(pairs,),
        in_specs=[
            pl.BlockSpec((queries, block), lambda i: (0, i)),
            pl.BlockSpec((keys, block), lambda i: (0, i)),
            pl.BlockSpec((keys, block), lambda i, p=pairs: (0, i + p)),
        ] + mask_specs(queries, keys),
        out_specs=[
            pl.BlockSpec((queries, block), lambda i: (0, i)),
            pl.BlockSpec((None, queries, 2), lambda i: (i, 0, 0)),
        ],
        out_shape=[
            jax.ShapeDtypeStruct((queries, width), jnp.float32),
            jax.ShapeDtypeStruct((pairs, queries, 2), jnp.float32),
        ],
        compiler_params=pltpu.CompilerParams(dimension_semantics=("arbitrary",)),
        cost_estimate=pl.CostEstimate(
            flops=4 * queries * keys * width, transcendentals=queries * keys * HEADS,
            bytes_accessed=2 * (queries + 2 * keys) * width + 4 * queries * width,
        ),
    )(q, kv, kv, *masks)


def attention_backward(q, kv, do, lse, masks):
    queries, width = q.shape
    keys = kv.shape[0]
    block = 2 * HDIM
    pairs = width // block
    return pl.pallas_call(
        attention_backward_kernel,
        grid=(pairs,),
        in_specs=[
            pl.BlockSpec((queries, block), lambda i: (0, i)),
            pl.BlockSpec((keys, block), lambda i: (0, i)),
            pl.BlockSpec((keys, block), lambda i, p=pairs: (0, i + p)),
            pl.BlockSpec((queries, block), lambda i: (0, i)),
            pl.BlockSpec((None, queries, 2), lambda i: (i, 0, 0)),
        ] + mask_specs(queries, keys),
        out_specs=[
            pl.BlockSpec((queries, block), lambda i: (0, i)),
            pl.BlockSpec((keys, block), lambda i: (0, i)),
            pl.BlockSpec((keys, block), lambda i: (0, i)),
        ],
        out_shape=[
            jax.ShapeDtypeStruct((queries, width), jnp.float32),
            jax.ShapeDtypeStruct((keys, width), jnp.float32),
            jax.ShapeDtypeStruct((keys, width), jnp.float32),
        ],
        compiler_params=pltpu.CompilerParams(dimension_semantics=("arbitrary",)),
        cost_estimate=pl.CostEstimate(
            flops=10 * queries * keys * width, transcendentals=queries * keys * HEADS,
            bytes_accessed=2 * (2 * queries + 2 * keys) * width + 4 * (queries + 2 * keys) * width,
        ),
    )(q, kv, kv, do, lse, *masks)


def shift(x, axis, n, step):
    return lax.ppermute(x, axis, [(i, (i + step) % n) for i in range(n)])


def place(buf, piece, index, dim):
    start = [0] * buf.ndim
    start[dim] = index * piece.shape[dim]
    return lax.dynamic_update_slice(buf, piece, start)


def ring_gather(piece, axis, n, dim, direct=False):
    if n == 1:
        return piece
    me = lax.axis_index(axis)
    shape = list(piece.shape)
    shape[dim] *= n
    buf = place(jnp.zeros(shape, piece.dtype), piece, me, dim)
    if n == 2 or direct:
        for k in range(1, n):
            buf = place(buf, shift(piece, axis, n, k), (me - k) % n, dim)
        return buf
    back = piece
    ahead = piece
    for step in range(1, n // 2 + 1):
        if step < n - step:
            back = shift(back, axis, n, 1)
            ahead = shift(ahead, axis, n, -1)
            buf = place(buf, back, (me - step) % n, dim)
            buf = place(buf, ahead, (me + step) % n, dim)
        else:
            half = piece.shape[dim] // 2
            first = shift(lax.slice_in_dim(back, 0, half, axis=dim), axis, n, 1)
            second = shift(lax.slice_in_dim(ahead, half, piece.shape[dim], axis=dim), axis, n, -1)
            buf = place(buf, jnp.concatenate([first, second], axis=dim), (me + step) % n, dim)
    return buf


def ring_reduce(x, axis, n, dim, hdim, direct=False):
    if n == 1:
        return x
    me = lax.axis_index(axis)
    size = x.shape[dim] // n

    def chunk(k):
        return lax.dynamic_slice_in_dim(x, (k % n) * size, size, axis=dim)

    def low(v):
        return v.astype(jnp.bfloat16)

    if n == 2 or direct:
        acc = chunk(me)
        for k in range(1, n):
            acc = acc + shift(low(chunk(me + k)), axis, n, k).astype(jnp.float32)
        return acc
    assert n == 4
    half = x.shape[hdim] // 2

    def part(k, which):
        c = chunk(k)
        return lax.slice_in_dim(c, 0, half, axis=hdim) if which == 0 else lax.slice_in_dim(
            c, half, c.shape[hdim], axis=hdim
        )

    from_ahead = shift(low(jnp.stack([part(me - 2, 0), part(me - 1, 1)])), axis, n, -1)
    from_back = shift(low(jnp.stack([part(me + 2, 1), part(me + 1, 0)])), axis, n, 1)
    relay_ahead = shift(low(from_ahead[0].astype(jnp.float32) + part(me - 1, 0)), axis, n, -1)
    relay_back = shift(low(from_back[0].astype(jnp.float32) + part(me + 1, 1)), axis, n, 1)
    first = part(me, 0) + from_back[1].astype(jnp.float32) + relay_ahead.astype(jnp.float32)
    second = part(me, 1) + from_ahead[1].astype(jnp.float32) + relay_back.astype(jnp.float32)
    return jnp.concatenate([first, second], axis=hdim)


def cross(x):
    return lax.ppermute(x, ("xl", "xh"), [(i, 3 - i) for i in range(4)])


def swap_core(x):
    return lax.ppermute(x, "c", [(0, 1), (1, 0)])


def absolute(parts, rows):
    xh = lax.axis_index("xh")
    c = lax.axis_index("c")
    same = jnp.where(c == 0, jnp.concatenate(parts[0:2]), jnp.concatenate(parts[1::-1]))
    other = jnp.where(c == 0, jnp.concatenate(parts[2:4]), jnp.concatenate(parts[3:1:-1]))
    return jnp.where(xh == 0, jnp.concatenate([same, other]), jnp.concatenate([other, same]))


def gather_group(own, axis, n, direct):
    size = own.shape[0] // n
    me = lax.axis_index(axis)
    mine = lax.dynamic_slice_in_dim(own, me * size, size, axis=0)
    other = ring_gather(cross(mine), axis, n, 0, direct)
    partner = swap_core(jnp.concatenate([own, other]))
    rows = own.shape[0]
    return [own, partner[:rows], other, partner[rows:]]


def gather_weights(group, axis, sizes, direct):
    parts = gather_group(jnp.concatenate(group), axis, sizes[axis], direct)
    out = []
    start = 0
    for s in group:
        rows = s.shape[0]
        out.append(absolute([p[start:start + rows] for p in parts], rows))
        start += rows
    return out


def reduce_group(grads, sizes, direct):
    g = lax.axis_index("xh") * 2 + lax.axis_index("c")

    def shard(w, j):
        rows = w.shape[-2] // 4
        part = lax.dynamic_slice_in_dim(w, jnp.bitwise_xor(g, j) * rows, rows, axis=w.ndim - 2)
        return part.reshape(-1, w.shape[-1])

    send = jnp.concatenate([shard(w, 1) for w in grads] + [shard(w, 3) for w in grads])
    got = swap_core(send.astype(jnp.bfloat16))
    total = got.shape[0] // 2
    kept = jnp.stack(
        [jnp.concatenate([shard(w, 0) for w in grads]), jnp.concatenate([shard(w, 2) for w in grads])]
    )
    pair = kept.astype(jnp.float32) + got.reshape(2, total, -1).astype(jnp.float32)
    ny, nz = sizes["y"], sizes["z"]
    rows = pair.shape[1]
    own = ring_reduce(pair[0], "y", ny, 0, 1, direct)
    own = ring_reduce(own, "z", nz, 0, 1, True)
    oth = ring_reduce(pair[1].reshape(ny, rows // ny, -1), "z", nz, 1, 2, direct)
    oth = ring_reduce(oth, "y", ny, 0, 2, True).reshape(own.shape)
    low_own = own.astype(jnp.bfloat16)
    low_oth = oth.astype(jnp.bfloat16)
    mine = (
        own
        + lax.ppermute(low_own, "xl", [(0, 1), (1, 0)]).astype(jnp.float32)
        + cross(low_oth).astype(jnp.float32)
        + lax.ppermute(low_oth, "xh", [(0, 1), (1, 0)]).astype(jnp.float32)
    )
    full = ring_gather(mine.astype(jnp.bfloat16), "z", sizes["z"], 0, True)
    full = ring_gather(full, "y", sizes["y"], 0, direct)
    out = []
    start = 0
    for w in grads:
        rows = w.size // (4 * w.shape[-1])
        out.append(full[start:start + rows].astype(jnp.float32))
        start += rows
    return out


def to_sequence(x):
    xh = lax.axis_index("xh")
    c = lax.axis_index("c")
    first = lax.ppermute(lax.dynamic_index_in_dim(x, c, 0, False), GRP, [(0, 0), (1, 2), (2, 1), (3, 3)])
    second = lax.ppermute(lax.dynamic_index_in_dim(x, 1 - c, 0, False), GRP, [(0, 2), (1, 0), (2, 3), (3, 1)])
    return jnp.where(xh == 0, jnp.concatenate([first, second]), jnp.concatenate([second, first]))


def from_sequence(x):
    xh = lax.axis_index("xh")
    c = lax.axis_index("c")
    length = x.shape[0] // 2
    first = jnp.where(xh == 0, x[:length], x[length:])
    second = jnp.where(xh == 0, x[length:], x[:length])
    first = lax.ppermute(first, GRP, [(0, 0), (1, 2), (2, 1), (3, 3)])
    second = lax.ppermute(second, GRP, [(2, 0), (0, 1), (3, 2), (1, 3)])
    return jnp.where(c == 0, jnp.stack([first, second]), jnp.stack([second, first]))


def body(
    tokens, segment, piece_start, w_query, w_key, w_value, w_out, w_gate, w_up, w_down, cotangent
):
    sizes = {"y": lax.axis_size("y"), "z": lax.axis_size("z"), "xl": lax.axis_size("xl")}
    width = tokens.shape[2]
    local_length = tokens.shape[1] * 2
    full_length = segment.shape[1]
    head_count = HEADS
    head_size = HDIM
    scale = head_size ** (-0.5)
    xh = lax.axis_index("xh")
    c = lax.axis_index("c")
    first_row = c * local_length
    rows = first_row + jnp.arange(local_length, dtype=jnp.int32)
    columns = jnp.arange(full_length, dtype=jnp.int32)
    inverse = 10000.0 ** (-jnp.arange(0, head_size, 2).astype(jnp.float32) / head_size)
    angles = rows.astype(jnp.float32)[:, None] * inverse[None, :]
    cosine = jnp.cos(angles)[:, None, :]
    sine = jnp.sin(angles)[:, None, :]

    query_weight, key_weight, value_weight = gather_weights(
        (w_query, w_key, w_value), "y", sizes, True
    )

    both_in = to_sequence(jnp.concatenate([tokens, cotangent], axis=2))
    hidden = both_in[:, :width].astype(jnp.float32)
    grad_result = both_in[:, width:]
    seg_row = lax.dynamic_index_in_dim(segment, xh, 0, False)
    start_row = lax.dynamic_index_in_dim(piece_start, xh, 0, False)

    normed, norm_one_back = jax.vjp(layer_norm, hidden)
    normed_low = normed.astype(jnp.bfloat16)
    query_heads = rotate(
        matmul(normed_low, query_weight).reshape(local_length, head_count, head_size),
        cosine,
        sine,
    ).astype(jnp.bfloat16)
    keys = (
        rotate(
            matmul(normed_low, key_weight).reshape(local_length, head_count, head_size),
            cosine,
            sine,
        )
        .reshape(local_length, width)
        .astype(jnp.bfloat16)
    )
    values = matmul(normed_low, value_weight).astype(jnp.bfloat16)
    w_out, w_down, w_gate, w_up, values = lax.optimization_barrier((w_out, w_down, w_gate, w_up, values))
    out_weight, down_weight = gather_weights((w_out, w_down), "z", sizes, False)
    gate_weight, up_weight = gather_weights((w_gate, w_up), "y", sizes, False)
    mine_kv = jnp.concatenate([keys, values], axis=1)
    both = jnp.concatenate([mine_kv, swap_core(mine_kv)])
    other_row = (1 - c) * local_length
    seg_local = lax.dynamic_slice_in_dim(seg_row, first_row, local_length)
    start_local = lax.dynamic_slice_in_dim(start_row, first_row, local_length)
    key_rows = jnp.concatenate([rows, other_row + jnp.arange(local_length, dtype=jnp.int32)])
    seg_keys = jnp.concatenate([seg_local, lax.dynamic_slice_in_dim(seg_row, other_row, local_length)])
    start_keys = jnp.concatenate(
        [start_local, lax.dynamic_slice_in_dim(start_row, other_row, local_length)]
    )
    masks = (
        rows[:, None],
        seg_local[:, None],
        start_local[:, None],
        seg_keys[None, :],
        start_keys[None, :],
        key_rows[None, :],
    )
    query_flat = query_heads.reshape(local_length, width)
    mixed, log_total = attention_forward(query_flat, both, masks)
    mixed_low = mixed.reshape(local_length, width).astype(jnp.bfloat16)
    after = hidden + matmul(mixed_low, out_weight)
    normed_two, norm_two_back = jax.vjp(layer_norm, after)
    normed_two_low = normed_two.astype(jnp.bfloat16)
    gate = matmul(normed_two_low, gate_weight)
    upper = matmul(normed_two_low, up_weight)
    active, gate_back = jax.vjp(gated, gate, upper)
    active_low = active.astype(jnp.bfloat16)
    result = after + matmul(active_low, down_weight)
    result_low = result.astype(jnp.bfloat16)

    grads = [None] * 7
    grads[6] = contract_rows(active_low, grad_result)
    grad_active = contract_cols(grad_result, down_weight)
    grad_gate, grad_upper = gate_back(grad_active)
    gate_low = grad_gate.astype(jnp.bfloat16)
    upper_low = grad_upper.astype(jnp.bfloat16)
    def blocked_grad(left, right):
        count = right.shape[1] // width
        return jnp.stack(
            [contract_rows(left, right[:, i * width:(i + 1) * width]) for i in range(count)]
        )

    grads[4] = blocked_grad(normed_two_low, gate_low)
    grads[5] = blocked_grad(normed_two_low, upper_low)
    grad_normed_two = contract_cols(gate_low, gate_weight) + contract_cols(upper_low, up_weight)
    grad_after = grad_result.astype(jnp.float32) + norm_two_back(grad_normed_two)[0]
    after_low = grad_after.astype(jnp.bfloat16)
    grads[3] = contract_rows(mixed_low, after_low)
    grad_mixed = (
        contract_cols(after_low, out_weight)
        .astype(jnp.bfloat16)
        .reshape(local_length, head_count, head_size)
    )
    grad_query, grad_keys, grad_values = attention_backward(
        query_flat, both, grad_mixed.reshape(local_length, width), log_total, masks
    )
    grad_query = grad_query.reshape(local_length, head_count, head_size)
    grad_kv = jnp.concatenate([grad_keys, grad_values], axis=1)
    own_kv = grad_kv[:local_length] + swap_core(grad_kv[local_length:])
    own_keys = own_kv[:, :width]
    own_values = own_kv[:, width:]
    query_low = (
        rotate(grad_query, cosine, -sine).reshape(local_length, width).astype(jnp.bfloat16)
    )
    keys_low = (
        rotate(own_keys.reshape(local_length, head_count, head_size), cosine, -sine)
        .reshape(local_length, width)
        .astype(jnp.bfloat16)
    )
    values_low = own_values.astype(jnp.bfloat16)
    grads[0] = contract_rows(normed_low, query_low)
    grads[1] = contract_rows(normed_low, keys_low)
    grads[2] = contract_rows(normed_low, values_low)
    grad_normed = (
        contract_cols(query_low, query_weight)
        + contract_cols(keys_low, key_weight)
        + contract_cols(values_low, value_weight)
    )
    grad_hidden = grad_after + norm_one_back(grad_normed)[0]
    both_out = from_sequence(jnp.concatenate([result_low, grad_hidden.astype(jnp.bfloat16)], axis=1))
    output = both_out[..., :width]
    input_grads = both_out[..., width:]
    blocks, gate_rows = grads[4].shape[0], grads[4].shape[1]
    low = [w.astype(jnp.bfloat16) for w in grads]
    owned = reduce_group(low, sizes, False)
    for i in (4, 5):
        owned[i] = owned[i].reshape(blocks, gate_rows // 4, width).transpose(1, 0, 2).reshape(
            gate_rows // 4, blocks * width
        )

    return (output, input_grads, *owned)


def solution(mesh):
    rep, grp = mesh.devices.shape
    side = int(round((rep // 2) ** 0.5))
    devices = mesh.devices.reshape(side, rep // (2 * side), 2, grp // 2, 2)
    fine = Mesh(devices, ("y", "z", "xl", "xh", "c"))
    seqs = P(REP, GRP, None)
    rows = P(GRP, None)
    placed = (seqs, P(REP, None), P(REP, None), rows, rows, rows, rows, rows, rows, rows, seqs)
    return jax.shard_map(
        body,
        mesh=fine,
        in_specs=placed,
        out_specs=(seqs, seqs, rows, rows, rows, rows, rows, rows, rows),
        check_vma=False,
    )
```

```python
import jax
import jax.numpy as jnp
from jax import lax
from jax.sharding import Mesh
from jax.sharding import PartitionSpec as P
from jax.experimental import pallas as pl
from jax.experimental.pallas import tpu as pltpu

HEADS = 12
HDIM = 64
REP = ("y", "z", "xl")
GRP = ("xh", "c")


def layer_norm(hidden):
    centred = hidden - jnp.mean(hidden, axis=-1, keepdims=True)
    spread = jnp.mean(centred * centred, axis=-1, keepdims=True)
    return centred * lax.rsqrt(spread + 1e-05)


def rotate(heads, cosine, sine):
    half = heads.shape[-1] // 2
    first = heads[..., :half]
    second = heads[..., half:]
    return jnp.concatenate(
        [first * cosine - second * sine, second * cosine + first * sine], axis=-1
    )


def gated(gate, upper):
    return gate / (1.0 + jnp.exp(-gate)) * upper


def matmul(left, right):
    return jnp.dot(left, right, preferred_element_type=jnp.float32)


def contract_rows(left, right):
    return lax.dot_general(
        left, right, (((0,), (0,)), ((), ())), preferred_element_type=jnp.float32
    )


def contract_cols(left, right):
    return lax.dot_general(
        left, right, (((1,), (1,)), ((), ())), preferred_element_type=jnp.float32
    )


def allowed_mask(rq_ref, sq_ref, pq_ref, sk_ref, pk_ref, rk_ref):
    return (sq_ref[...] == sk_ref[...]) & (
        (rk_ref[...] <= rq_ref[...]) | (pq_ref[...] == pk_ref[...])
    )


def attention_forward_kernel(
    q_ref, k_ref, v_ref, rq_ref, sq_ref, pq_ref, sk_ref, pk_ref, rk_ref, o_ref, lse_ref
):
    queries = q_ref.shape[0]
    keys = k_ref.shape[0]
    allowed = allowed_mask(rq_ref, sq_ref, pq_ref, sk_ref, pk_ref, rk_ref)
    scale = HDIM ** (-0.5)
    for h in range(q_ref.shape[1] // HDIM):
        cols = slice(h * HDIM, (h + 1) * HDIM)
        raw = lax.dot_general(
            q_ref[:, cols], k_ref[:, cols], (((1,), (1,)), ((), ())),
            preferred_element_type=jnp.float32,
        )
        scores = jnp.where(allowed, raw * scale, -1e30)
        highest = jnp.max(scores, axis=1, keepdims=True)
        expd = jnp.exp(scores - highest)
        total = jnp.sum(expd, axis=1, keepdims=True)
        probs_low = (expd / total).astype(jnp.bfloat16)
        o_ref[:, cols] = jnp.dot(probs_low, v_ref[:, cols], preferred_element_type=jnp.float32)
        lse_ref[:, h:h + 1] = highest + jnp.log(total)


def attention_backward_kernel(
    q_ref, k_ref, v_ref, do_ref, lse_ref, rq_ref, sq_ref, pq_ref, sk_ref, pk_ref, rk_ref,
    dq_ref, dk_ref, dv_ref,
):
    queries = q_ref.shape[0]
    keys = k_ref.shape[0]
    allowed = allowed_mask(rq_ref, sq_ref, pq_ref, sk_ref, pk_ref, rk_ref)
    scale = HDIM ** (-0.5)
    for h in range(q_ref.shape[1] // HDIM):
        cols = slice(h * HDIM, (h + 1) * HDIM)
        q = q_ref[:, cols]
        k = k_ref[:, cols]
        v = v_ref[:, cols]
        do = do_ref[:, cols]
        raw = lax.dot_general(q, k, (((1,), (1,)), ((), ())), preferred_element_type=jnp.float32)
        scores = jnp.where(allowed, raw * scale, -1e30)
        probs = jnp.exp(scores - lse_ref[:, h:h + 1])
        grad_probs = lax.dot_general(do, v, (((1,), (1,)), ((), ())), preferred_element_type=jnp.float32)
        inner = jnp.sum(probs * grad_probs, axis=1, keepdims=True)
        grad_raw = (probs * (grad_probs - inner) * scale).astype(jnp.bfloat16)
        dq_ref[:, cols] = jnp.dot(grad_raw, k, preferred_element_type=jnp.float32)
        dk_ref[:, cols] = lax.dot_general(
            grad_raw, q, (((0,), (0,)), ((), ())), preferred_element_type=jnp.float32
        )
        dv_ref[:, cols] = lax.dot_general(
            probs.astype(jnp.bfloat16), do, (((0,), (0,)), ((), ())), preferred_element_type=jnp.float32
        )


def mask_specs(queries, keys):
    column = pl.BlockSpec((queries, 1), lambda i: (0, 0))
    row = pl.BlockSpec((1, keys), lambda i: (0, 0))
    return [column, column, column, row, row, row]


def attention_forward(q, kv, masks):
    queries, width = q.shape
    keys = kv.shape[0]
    block = 2 * HDIM
    pairs = width // block
    return pl.pallas_call(
        attention_forward_kernel,
        grid=(pairs,),
        in_specs=[
            pl.BlockSpec((queries, block), lambda i: (0, i)),
            pl.BlockSpec((keys, block), lambda i: (0, i)),
            pl.BlockSpec((keys, block), lambda i, p=pairs: (0, i + p)),
        ] + mask_specs(queries, keys),
        out_specs=[
            pl.BlockSpec((queries, block), lambda i: (0, i)),
            pl.BlockSpec((None, queries, 2), lambda i: (i, 0, 0)),
        ],
        out_shape=[
            jax.ShapeDtypeStruct((queries, width), jnp.float32),
            jax.ShapeDtypeStruct((pairs, queries, 2), jnp.float32),
        ],
        compiler_params=pltpu.CompilerParams(dimension_semantics=("arbitrary",)),
        cost_estimate=pl.CostEstimate(
            flops=4 * queries * keys * width, transcendentals=queries * keys * HEADS,
            bytes_accessed=2 * (queries + 2 * keys) * width + 4 * queries * width,
        ),
    )(q, kv, kv, *masks)


def attention_backward(q, kv, do, lse, masks):
    queries, width = q.shape
    keys = kv.shape[0]
    block = 2 * HDIM
    pairs = width // block
    return pl.pallas_call(
        attention_backward_kernel,
        grid=(pairs,),
        in_specs=[
            pl.BlockSpec((queries, block), lambda i: (0, i)),
            pl.BlockSpec((keys, block), lambda i: (0, i)),
            pl.BlockSpec((keys, block), lambda i, p=pairs: (0, i + p)),
            pl.BlockSpec((queries, block), lambda i: (0, i)),
            pl.BlockSpec((None, queries, 2), lambda i: (i, 0, 0)),
        ] + mask_specs(queries, keys),
        out_specs=[
            pl.BlockSpec((queries, block), lambda i: (0, i)),
            pl.BlockSpec((keys, block), lambda i: (0, i)),
            pl.BlockSpec((keys, block), lambda i: (0, i)),
        ],
        out_shape=[
            jax.ShapeDtypeStruct((queries, width), jnp.float32),
            jax.ShapeDtypeStruct((keys, width), jnp.float32),
            jax.ShapeDtypeStruct((keys, width), jnp.float32),
        ],
        compiler_params=pltpu.CompilerParams(dimension_semantics=("arbitrary",)),
        cost_estimate=pl.CostEstimate(
            flops=10 * queries * keys * width, transcendentals=queries * keys * HEADS,
            bytes_accessed=2 * (2 * queries + 2 * keys) * width + 4 * (queries + 2 * keys) * width,
        ),
    )(q, kv, kv, do, lse, *masks)


def shift(x, axis, n, step):
    return lax.ppermute(x, axis, [(i, (i + step) % n) for i in range(n)])


def place(buf, piece, index, dim):
    start = [0] * buf.ndim
    start[dim] = index * piece.shape[dim]
    return lax.dynamic_update_slice(buf, piece, start)


def ring_gather(piece, axis, n, dim, direct=False):
    if n == 1:
        return piece
    me = lax.axis_index(axis)
    shape = list(piece.shape)
    shape[dim] *= n
    buf = place(jnp.zeros(shape, piece.dtype), piece, me, dim)
    if n == 2 or direct:
        for k in range(1, n):
            buf = place(buf, shift(piece, axis, n, k), (me - k) % n, dim)
        return buf
    back = piece
    ahead = piece
    for step in range(1, n // 2 + 1):
        if step < n - step:
            back = shift(back, axis, n, 1)
            ahead = shift(ahead, axis, n, -1)
            buf = place(buf, back, (me - step) % n, dim)
            buf = place(buf, ahead, (me + step) % n, dim)
        else:
            half = piece.shape[dim] // 2
            first = shift(lax.slice_in_dim(back, 0, half, axis=dim), axis, n, 1)
            second = shift(lax.slice_in_dim(ahead, half, piece.shape[dim], axis=dim), axis, n, -1)
            buf = place(buf, jnp.concatenate([first, second], axis=dim), (me + step) % n, dim)
    return buf


def ring_reduce(x, axis, n, dim, hdim, direct=False):
    if n == 1:
        return x
    me = lax.axis_index(axis)
    size = x.shape[dim] // n

    def chunk(k):
        return lax.dynamic_slice_in_dim(x, (k % n) * size, size, axis=dim)

    def low(v):
        return v.astype(jnp.bfloat16)

    if n == 2 or direct:
        acc = chunk(me)
        for k in range(1, n):
            acc = acc + shift(low(chunk(me + k)), axis, n, k).astype(jnp.float32)
        return acc
    assert n == 4
    half = x.shape[hdim] // 2

    def part(k, which):
        c = chunk(k)
        return lax.slice_in_dim(c, 0, half, axis=hdim) if which == 0 else lax.slice_in_dim(
            c, half, c.shape[hdim], axis=hdim
        )

    from_ahead = shift(low(jnp.stack([part(me - 2, 0), part(me - 1, 1)])), axis, n, -1)
    from_back = shift(low(jnp.stack([part(me + 2, 1), part(me + 1, 0)])), axis, n, 1)
    relay_ahead = shift(low(from_ahead[0].astype(jnp.float32) + part(me - 1, 0)), axis, n, -1)
    relay_back = shift(low(from_back[0].astype(jnp.float32) + part(me + 1, 1)), axis, n, 1)
    first = part(me, 0) + from_back[1].astype(jnp.float32) + relay_ahead.astype(jnp.float32)
    second = part(me, 1) + from_ahead[1].astype(jnp.float32) + relay_back.astype(jnp.float32)
    return jnp.concatenate([first, second], axis=hdim)


def cross(x):
    return lax.ppermute(x, ("xl", "xh"), [(i, 3 - i) for i in range(4)])


def swap_core(x):
    return lax.ppermute(x, "c", [(0, 1), (1, 0)])


def absolute(parts, rows):
    xh = lax.axis_index("xh")
    c = lax.axis_index("c")
    same = jnp.where(c == 0, jnp.concatenate(parts[0:2]), jnp.concatenate(parts[1::-1]))
    other = jnp.where(c == 0, jnp.concatenate(parts[2:4]), jnp.concatenate(parts[3:1:-1]))
    return jnp.where(xh == 0, jnp.concatenate([same, other]), jnp.concatenate([other, same]))


def gather_group(own, axis, n, direct):
    size = own.shape[0] // n
    me = lax.axis_index(axis)
    mine = lax.dynamic_slice_in_dim(own, me * size, size, axis=0)
    other = ring_gather(cross(mine), axis, n, 0, direct)
    partner = swap_core(jnp.concatenate([own, other]))
    rows = own.shape[0]
    return [own, partner[:rows], other, partner[rows:]]


def gather_weights(group, axis, sizes, direct):
    parts = gather_group(jnp.concatenate(group), axis, sizes[axis], direct)
    out = []
    start = 0
    for s in group:
        rows = s.shape[0]
        out.append(absolute([p[start:start + rows] for p in parts], rows))
        start += rows
    return out


def reduce_group(grads, sizes, direct):
    g = lax.axis_index("xh") * 2 + lax.axis_index("c")

    def shard(w, j):
        rows = w.shape[-2] // 4
        part = lax.dynamic_slice_in_dim(w, jnp.bitwise_xor(g, j) * rows, rows, axis=w.ndim - 2)
        return part.reshape(-1, w.shape[-1])

    send = jnp.concatenate([shard(w, 1) for w in grads] + [shard(w, 3) for w in grads])
    got = swap_core(send.astype(jnp.bfloat16))
    total = got.shape[0] // 2
    kept = jnp.stack(
        [jnp.concatenate([shard(w, 0) for w in grads]), jnp.concatenate([shard(w, 2) for w in grads])]
    )
    pair = kept.astype(jnp.float32) + got.reshape(2, total, -1).astype(jnp.float32)
    ny, nz = sizes["y"], sizes["z"]
    rows = pair.shape[1]
    own = ring_reduce(pair[0], "y", ny, 0, 1, direct)
    own = ring_reduce(own, "z", nz, 0, 1, True)
    oth = ring_reduce(pair[1].reshape(ny, rows // ny, -1), "z", nz, 1, 2, direct)
    oth = ring_reduce(oth, "y", ny, 0, 2, True).reshape(own.shape)
    low_own = own.astype(jnp.bfloat16)
    low_oth = oth.astype(jnp.bfloat16)
    mine = (
        own
        + lax.ppermute(low_own, "xl", [(0, 1), (1, 0)]).astype(jnp.float32)
        + cross(low_oth).astype(jnp.float32)
        + lax.ppermute(low_oth, "xh", [(0, 1), (1, 0)]).astype(jnp.float32)
    )
    full = ring_gather(mine.astype(jnp.bfloat16), "z", sizes["z"], 0, True)
    full = ring_gather(full, "y", sizes["y"], 0, direct)
    out = []
    start = 0
    for w in grads:
        rows = w.size // (4 * w.shape[-1])
        out.append(full[start:start + rows].astype(jnp.float32))
        start += rows
    return out


def to_sequence(x):
    xh = lax.axis_index("xh")
    c = lax.axis_index("c")
    first = lax.ppermute(lax.dynamic_index_in_dim(x, c, 0, False), GRP, [(0, 0), (1, 2), (2, 1), (3, 3)])
    second = lax.ppermute(lax.dynamic_index_in_dim(x, 1 - c, 0, False), GRP, [(0, 2), (1, 0), (2, 3), (3, 1)])
    return jnp.where(xh == 0, jnp.concatenate([first, second]), jnp.concatenate([second, first]))


def from_sequence(x):
    xh = lax.axis_index("xh")
    c = lax.axis_index("c")
    length = x.shape[0] // 2
    first = jnp.where(xh == 0, x[:length], x[length:])
    second = jnp.where(xh == 0, x[length:], x[:length])
    first = lax.ppermute(first, GRP, [(0, 0), (1, 2), (2, 1), (3, 3)])
    second = lax.ppermute(second, GRP, [(2, 0), (0, 1), (3, 2), (1, 3)])
    return jnp.where(c == 0, jnp.stack([first, second]), jnp.stack([second, first]))


def body(
    tokens, segment, piece_start, w_query, w_key, w_value, w_out, w_gate, w_up, w_down, cotangent
):
    sizes = {"y": lax.axis_size("y"), "z": lax.axis_size("z"), "xl": lax.axis_size("xl")}
    width = tokens.shape[2]
    local_length = tokens.shape[1] * 2
    full_length = segment.shape[1]
    head_count = HEADS
    head_size = HDIM
    scale = head_size ** (-0.5)
    xh = lax.axis_index("xh")
    c = lax.axis_index("c")
    first_row = c * local_length
    rows = first_row + jnp.arange(local_length, dtype=jnp.int32)
    columns = jnp.arange(full_length, dtype=jnp.int32)
    inverse = 10000.0 ** (-jnp.arange(0, head_size, 2).astype(jnp.float32) / head_size)
    angles = rows.astype(jnp.float32)[:, None] * inverse[None, :]
    cosine = jnp.cos(angles)[:, None, :]
    sine = jnp.sin(angles)[:, None, :]

    query_weight, key_weight, value_weight = gather_weights(
        (w_query, w_key, w_value), "y", sizes, True
    )

    both_in = to_sequence(jnp.concatenate([tokens, cotangent], axis=2))
    hidden = both_in[:, :width].astype(jnp.float32)
    grad_result = both_in[:, width:]
    seg_row = lax.dynamic_index_in_dim(segment, xh, 0, False)
    start_row = lax.dynamic_index_in_dim(piece_start, xh, 0, False)

    normed, norm_one_back = jax.vjp(layer_norm, hidden)
    normed_low = normed.astype(jnp.bfloat16)
    query_heads = rotate(
        matmul(normed_low, query_weight).reshape(local_length, head_count, head_size),
        cosine,
        sine,
    ).astype(jnp.bfloat16)
    keys = (
        rotate(
            matmul(normed_low, key_weight).reshape(local_length, head_count, head_size),
            cosine,
            sine,
        )
        .reshape(local_length, width)
        .astype(jnp.bfloat16)
    )
    values = matmul(normed_low, value_weight).astype(jnp.bfloat16)
    out_weight, down_weight = gather_weights((w_out, w_down), "z", sizes, False)
    gate_weight, up_weight = gather_weights((w_gate, w_up), "y", sizes, False)
    mine_kv = jnp.concatenate([keys, values], axis=1)
    both = jnp.concatenate([mine_kv, swap_core(mine_kv)])
    other_row = (1 - c) * local_length
    seg_local = lax.dynamic_slice_in_dim(seg_row, first_row, local_length)
    start_local = lax.dynamic_slice_in_dim(start_row, first_row, local_length)
    key_rows = jnp.concatenate([rows, other_row + jnp.arange(local_length, dtype=jnp.int32)])
    seg_keys = jnp.concatenate([seg_local, lax.dynamic_slice_in_dim(seg_row, other_row, local_length)])
    start_keys = jnp.concatenate(
        [start_local, lax.dynamic_slice_in_dim(start_row, other_row, local_length)]
    )
    masks = (
        rows[:, None],
        seg_local[:, None],
        start_local[:, None],
        seg_keys[None, :],
        start_keys[None, :],
        key_rows[None, :],
    )
    query_flat = query_heads.reshape(local_length, width)
    mixed, log_total = attention_forward(query_flat, both, masks)
    mixed_low = mixed.reshape(local_length, width).astype(jnp.bfloat16)
    after = hidden + matmul(mixed_low, out_weight)
    normed_two, norm_two_back = jax.vjp(layer_norm, after)
    normed_two_low = normed_two.astype(jnp.bfloat16)
    gate = matmul(normed_two_low, gate_weight)
    upper = matmul(normed_two_low, up_weight)
    active, gate_back = jax.vjp(gated, gate, upper)
    active_low = active.astype(jnp.bfloat16)
    result = after + matmul(active_low, down_weight)
    result_low = result.astype(jnp.bfloat16)

    grads = [None] * 7
    grads[6] = contract_rows(active_low, grad_result)
    grad_active = contract_cols(grad_result, down_weight)
    grad_gate, grad_upper = gate_back(grad_active)
    gate_low = grad_gate.astype(jnp.bfloat16)
    upper_low = grad_upper.astype(jnp.bfloat16)
    def blocked_grad(left, right):
        count = right.shape[1] // width
        return jnp.stack(
            [contract_rows(left, right[:, i * width:(i + 1) * width]) for i in range(count)]
        )

    grads[4] = blocked_grad(normed_two_low, gate_low)
    grads[5] = blocked_grad(normed_two_low, upper_low)
    grad_normed_two = contract_cols(gate_low, gate_weight) + contract_cols(upper_low, up_weight)
    grad_after = grad_result.astype(jnp.float32) + norm_two_back(grad_normed_two)[0]
    after_low = grad_after.astype(jnp.bfloat16)
    grads[3] = contract_rows(mixed_low, after_low)
    grad_mixed = (
        contract_cols(after_low, out_weight)
        .astype(jnp.bfloat16)
        .reshape(local_length, head_count, head_size)
    )
    grad_query, grad_keys, grad_values = attention_backward(
        query_flat, both, grad_mixed.reshape(local_length, width), log_total, masks
    )
    grad_query = grad_query.reshape(local_length, head_count, head_size)
    grad_kv = jnp.concatenate([grad_keys, grad_values], axis=1)
    own_kv = grad_kv[:local_length] + swap_core(grad_kv[local_length:])
    own_keys = own_kv[:, :width]
    own_values = own_kv[:, width:]
    query_low = (
        rotate(grad_query, cosine, -sine).reshape(local_length, width).astype(jnp.bfloat16)
    )
    keys_low = (
        rotate(own_keys.reshape(local_length, head_count, head_size), cosine, -sine)
        .reshape(local_length, width)
        .astype(jnp.bfloat16)
    )
    values_low = own_values.astype(jnp.bfloat16)
    grads[0] = contract_rows(normed_low, query_low)
    grads[1] = contract_rows(normed_low, keys_low)
    grads[2] = contract_rows(normed_low, values_low)
    grad_normed = (
        contract_cols(query_low, query_weight)
        + contract_cols(keys_low, key_weight)
        + contract_cols(values_low, value_weight)
    )
    grad_hidden = grad_after + norm_one_back(grad_normed)[0]
    both_out = from_sequence(jnp.concatenate([result_low, grad_hidden.astype(jnp.bfloat16)], axis=1))
    output = both_out[..., :width]
    input_grads = both_out[..., width:]
    blocks, gate_rows = grads[4].shape[0], grads[4].shape[1]
    low = [w.astype(jnp.bfloat16) for w in grads]
    owned = reduce_group(low, sizes, False)
    for i in (4, 5):
        owned[i] = owned[i].reshape(blocks, gate_rows // 4, width).transpose(1, 0, 2).reshape(
            gate_rows // 4, blocks * width
        )

    return (output, input_grads, *owned)


def solution(mesh):
    rep, grp = mesh.devices.shape
    side = int(round((rep // 2) ** 0.5))
    devices = mesh.devices.reshape(side, rep // (2 * side), 2, grp // 2, 2)
    fine = Mesh(devices, ("y", "z", "xl", "xh", "c"))
    seqs = P(REP, GRP, None)
    rows = P(GRP, None)
    placed = (seqs, P(REP, None), P(REP, None), rows, rows, rows, rows, rows, rows, rows, seqs)
    return jax.shard_map(
        body,
        mesh=fine,
        in_specs=placed,
        out_specs=(seqs, seqs, rows, rows, rows, rows, rows, rows, rows),
        check_vma=False,
    )
```

```python
import jax
import jax.numpy as jnp
from jax import lax
from jax.sharding import Mesh
from jax.sharding import PartitionSpec as P
from jax.experimental import pallas as pl
from jax.experimental.pallas import tpu as pltpu

HEADS = 12
HDIM = 64
REP = ("y", "z", "xl")
GRP = ("xh", "c")


def layer_norm(hidden):
    centred = hidden - jnp.mean(hidden, axis=-1, keepdims=True)
    spread = jnp.mean(centred * centred, axis=-1, keepdims=True)
    return centred * lax.rsqrt(spread + 1e-05)


def rotate(heads, cosine, sine):
    half = heads.shape[-1] // 2
    first = heads[..., :half]
    second = heads[..., half:]
    return jnp.concatenate(
        [first * cosine - second * sine, second * cosine + first * sine], axis=-1
    )


def gated(gate, upper):
    return gate / (1.0 + jnp.exp(-gate)) * upper


def matmul(left, right):
    return jnp.dot(left, right, preferred_element_type=jnp.float32)


def contract_rows(left, right):
    return lax.dot_general(
        left, right, (((0,), (0,)), ((), ())), preferred_element_type=jnp.float32
    )


def contract_cols(left, right):
    return lax.dot_general(
        left, right, (((1,), (1,)), ((), ())), preferred_element_type=jnp.float32
    )


def allowed_mask(rq_ref, sq_ref, pq_ref, sk_ref, pk_ref, rk_ref):
    return (sq_ref[...] == sk_ref[...]) & (
        (rk_ref[...] <= rq_ref[...]) | (pq_ref[...] == pk_ref[...])
    )


def attention_forward_kernel(
    q_ref, k_ref, v_ref, rq_ref, sq_ref, pq_ref, sk_ref, pk_ref, rk_ref, o_ref, lse_ref
):
    queries = q_ref.shape[0]
    keys = k_ref.shape[0]
    allowed = allowed_mask(rq_ref, sq_ref, pq_ref, sk_ref, pk_ref, rk_ref)
    scale = HDIM ** (-0.5)
    for h in range(q_ref.shape[1] // HDIM):
        cols = slice(h * HDIM, (h + 1) * HDIM)
        raw = lax.dot_general(
            q_ref[:, cols], k_ref[:, cols], (((1,), (1,)), ((), ())),
            preferred_element_type=jnp.float32,
        )
        scores = jnp.where(allowed, raw * scale, -1e30)
        highest = jnp.max(scores, axis=1, keepdims=True)
        expd = jnp.exp(scores - highest)
        total = jnp.sum(expd, axis=1, keepdims=True)
        probs_low = (expd / total).astype(jnp.bfloat16)
        o_ref[:, cols] = jnp.dot(probs_low, v_ref[:, cols], preferred_element_type=jnp.float32)
        lse_ref[:, h:h + 1] = highest + jnp.log(total)


def attention_backward_kernel(
    q_ref, k_ref, v_ref, do_ref, lse_ref, rq_ref, sq_ref, pq_ref, sk_ref, pk_ref, rk_ref,
    dq_ref, dk_ref, dv_ref,
):
    queries = q_ref.shape[0]
    keys = k_ref.shape[0]
    allowed = allowed_mask(rq_ref, sq_ref, pq_ref, sk_ref, pk_ref, rk_ref)
    scale = HDIM ** (-0.5)
    for h in range(q_ref.shape[1] // HDIM):
        cols = slice(h * HDIM, (h + 1) * HDIM)
        q = q_ref[:, cols]
        k = k_ref[:, cols]
        v = v_ref[:, cols]
        do = do_ref[:, cols]
        raw = lax.dot_general(q, k, (((1,), (1,)), ((), ())), preferred_element_type=jnp.float32)
        scores = jnp.where(allowed, raw * scale, -1e30)
        probs = jnp.exp(scores - lse_ref[:, h:h + 1])
        grad_probs = lax.dot_general(do, v, (((1,), (1,)), ((), ())), preferred_element_type=jnp.float32)
        inner = jnp.sum(probs * grad_probs, axis=1, keepdims=True)
        grad_raw = (probs * (grad_probs - inner) * scale).astype(jnp.bfloat16)
        dq_ref[:, cols] = jnp.dot(grad_raw, k, preferred_element_type=jnp.float32)
        dk_ref[:, cols] = lax.dot_general(
            grad_raw, q, (((0,), (0,)), ((), ())), preferred_element_type=jnp.float32
        )
        dv_ref[:, cols] = lax.dot_general(
            probs.astype(jnp.bfloat16), do, (((0,), (0,)), ((), ())), preferred_element_type=jnp.float32
        )


def mask_specs(queries, keys):
    column = pl.BlockSpec((queries, 1), lambda i: (0, 0))
    row = pl.BlockSpec((1, keys), lambda i: (0, 0))
    return [column, column, column, row, row, row]


def attention_forward(q, kv, masks):
    queries, width = q.shape
    keys = kv.shape[0]
    block = 2 * HDIM
    pairs = width // block
    return pl.pallas_call(
        attention_forward_kernel,
        grid=(pairs,),
        in_specs=[
            pl.BlockSpec((queries, block), lambda i: (0, i)),
            pl.BlockSpec((keys, block), lambda i: (0, i)),
            pl.BlockSpec((keys, block), lambda i, p=pairs: (0, i + p)),
        ] + mask_specs(queries, keys),
        out_specs=[
            pl.BlockSpec((queries, block), lambda i: (0, i)),
            pl.BlockSpec((None, queries, 2), lambda i: (i, 0, 0)),
        ],
        out_shape=[
            jax.ShapeDtypeStruct((queries, width), jnp.float32),
            jax.ShapeDtypeStruct((pairs, queries, 2), jnp.float32),
        ],
        compiler_params=pltpu.CompilerParams(dimension_semantics=("arbitrary",)),
        cost_estimate=pl.CostEstimate(
            flops=4 * queries * keys * width, transcendentals=queries * keys * HEADS,
            bytes_accessed=2 * (queries + 2 * keys) * width + 4 * queries * width,
        ),
    )(q, kv, kv, *masks)


def attention_backward(q, kv, do, lse, masks):
    queries, width = q.shape
    keys = kv.shape[0]
    block = 2 * HDIM
    pairs = width // block
    return pl.pallas_call(
        attention_backward_kernel,
        grid=(pairs,),
        in_specs=[
            pl.BlockSpec((queries, block), lambda i: (0, i)),
            pl.BlockSpec((keys, block), lambda i: (0, i)),
            pl.BlockSpec((keys, block), lambda i, p=pairs: (0, i + p)),
            pl.BlockSpec((queries, block), lambda i: (0, i)),
            pl.BlockSpec((None, queries, 2), lambda i: (i, 0, 0)),
        ] + mask_specs(queries, keys),
        out_specs=[
            pl.BlockSpec((queries, block), lambda i: (0, i)),
            pl.BlockSpec((keys, block), lambda i: (0, i)),
            pl.BlockSpec((keys, block), lambda i: (0, i)),
        ],
        out_shape=[
            jax.ShapeDtypeStruct((queries, width), jnp.float32),
            jax.ShapeDtypeStruct((keys, width), jnp.float32),
            jax.ShapeDtypeStruct((keys, width), jnp.float32),
        ],
        compiler_params=pltpu.CompilerParams(dimension_semantics=("arbitrary",)),
        cost_estimate=pl.CostEstimate(
            flops=10 * queries * keys * width, transcendentals=queries * keys * HEADS,
            bytes_accessed=2 * (2 * queries + 2 * keys) * width + 4 * (queries + 2 * keys) * width,
        ),
    )(q, kv, kv, do, lse, *masks)


def shift(x, axis, n, step):
    return lax.ppermute(x, axis, [(i, (i + step) % n) for i in range(n)])


def place(buf, piece, index, dim):
    start = [0] * buf.ndim
    start[dim] = index * piece.shape[dim]
    return lax.dynamic_update_slice(buf, piece, start)


def ring_gather(piece, axis, n, dim, direct=False):
    if n == 1:
        return piece
    me = lax.axis_index(axis)
    shape = list(piece.shape)
    shape[dim] *= n
    buf = place(jnp.zeros(shape, piece.dtype), piece, me, dim)
    if n == 2 or direct:
        for k in range(1, n):
            buf = place(buf, shift(piece, axis, n, k), (me - k) % n, dim)
        return buf
    back = piece
    ahead = piece
    for step in range(1, n // 2 + 1):
        if step < n - step:
            back = shift(back, axis, n, 1)
            ahead = shift(ahead, axis, n, -1)
            buf = place(buf, back, (me - step) % n, dim)
            buf = place(buf, ahead, (me + step) % n, dim)
        else:
            half = piece.shape[dim] // 2
            first = shift(lax.slice_in_dim(back, 0, half, axis=dim), axis, n, 1)
            second = shift(lax.slice_in_dim(ahead, half, piece.shape[dim], axis=dim), axis, n, -1)
            buf = place(buf, jnp.concatenate([first, second], axis=dim), (me + step) % n, dim)
    return buf


def ring_reduce(x, axis, n, dim, hdim, direct=False):
    if n == 1:
        return x
    me = lax.axis_index(axis)
    size = x.shape[dim] // n

    def chunk(k):
        return lax.dynamic_slice_in_dim(x, (k % n) * size, size, axis=dim)

    def low(v):
        return v.astype(jnp.bfloat16)

    if n == 2 or direct:
        acc = chunk(me)
        for k in range(1, n):
            acc = acc + shift(low(chunk(me + k)), axis, n, k).astype(jnp.float32)
        return acc
    assert n == 4
    half = x.shape[hdim] // 2

    def part(k, which):
        c = chunk(k)
        return lax.slice_in_dim(c, 0, half, axis=hdim) if which == 0 else lax.slice_in_dim(
            c, half, c.shape[hdim], axis=hdim
        )

    from_ahead = shift(low(jnp.stack([part(me - 2, 0), part(me - 1, 1)])), axis, n, -1)
    from_back = shift(low(jnp.stack([part(me + 2, 1), part(me + 1, 0)])), axis, n, 1)
    relay_ahead = shift(low(from_ahead[0].astype(jnp.float32) + part(me - 1, 0)), axis, n, -1)
    relay_back = shift(low(from_back[0].astype(jnp.float32) + part(me + 1, 1)), axis, n, 1)
    first = part(me, 0) + from_back[1].astype(jnp.float32) + relay_ahead.astype(jnp.float32)
    second = part(me, 1) + from_ahead[1].astype(jnp.float32) + relay_back.astype(jnp.float32)
    return jnp.concatenate([first, second], axis=hdim)


def cross(x):
    return lax.ppermute(x, ("xl", "xh"), [(i, 3 - i) for i in range(4)])


def swap_core(x):
    return lax.ppermute(x, "c", [(0, 1), (1, 0)])


def absolute(parts, rows):
    xh = lax.axis_index("xh")
    c = lax.axis_index("c")
    same = jnp.where(c == 0, jnp.concatenate(parts[0:2]), jnp.concatenate(parts[1::-1]))
    other = jnp.where(c == 0, jnp.concatenate(parts[2:4]), jnp.concatenate(parts[3:1:-1]))
    return jnp.where(xh == 0, jnp.concatenate([same, other]), jnp.concatenate([other, same]))


def gather_group(own, axis, n, direct):
    size = own.shape[0] // n
    me = lax.axis_index(axis)
    mine = lax.dynamic_slice_in_dim(own, me * size, size, axis=0)
    other = ring_gather(cross(mine), axis, n, 0, direct)
    partner = swap_core(jnp.concatenate([own, other]))
    rows = own.shape[0]
    return [own, partner[:rows], other, partner[rows:]]


def gather_weights(group, axis, sizes, direct):
    parts = gather_group(jnp.concatenate(group), axis, sizes[axis], direct)
    out = []
    start = 0
    for s in group:
        rows = s.shape[0]
        out.append(absolute([p[start:start + rows] for p in parts], rows))
        start += rows
    return out


def reduce_group(grads, sizes, direct):
    g = lax.axis_index("xh") * 2 + lax.axis_index("c")

    def by_shard(w):
        if w.ndim == 2:
            return w.reshape(4, -1, w.shape[-1])
        blocks, rows, width = w.shape
        return w.reshape(blocks, 4, rows // 4, width).transpose(1, 0, 2, 3).reshape(4, -1, width)

    every = jnp.concatenate([by_shard(w) for w in grads], axis=1)

    def shard(j):
        return lax.dynamic_index_in_dim(every, jnp.bitwise_xor(g, j), 0, False)

    got = swap_core(jnp.stack([shard(1), shard(3)]))
    pair = jnp.stack([shard(0), shard(2)]).astype(jnp.float32) + got.astype(jnp.float32)
    ny, nz = sizes["y"], sizes["z"]
    rows = pair.shape[1]
    own = ring_reduce(pair[0], "y", ny, 0, 1, direct)
    own = ring_reduce(own, "z", nz, 0, 1, True)
    oth = ring_reduce(pair[1].reshape(ny, rows // ny, -1), "z", nz, 1, 2, direct)
    oth = ring_reduce(oth, "y", ny, 0, 2, True).reshape(own.shape)
    low_own = own.astype(jnp.bfloat16)
    low_oth = oth.astype(jnp.bfloat16)
    mine = (
        own
        + lax.ppermute(low_own, "xl", [(0, 1), (1, 0)]).astype(jnp.float32)
        + cross(low_oth).astype(jnp.float32)
        + lax.ppermute(low_oth, "xh", [(0, 1), (1, 0)]).astype(jnp.float32)
    )
    full = ring_gather(mine.astype(jnp.bfloat16), "z", sizes["z"], 0, True)
    full = ring_gather(full, "y", sizes["y"], 0, direct)
    out = []
    start = 0
    for w in grads:
        rows = w.size // (4 * w.shape[-1])
        out.append(full[start:start + rows].astype(jnp.float32))
        start += rows
    return out


def to_sequence(x):
    xh = lax.axis_index("xh")
    c = lax.axis_index("c")
    first = lax.ppermute(lax.dynamic_index_in_dim(x, c, 0, False), GRP, [(0, 0), (1, 2), (2, 1), (3, 3)])
    second = lax.ppermute(lax.dynamic_index_in_dim(x, 1 - c, 0, False), GRP, [(0, 2), (1, 0), (2, 3), (3, 1)])
    return jnp.where(xh == 0, jnp.concatenate([first, second]), jnp.concatenate([second, first]))


def from_sequence(x):
    xh = lax.axis_index("xh")
    c = lax.axis_index("c")
    length = x.shape[0] // 2
    first = jnp.where(xh == 0, x[:length], x[length:])
    second = jnp.where(xh == 0, x[length:], x[:length])
    first = lax.ppermute(first, GRP, [(0, 0), (1, 2), (2, 1), (3, 3)])
    second = lax.ppermute(second, GRP, [(2, 0), (0, 1), (3, 2), (1, 3)])
    return jnp.where(c == 0, jnp.stack([first, second]), jnp.stack([second, first]))


def body(
    tokens, segment, piece_start, w_query, w_key, w_value, w_out, w_gate, w_up, w_down, cotangent
):
    sizes = {"y": lax.axis_size("y"), "z": lax.axis_size("z"), "xl": lax.axis_size("xl")}
    width = tokens.shape[2]
    local_length = tokens.shape[1] * 2
    full_length = segment.shape[1]
    head_count = HEADS
    head_size = HDIM
    scale = head_size ** (-0.5)
    xh = lax.axis_index("xh")
    c = lax.axis_index("c")
    first_row = c * local_length
    rows = first_row + jnp.arange(local_length, dtype=jnp.int32)
    columns = jnp.arange(full_length, dtype=jnp.int32)
    inverse = 10000.0 ** (-jnp.arange(0, head_size, 2).astype(jnp.float32) / head_size)
    angles = rows.astype(jnp.float32)[:, None] * inverse[None, :]
    cosine = jnp.cos(angles)[:, None, :]
    sine = jnp.sin(angles)[:, None, :]

    query_weight, key_weight, value_weight = gather_weights(
        (w_query, w_key, w_value), "y", sizes, True
    )

    both_in = to_sequence(jnp.concatenate([tokens, cotangent], axis=2))
    hidden = both_in[:, :width].astype(jnp.float32)
    grad_result = both_in[:, width:]
    seg_row = lax.dynamic_index_in_dim(segment, xh, 0, False)
    start_row = lax.dynamic_index_in_dim(piece_start, xh, 0, False)

    normed, norm_one_back = jax.vjp(layer_norm, hidden)
    normed_low = normed.astype(jnp.bfloat16)
    query_heads = rotate(
        matmul(normed_low, query_weight).reshape(local_length, head_count, head_size),
        cosine,
        sine,
    ).astype(jnp.bfloat16)
    keys = (
        rotate(
            matmul(normed_low, key_weight).reshape(local_length, head_count, head_size),
            cosine,
            sine,
        )
        .reshape(local_length, width)
        .astype(jnp.bfloat16)
    )
    values = matmul(normed_low, value_weight).astype(jnp.bfloat16)
    out_weight, down_weight = gather_weights((w_out, w_down), "z", sizes, False)
    gate_weight, up_weight = gather_weights((w_gate, w_up), "y", sizes, False)
    mine_kv = jnp.concatenate([keys, values], axis=1)
    both = jnp.concatenate([mine_kv, swap_core(mine_kv)])
    other_row = (1 - c) * local_length
    seg_local = lax.dynamic_slice_in_dim(seg_row, first_row, local_length)
    start_local = lax.dynamic_slice_in_dim(start_row, first_row, local_length)
    key_rows = jnp.concatenate([rows, other_row + jnp.arange(local_length, dtype=jnp.int32)])
    seg_keys = jnp.concatenate([seg_local, lax.dynamic_slice_in_dim(seg_row, other_row, local_length)])
    start_keys = jnp.concatenate(
        [start_local, lax.dynamic_slice_in_dim(start_row, other_row, local_length)]
    )
    masks = (
        rows[:, None],
        seg_local[:, None],
        start_local[:, None],
        seg_keys[None, :],
        start_keys[None, :],
        key_rows[None, :],
    )
    query_flat = query_heads.reshape(local_length, width)
    mixed, log_total = attention_forward(query_flat, both, masks)
    mixed_low = mixed.reshape(local_length, width).astype(jnp.bfloat16)
    after = hidden + matmul(mixed_low, out_weight)
    normed_two, norm_two_back = jax.vjp(layer_norm, after)
    normed_two_low = normed_two.astype(jnp.bfloat16)
    gate = matmul(normed_two_low, gate_weight)
    upper = matmul(normed_two_low, up_weight)
    active, gate_back = jax.vjp(gated, gate, upper)
    active_low = active.astype(jnp.bfloat16)
    result = after + matmul(active_low, down_weight)
    result_low = result.astype(jnp.bfloat16)

    grads = [None] * 7
    grads[6] = contract_rows(active_low, grad_result)
    grad_active = contract_cols(grad_result, down_weight)
    grad_gate, grad_upper = gate_back(grad_active)
    gate_low = grad_gate.astype(jnp.bfloat16)
    upper_low = grad_upper.astype(jnp.bfloat16)
    def blocked_grad(left, right):
        count = right.shape[1] // width
        return jnp.stack(
            [contract_rows(left, right[:, i * width:(i + 1) * width]) for i in range(count)]
        )

    grads[4] = blocked_grad(normed_two_low, gate_low)
    grads[5] = blocked_grad(normed_two_low, upper_low)
    grad_normed_two = contract_cols(gate_low, gate_weight) + contract_cols(upper_low, up_weight)
    grad_after = grad_result.astype(jnp.float32) + norm_two_back(grad_normed_two)[0]
    after_low = grad_after.astype(jnp.bfloat16)
    grads[3] = contract_rows(mixed_low, after_low)
    grad_mixed = (
        contract_cols(after_low, out_weight)
        .astype(jnp.bfloat16)
        .reshape(local_length, head_count, head_size)
    )
    grad_query, grad_keys, grad_values = attention_backward(
        query_flat, both, grad_mixed.reshape(local_length, width), log_total, masks
    )
    grad_query = grad_query.reshape(local_length, head_count, head_size)
    grad_kv = jnp.concatenate([grad_keys, grad_values], axis=1)
    own_kv = grad_kv[:local_length] + swap_core(grad_kv[local_length:])
    own_keys = own_kv[:, :width]
    own_values = own_kv[:, width:]
    query_low = (
        rotate(grad_query, cosine, -sine).reshape(local_length, width).astype(jnp.bfloat16)
    )
    keys_low = (
        rotate(own_keys.reshape(local_length, head_count, head_size), cosine, -sine)
        .reshape(local_length, width)
        .astype(jnp.bfloat16)
    )
    values_low = own_values.astype(jnp.bfloat16)
    grads[0] = contract_rows(normed_low, query_low)
    grads[1] = contract_rows(normed_low, keys_low)
    grads[2] = contract_rows(normed_low, values_low)
    grad_normed = (
        contract_cols(query_low, query_weight)
        + contract_cols(keys_low, key_weight)
        + contract_cols(values_low, value_weight)
    )
    grad_hidden = grad_after + norm_one_back(grad_normed)[0]
    both_out = from_sequence(jnp.concatenate([result_low, grad_hidden.astype(jnp.bfloat16)], axis=1))
    output = both_out[..., :width]
    input_grads = both_out[..., width:]
    blocks, gate_rows = grads[4].shape[0], grads[4].shape[1]
    low = [w.astype(jnp.bfloat16) for w in grads]
    owned = reduce_group(low, sizes, False)
    for i in (4, 5):
        owned[i] = owned[i].reshape(blocks, gate_rows // 4, width).transpose(1, 0, 2).reshape(
            gate_rows // 4, blocks * width
        )

    return (output, input_grads, *owned)


def solution(mesh):
    rep, grp = mesh.devices.shape
    side = int(round((rep // 2) ** 0.5))
    devices = mesh.devices.reshape(side, rep // (2 * side), 2, grp // 2, 2)
    fine = Mesh(devices, ("y", "z", "xl", "xh", "c"))
    seqs = P(REP, GRP, None)
    rows = P(GRP, None)
    placed = (seqs, P(REP, None), P(REP, None), rows, rows, rows, rows, rows, rows, rows, seqs)
    return jax.shard_map(
        body,
        mesh=fine,
        in_specs=placed,
        out_specs=(seqs, seqs, rows, rows, rows, rows, rows, rows, rows),
        check_vma=False,
    )
```

```python
import jax
import jax.numpy as jnp
from jax import lax
from jax.sharding import Mesh
from jax.sharding import PartitionSpec as P
from jax.experimental import pallas as pl
from jax.experimental.pallas import tpu as pltpu

HEADS = 12
HDIM = 64
REP = ("y", "z", "xl")
GRP = ("xh", "c")


def layer_norm(hidden):
    centred = hidden - jnp.mean(hidden, axis=-1, keepdims=True)
    spread = jnp.mean(centred * centred, axis=-1, keepdims=True)
    return centred * lax.rsqrt(spread + 1e-05)


def rotate(heads, cosine, sine):
    half = heads.shape[-1] // 2
    first = heads[..., :half]
    second = heads[..., half:]
    return jnp.concatenate(
        [first * cosine - second * sine, second * cosine + first * sine], axis=-1
    )


def gated(gate, upper):
    return gate / (1.0 + jnp.exp(-gate)) * upper


def matmul(left, right):
    return jnp.dot(left, right, preferred_element_type=jnp.float32)


def contract_rows(left, right):
    return lax.dot_general(
        left, right, (((0,), (0,)), ((), ())), preferred_element_type=jnp.float32
    )


def contract_cols(left, right):
    return lax.dot_general(
        left, right, (((1,), (1,)), ((), ())), preferred_element_type=jnp.float32
    )


def allowed_mask(rq_ref, sq_ref, pq_ref, sk_ref, pk_ref, rk_ref):
    return (sq_ref[...] == sk_ref[...]) & (
        (rk_ref[...] <= rq_ref[...]) | (pq_ref[...] == pk_ref[...])
    )


def attention_forward_kernel(
    q_ref, k_ref, v_ref, rq_ref, sq_ref, pq_ref, sk_ref, pk_ref, rk_ref, o_ref, lse_ref
):
    queries = q_ref.shape[0]
    keys = k_ref.shape[0]
    allowed = allowed_mask(rq_ref, sq_ref, pq_ref, sk_ref, pk_ref, rk_ref)
    scale = HDIM ** (-0.5)
    for h in range(q_ref.shape[1] // HDIM):
        cols = slice(h * HDIM, (h + 1) * HDIM)
        raw = lax.dot_general(
            q_ref[:, cols], k_ref[:, cols], (((1,), (1,)), ((), ())),
            preferred_element_type=jnp.float32,
        )
        scores = jnp.where(allowed, raw * scale, -1e30)
        highest = jnp.max(scores, axis=1, keepdims=True)
        expd = jnp.exp(scores - highest)
        total = jnp.sum(expd, axis=1, keepdims=True)
        probs_low = (expd / total).astype(jnp.bfloat16)
        o_ref[:, cols] = jnp.dot(probs_low, v_ref[:, cols], preferred_element_type=jnp.float32)
        lse_ref[:, h:h + 1] = highest + jnp.log(total)


def attention_backward_kernel(
    q_ref, k_ref, v_ref, do_ref, lse_ref, rq_ref, sq_ref, pq_ref, sk_ref, pk_ref, rk_ref,
    dq_ref, dk_ref, dv_ref,
):
    queries = q_ref.shape[0]
    keys = k_ref.shape[0]
    allowed = allowed_mask(rq_ref, sq_ref, pq_ref, sk_ref, pk_ref, rk_ref)
    scale = HDIM ** (-0.5)
    for h in range(q_ref.shape[1] // HDIM):
        cols = slice(h * HDIM, (h + 1) * HDIM)
        q = q_ref[:, cols]
        k = k_ref[:, cols]
        v = v_ref[:, cols]
        do = do_ref[:, cols]
        raw = lax.dot_general(q, k, (((1,), (1,)), ((), ())), preferred_element_type=jnp.float32)
        scores = jnp.where(allowed, raw * scale, -1e30)
        probs = jnp.exp(scores - lse_ref[:, h:h + 1])
        grad_probs = lax.dot_general(do, v, (((1,), (1,)), ((), ())), preferred_element_type=jnp.float32)
        inner = jnp.sum(probs * grad_probs, axis=1, keepdims=True)
        grad_raw = (probs * (grad_probs - inner) * scale).astype(jnp.bfloat16)
        dq_ref[:, cols] = jnp.dot(grad_raw, k, preferred_element_type=jnp.float32)
        dk_ref[:, cols] = lax.dot_general(
            grad_raw, q, (((0,), (0,)), ((), ())), preferred_element_type=jnp.float32
        )
        dv_ref[:, cols] = lax.dot_general(
            probs.astype(jnp.bfloat16), do, (((0,), (0,)), ((), ())), preferred_element_type=jnp.float32
        )


def mask_specs(queries, keys):
    column = pl.BlockSpec((queries, 1), lambda i: (0, 0))
    row = pl.BlockSpec((1, keys), lambda i: (0, 0))
    return [column, column, column, row, row, row]


def attention_forward(q, kv, masks):
    queries, width = q.shape
    keys = kv.shape[0]
    block = 2 * HDIM
    pairs = width // block
    return pl.pallas_call(
        attention_forward_kernel,
        grid=(pairs,),
        in_specs=[
            pl.BlockSpec((queries, block), lambda i: (0, i)),
            pl.BlockSpec((keys, block), lambda i: (0, i)),
            pl.BlockSpec((keys, block), lambda i, p=pairs: (0, i + p)),
        ] + mask_specs(queries, keys),
        out_specs=[
            pl.BlockSpec((queries, block), lambda i: (0, i)),
            pl.BlockSpec((None, queries, 2), lambda i: (i, 0, 0)),
        ],
        out_shape=[
            jax.ShapeDtypeStruct((queries, width), jnp.float32),
            jax.ShapeDtypeStruct((pairs, queries, 2), jnp.float32),
        ],
        compiler_params=pltpu.CompilerParams(dimension_semantics=("arbitrary",)),
        cost_estimate=pl.CostEstimate(
            flops=4 * queries * keys * width, transcendentals=queries * keys * HEADS,
            bytes_accessed=2 * (queries + 2 * keys) * width + 4 * queries * width,
        ),
    )(q, kv, kv, *masks)


def attention_backward(q, kv, do, lse, masks):
    queries, width = q.shape
    keys = kv.shape[0]
    block = 2 * HDIM
    pairs = width // block
    return pl.pallas_call(
        attention_backward_kernel,
        grid=(pairs,),
        in_specs=[
            pl.BlockSpec((queries, block), lambda i: (0, i)),
            pl.BlockSpec((keys, block), lambda i: (0, i)),
            pl.BlockSpec((keys, block), lambda i, p=pairs: (0, i + p)),
            pl.BlockSpec((queries, block), lambda i: (0, i)),
            pl.BlockSpec((None, queries, 2), lambda i: (i, 0, 0)),
        ] + mask_specs(queries, keys),
        out_specs=[
            pl.BlockSpec((queries, block), lambda i: (0, i)),
            pl.BlockSpec((keys, block), lambda i: (0, i)),
            pl.BlockSpec((keys, block), lambda i: (0, i)),
        ],
        out_shape=[
            jax.ShapeDtypeStruct((queries, width), jnp.float32),
            jax.ShapeDtypeStruct((keys, width), jnp.float32),
            jax.ShapeDtypeStruct((keys, width), jnp.float32),
        ],
        compiler_params=pltpu.CompilerParams(dimension_semantics=("arbitrary",)),
        cost_estimate=pl.CostEstimate(
            flops=10 * queries * keys * width, transcendentals=queries * keys * HEADS,
            bytes_accessed=2 * (2 * queries + 2 * keys) * width + 4 * (queries + 2 * keys) * width,
        ),
    )(q, kv, kv, do, lse, *masks)


def shift(x, axis, n, step):
    return lax.ppermute(x, axis, [(i, (i + step) % n) for i in range(n)])


def place(buf, piece, index, dim):
    start = [0] * buf.ndim
    start[dim] = index * piece.shape[dim]
    return lax.dynamic_update_slice(buf, piece, start)


def ring_gather(piece, axis, n, dim, direct=False):
    if n == 1:
        return piece
    me = lax.axis_index(axis)
    by_offset = [piece] + [None] * (n - 1)
    if n == 2 or direct:
        for k in range(1, n):
            by_offset[(-k) % n] = shift(piece, axis, n, k)
    else:
        back = piece
        ahead = piece
        for step in range(1, n // 2 + 1):
            if step < n - step:
                back = shift(back, axis, n, 1)
                ahead = shift(ahead, axis, n, -1)
                by_offset[(-step) % n] = back
                by_offset[step % n] = ahead
            else:
                half = piece.shape[dim] // 2
                first = shift(lax.slice_in_dim(back, 0, half, axis=dim), axis, n, 1)
                second = shift(lax.slice_in_dim(ahead, half, piece.shape[dim], axis=dim), axis, n, -1)
                by_offset[step % n] = jnp.concatenate([first, second], axis=dim)
    doubled = jnp.concatenate(by_offset + by_offset, axis=dim)
    size = piece.shape[dim]
    return lax.dynamic_slice_in_dim(doubled, ((n - me) % n) * size, n * size, axis=dim)


def ring_reduce(x, axis, n, dim, hdim, direct=False):
    if n == 1:
        return x
    me = lax.axis_index(axis)
    size = x.shape[dim] // n

    def chunk(k):
        return lax.dynamic_slice_in_dim(x, (k % n) * size, size, axis=dim)

    def low(v):
        return v.astype(jnp.bfloat16)

    if n == 2 or direct:
        acc = chunk(me)
        for k in range(1, n):
            acc = acc + shift(low(chunk(me + k)), axis, n, k).astype(jnp.float32)
        return acc
    assert n == 4
    half = x.shape[hdim] // 2

    def part(k, which):
        c = chunk(k)
        return lax.slice_in_dim(c, 0, half, axis=hdim) if which == 0 else lax.slice_in_dim(
            c, half, c.shape[hdim], axis=hdim
        )

    from_ahead = shift(low(jnp.stack([part(me - 2, 0), part(me - 1, 1)])), axis, n, -1)
    from_back = shift(low(jnp.stack([part(me + 2, 1), part(me + 1, 0)])), axis, n, 1)
    relay_ahead = shift(low(from_ahead[0].astype(jnp.float32) + part(me - 1, 0)), axis, n, -1)
    relay_back = shift(low(from_back[0].astype(jnp.float32) + part(me + 1, 1)), axis, n, 1)
    first = part(me, 0) + from_back[1].astype(jnp.float32) + relay_ahead.astype(jnp.float32)
    second = part(me, 1) + from_ahead[1].astype(jnp.float32) + relay_back.astype(jnp.float32)
    return jnp.concatenate([first, second], axis=hdim)


def cross(x):
    return lax.ppermute(x, ("xl", "xh"), [(i, 3 - i) for i in range(4)])


def swap_core(x):
    return lax.ppermute(x, "c", [(0, 1), (1, 0)])


def absolute(parts, rows):
    xh = lax.axis_index("xh")
    c = lax.axis_index("c")
    same = jnp.where(c == 0, jnp.concatenate(parts[0:2]), jnp.concatenate(parts[1::-1]))
    other = jnp.where(c == 0, jnp.concatenate(parts[2:4]), jnp.concatenate(parts[3:1:-1]))
    return jnp.where(xh == 0, jnp.concatenate([same, other]), jnp.concatenate([other, same]))


def gather_group(own, axis, n, direct):
    size = own.shape[0] // n
    me = lax.axis_index(axis)
    mine = lax.dynamic_slice_in_dim(own, me * size, size, axis=0)
    other = ring_gather(cross(mine), axis, n, 0, direct)
    partner = swap_core(jnp.concatenate([own, other]))
    rows = own.shape[0]
    return [own, partner[:rows], other, partner[rows:]]


def gather_weights(group, axis, sizes, direct):
    parts = gather_group(jnp.concatenate(group), axis, sizes[axis], direct)
    out = []
    start = 0
    for s in group:
        rows = s.shape[0]
        out.append(absolute([p[start:start + rows] for p in parts], rows))
        start += rows
    return out


def reduce_group(grads, sizes, direct):
    g = lax.axis_index("xh") * 2 + lax.axis_index("c")

    def by_shard(w):
        if w.ndim == 2:
            return w.reshape(4, -1, w.shape[-1])
        blocks, rows, width = w.shape
        return w.reshape(blocks, 4, rows // 4, width).transpose(1, 0, 2, 3).reshape(4, -1, width)

    every = jnp.concatenate([by_shard(w) for w in grads], axis=1)

    def shard(j):
        return lax.dynamic_index_in_dim(every, jnp.bitwise_xor(g, j), 0, False)

    got = swap_core(jnp.stack([shard(1), shard(3)]))
    pair = jnp.stack([shard(0), shard(2)]).astype(jnp.float32) + got.astype(jnp.float32)
    ny, nz = sizes["y"], sizes["z"]
    rows = pair.shape[1]
    own = ring_reduce(pair[0], "y", ny, 0, 1, direct)
    own = ring_reduce(own, "z", nz, 0, 1, True)
    oth = ring_reduce(pair[1].reshape(ny, rows // ny, -1), "z", nz, 1, 2, direct)
    oth = ring_reduce(oth, "y", ny, 0, 2, True).reshape(own.shape)
    low_own = own.astype(jnp.bfloat16)
    low_oth = oth.astype(jnp.bfloat16)
    mine = (
        own
        + lax.ppermute(low_own, "xl", [(0, 1), (1, 0)]).astype(jnp.float32)
        + cross(low_oth).astype(jnp.float32)
        + lax.ppermute(low_oth, "xh", [(0, 1), (1, 0)]).astype(jnp.float32)
    )
    full = ring_gather(mine.astype(jnp.bfloat16), "z", sizes["z"], 0, True)
    full = ring_gather(full, "y", sizes["y"], 0, direct)
    out = []
    start = 0
    for w in grads:
        rows = w.size // (4 * w.shape[-1])
        out.append(full[start:start + rows].astype(jnp.float32))
        start += rows
    return out


def to_sequence(x):
    xh = lax.axis_index("xh")
    c = lax.axis_index("c")
    first = lax.ppermute(lax.dynamic_index_in_dim(x, c, 0, False), GRP, [(0, 0), (1, 2), (2, 1), (3, 3)])
    second = lax.ppermute(lax.dynamic_index_in_dim(x, 1 - c, 0, False), GRP, [(0, 2), (1, 0), (2, 3), (3, 1)])
    return jnp.where(xh == 0, jnp.concatenate([first, second]), jnp.concatenate([second, first]))


def from_sequence(x):
    xh = lax.axis_index("xh")
    c = lax.axis_index("c")
    length = x.shape[0] // 2
    first = jnp.where(xh == 0, x[:length], x[length:])
    second = jnp.where(xh == 0, x[length:], x[:length])
    first = lax.ppermute(first, GRP, [(0, 0), (1, 2), (2, 1), (3, 3)])
    second = lax.ppermute(second, GRP, [(2, 0), (0, 1), (3, 2), (1, 3)])
    return jnp.where(c == 0, jnp.stack([first, second]), jnp.stack([second, first]))


def body(
    tokens, segment, piece_start, w_query, w_key, w_value, w_out, w_gate, w_up, w_down, cotangent
):
    sizes = {"y": lax.axis_size("y"), "z": lax.axis_size("z"), "xl": lax.axis_size("xl")}
    width = tokens.shape[2]
    local_length = tokens.shape[1] * 2
    full_length = segment.shape[1]
    head_count = HEADS
    head_size = HDIM
    scale = head_size ** (-0.5)
    xh = lax.axis_index("xh")
    c = lax.axis_index("c")
    first_row = c * local_length
    rows = first_row + jnp.arange(local_length, dtype=jnp.int32)
    columns = jnp.arange(full_length, dtype=jnp.int32)
    inverse = 10000.0 ** (-jnp.arange(0, head_size, 2).astype(jnp.float32) / head_size)
    angles = rows.astype(jnp.float32)[:, None] * inverse[None, :]
    cosine = jnp.cos(angles)[:, None, :]
    sine = jnp.sin(angles)[:, None, :]

    query_weight, key_weight, value_weight = gather_weights(
        (w_query, w_key, w_value), "y", sizes, True
    )

    both_in = to_sequence(jnp.concatenate([tokens, cotangent], axis=2))
    hidden = both_in[:, :width].astype(jnp.float32)
    grad_result = both_in[:, width:]
    seg_row = lax.dynamic_index_in_dim(segment, xh, 0, False)
    start_row = lax.dynamic_index_in_dim(piece_start, xh, 0, False)

    normed, norm_one_back = jax.vjp(layer_norm, hidden)
    normed_low = normed.astype(jnp.bfloat16)
    query_heads = rotate(
        matmul(normed_low, query_weight).reshape(local_length, head_count, head_size),
        cosine,
        sine,
    ).astype(jnp.bfloat16)
    keys = (
        rotate(
            matmul(normed_low, key_weight).reshape(local_length, head_count, head_size),
            cosine,
            sine,
        )
        .reshape(local_length, width)
        .astype(jnp.bfloat16)
    )
    values = matmul(normed_low, value_weight).astype(jnp.bfloat16)
    out_weight, down_weight = gather_weights((w_out, w_down), "z", sizes, False)
    gate_weight, up_weight = gather_weights((w_gate, w_up), "y", sizes, False)
    mine_kv = jnp.concatenate([keys, values], axis=1)
    both = jnp.concatenate([mine_kv, swap_core(mine_kv)])
    other_row = (1 - c) * local_length
    seg_local = lax.dynamic_slice_in_dim(seg_row, first_row, local_length)
    start_local = lax.dynamic_slice_in_dim(start_row, first_row, local_length)
    key_rows = jnp.concatenate([rows, other_row + jnp.arange(local_length, dtype=jnp.int32)])
    seg_keys = jnp.concatenate([seg_local, lax.dynamic_slice_in_dim(seg_row, other_row, local_length)])
    start_keys = jnp.concatenate(
        [start_local, lax.dynamic_slice_in_dim(start_row, other_row, local_length)]
    )
    masks = (
        rows[:, None],
        seg_local[:, None],
        start_local[:, None],
        seg_keys[None, :],
        start_keys[None, :],
        key_rows[None, :],
    )
    query_flat = query_heads.reshape(local_length, width)
    mixed, log_total = attention_forward(query_flat, both, masks)
    mixed_low = mixed.reshape(local_length, width).astype(jnp.bfloat16)
    after = hidden + matmul(mixed_low, out_weight)
    normed_two, norm_two_back = jax.vjp(layer_norm, after)
    normed_two_low = normed_two.astype(jnp.bfloat16)
    gate = matmul(normed_two_low, gate_weight)
    upper = matmul(normed_two_low, up_weight)
    active, gate_back = jax.vjp(gated, gate, upper)
    active_low = active.astype(jnp.bfloat16)
    result = after + matmul(active_low, down_weight)
    result_low = result.astype(jnp.bfloat16)

    grads = [None] * 7
    grads[6] = contract_rows(active_low, grad_result)
    grad_active = contract_cols(grad_result, down_weight)
    grad_gate, grad_upper = gate_back(grad_active)
    gate_low = grad_gate.astype(jnp.bfloat16)
    upper_low = grad_upper.astype(jnp.bfloat16)
    def blocked_grad(left, right):
        count = right.shape[1] // width
        return jnp.stack(
            [contract_rows(left, right[:, i * width:(i + 1) * width]) for i in range(count)]
        )

    grads[4] = blocked_grad(normed_two_low, gate_low)
    grads[5] = blocked_grad(normed_two_low, upper_low)
    grad_normed_two = contract_cols(gate_low, gate_weight) + contract_cols(upper_low, up_weight)
    grad_after = grad_result.astype(jnp.float32) + norm_two_back(grad_normed_two)[0]
    after_low = grad_after.astype(jnp.bfloat16)
    grads[3] = contract_rows(mixed_low, after_low)
    grad_mixed = (
        contract_cols(after_low, out_weight)
        .astype(jnp.bfloat16)
        .reshape(local_length, head_count, head_size)
    )
    grad_query, grad_keys, grad_values = attention_backward(
        query_flat, both, grad_mixed.reshape(local_length, width), log_total, masks
    )
    grad_query = grad_query.reshape(local_length, head_count, head_size)
    grad_kv = jnp.concatenate([grad_keys, grad_values], axis=1)
    own_kv = grad_kv[:local_length] + swap_core(grad_kv[local_length:])
    own_keys = own_kv[:, :width]
    own_values = own_kv[:, width:]
    query_low = (
        rotate(grad_query, cosine, -sine).reshape(local_length, width).astype(jnp.bfloat16)
    )
    keys_low = (
        rotate(own_keys.reshape(local_length, head_count, head_size), cosine, -sine)
        .reshape(local_length, width)
        .astype(jnp.bfloat16)
    )
    values_low = own_values.astype(jnp.bfloat16)
    grads[0] = contract_rows(normed_low, query_low)
    grads[1] = contract_rows(normed_low, keys_low)
    grads[2] = contract_rows(normed_low, values_low)
    grad_normed = (
        contract_cols(query_low, query_weight)
        + contract_cols(keys_low, key_weight)
        + contract_cols(values_low, value_weight)
    )
    grad_hidden = grad_after + norm_one_back(grad_normed)[0]
    both_out = from_sequence(jnp.concatenate([result_low, grad_hidden.astype(jnp.bfloat16)], axis=1))
    output = both_out[..., :width]
    input_grads = both_out[..., width:]
    blocks, gate_rows = grads[4].shape[0], grads[4].shape[1]
    low = [w.astype(jnp.bfloat16) for w in grads]
    owned = reduce_group(low, sizes, False)
    for i in (4, 5):
        owned[i] = owned[i].reshape(blocks, gate_rows // 4, width).transpose(1, 0, 2).reshape(
            gate_rows // 4, blocks * width
        )

    return (output, input_grads, *owned)


def solution(mesh):
    rep, grp = mesh.devices.shape
    side = int(round((rep // 2) ** 0.5))
    devices = mesh.devices.reshape(side, rep // (2 * side), 2, grp // 2, 2)
    fine = Mesh(devices, ("y", "z", "xl", "xh", "c"))
    seqs = P(REP, GRP, None)
    rows = P(GRP, None)
    placed = (seqs, P(REP, None), P(REP, None), rows, rows, rows, rows, rows, rows, rows, seqs)
    return jax.shard_map(
        body,
        mesh=fine,
        in_specs=placed,
        out_specs=(seqs, seqs, rows, rows, rows, rows, rows, rows, rows),
        check_vma=False,
    )
```

```python
import jax
import jax.numpy as jnp
from jax import lax
from jax.sharding import Mesh
from jax.sharding import PartitionSpec as P
from jax.experimental import pallas as pl
from jax.experimental.pallas import tpu as pltpu

HEADS = 12
HDIM = 64
REP = ("y", "z", "xl")
GRP = ("xh", "c")


def layer_norm(hidden):
    centred = hidden - jnp.mean(hidden, axis=-1, keepdims=True)
    spread = jnp.mean(centred * centred, axis=-1, keepdims=True)
    return centred * lax.rsqrt(spread + 1e-05)


def rotate(heads, cosine, sine):
    half = heads.shape[-1] // 2
    first = heads[..., :half]
    second = heads[..., half:]
    return jnp.concatenate(
        [first * cosine - second * sine, second * cosine + first * sine], axis=-1
    )


def gated(gate, upper):
    return gate / (1.0 + jnp.exp(-gate)) * upper


def matmul(left, right):
    return jnp.dot(left, right, preferred_element_type=jnp.float32)


def contract_rows(left, right):
    return lax.dot_general(
        left, right, (((0,), (0,)), ((), ())), preferred_element_type=jnp.float32
    )


def contract_cols(left, right):
    return lax.dot_general(
        left, right, (((1,), (1,)), ((), ())), preferred_element_type=jnp.float32
    )


def allowed_mask(rq_ref, sq_ref, pq_ref, sk_ref, pk_ref, rk_ref):
    return (sq_ref[...] == sk_ref[...]) & (
        (rk_ref[...] <= rq_ref[...]) | (pq_ref[...] == pk_ref[...])
    )


def attention_forward_kernel(
    q_ref, k_ref, v_ref, rq_ref, sq_ref, pq_ref, sk_ref, pk_ref, rk_ref, o_ref, lse_ref
):
    queries = q_ref.shape[0]
    keys = k_ref.shape[0]
    allowed = allowed_mask(rq_ref, sq_ref, pq_ref, sk_ref, pk_ref, rk_ref)
    scale = HDIM ** (-0.5)
    for h in range(q_ref.shape[1] // HDIM):
        cols = slice(h * HDIM, (h + 1) * HDIM)
        raw = lax.dot_general(
            q_ref[:, cols], k_ref[:, cols], (((1,), (1,)), ((), ())),
            preferred_element_type=jnp.float32,
        )
        scores = jnp.where(allowed, raw * scale, -1e30)
        highest = jnp.max(scores, axis=1, keepdims=True)
        expd = jnp.exp(scores - highest)
        total = jnp.sum(expd, axis=1, keepdims=True)
        probs_low = (expd * (1.0 / total)).astype(jnp.bfloat16)
        o_ref[:, cols] = jnp.dot(probs_low, v_ref[:, cols], preferred_element_type=jnp.float32)
        lse_ref[:, h:h + 1] = highest + jnp.log(total)


def attention_backward_kernel(
    q_ref, k_ref, v_ref, do_ref, lse_ref, rq_ref, sq_ref, pq_ref, sk_ref, pk_ref, rk_ref,
    dq_ref, dk_ref, dv_ref,
):
    queries = q_ref.shape[0]
    keys = k_ref.shape[0]
    allowed = allowed_mask(rq_ref, sq_ref, pq_ref, sk_ref, pk_ref, rk_ref)
    scale = HDIM ** (-0.5)
    for h in range(q_ref.shape[1] // HDIM):
        cols = slice(h * HDIM, (h + 1) * HDIM)
        q = q_ref[:, cols]
        k = k_ref[:, cols]
        v = v_ref[:, cols]
        do = do_ref[:, cols]
        raw = lax.dot_general(q, k, (((1,), (1,)), ((), ())), preferred_element_type=jnp.float32)
        scores = jnp.where(allowed, raw * scale, -1e30)
        probs = jnp.exp(scores - lse_ref[:, h:h + 1])
        grad_probs = lax.dot_general(do, v, (((1,), (1,)), ((), ())), preferred_element_type=jnp.float32)
        inner = jnp.sum(probs * grad_probs, axis=1, keepdims=True)
        grad_raw = (probs * (grad_probs - inner) * scale).astype(jnp.bfloat16)
        dq_ref[:, cols] = jnp.dot(grad_raw, k, preferred_element_type=jnp.float32)
        dk_ref[:, cols] = lax.dot_general(
            grad_raw, q, (((0,), (0,)), ((), ())), preferred_element_type=jnp.float32
        )
        dv_ref[:, cols] = lax.dot_general(
            probs.astype(jnp.bfloat16), do, (((0,), (0,)), ((), ())), preferred_element_type=jnp.float32
        )


def mask_specs(queries, keys):
    column = pl.BlockSpec((queries, 1), lambda i: (0, 0))
    row = pl.BlockSpec((1, keys), lambda i: (0, 0))
    return [column, column, column, row, row, row]


def attention_forward(q, kv, masks):
    queries, width = q.shape
    keys = kv.shape[0]
    block = 2 * HDIM
    pairs = width // block
    return pl.pallas_call(
        attention_forward_kernel,
        grid=(pairs,),
        in_specs=[
            pl.BlockSpec((queries, block), lambda i: (0, i)),
            pl.BlockSpec((keys, block), lambda i: (0, i)),
            pl.BlockSpec((keys, block), lambda i, p=pairs: (0, i + p)),
        ] + mask_specs(queries, keys),
        out_specs=[
            pl.BlockSpec((queries, block), lambda i: (0, i)),
            pl.BlockSpec((None, queries, 2), lambda i: (i, 0, 0)),
        ],
        out_shape=[
            jax.ShapeDtypeStruct((queries, width), jnp.float32),
            jax.ShapeDtypeStruct((pairs, queries, 2), jnp.float32),
        ],
        compiler_params=pltpu.CompilerParams(dimension_semantics=("arbitrary",)),
        cost_estimate=pl.CostEstimate(
            flops=4 * queries * keys * width, transcendentals=queries * keys * HEADS,
            bytes_accessed=2 * (queries + 2 * keys) * width + 4 * queries * width,
        ),
    )(q, kv, kv, *masks)


def attention_backward(q, kv, do, lse, masks):
    queries, width = q.shape
    keys = kv.shape[0]
    block = 2 * HDIM
    pairs = width // block
    return pl.pallas_call(
        attention_backward_kernel,
        grid=(pairs,),
        in_specs=[
            pl.BlockSpec((queries, block), lambda i: (0, i)),
            pl.BlockSpec((keys, block), lambda i: (0, i)),
            pl.BlockSpec((keys, block), lambda i, p=pairs: (0, i + p)),
            pl.BlockSpec((queries, block), lambda i: (0, i)),
            pl.BlockSpec((None, queries, 2), lambda i: (i, 0, 0)),
        ] + mask_specs(queries, keys),
        out_specs=[
            pl.BlockSpec((queries, block), lambda i: (0, i)),
            pl.BlockSpec((keys, block), lambda i: (0, i)),
            pl.BlockSpec((keys, block), lambda i: (0, i)),
        ],
        out_shape=[
            jax.ShapeDtypeStruct((queries, width), jnp.float32),
            jax.ShapeDtypeStruct((keys, width), jnp.float32),
            jax.ShapeDtypeStruct((keys, width), jnp.float32),
        ],
        compiler_params=pltpu.CompilerParams(dimension_semantics=("arbitrary",)),
        cost_estimate=pl.CostEstimate(
            flops=10 * queries * keys * width, transcendentals=queries * keys * HEADS,
            bytes_accessed=2 * (2 * queries + 2 * keys) * width + 4 * (queries + 2 * keys) * width,
        ),
    )(q, kv, kv, do, lse, *masks)


def shift(x, axis, n, step):
    return lax.ppermute(x, axis, [(i, (i + step) % n) for i in range(n)])


def place(buf, piece, index, dim):
    start = [0] * buf.ndim
    start[dim] = index * piece.shape[dim]
    return lax.dynamic_update_slice(buf, piece, start)


def ring_gather(piece, axis, n, dim, direct=False):
    if n == 1:
        return piece
    me = lax.axis_index(axis)
    shape = list(piece.shape)
    shape[dim] *= n
    buf = place(jnp.zeros(shape, piece.dtype), piece, me, dim)
    if n == 2 or direct:
        for k in range(1, n):
            buf = place(buf, shift(piece, axis, n, k), (me - k) % n, dim)
        return buf
    back = piece
    ahead = piece
    for step in range(1, n // 2 + 1):
        if step < n - step:
            back = shift(back, axis, n, 1)
            ahead = shift(ahead, axis, n, -1)
            buf = place(buf, back, (me - step) % n, dim)
            buf = place(buf, ahead, (me + step) % n, dim)
        else:
            half = piece.shape[dim] // 2
            first = shift(lax.slice_in_dim(back, 0, half, axis=dim), axis, n, 1)
            second = shift(lax.slice_in_dim(ahead, half, piece.shape[dim], axis=dim), axis, n, -1)
            buf = place(buf, jnp.concatenate([first, second], axis=dim), (me + step) % n, dim)
    return buf


def ring_reduce(x, axis, n, dim, hdim, direct=False):
    if n == 1:
        return x
    me = lax.axis_index(axis)
    size = x.shape[dim] // n

    def chunk(k):
        return lax.dynamic_slice_in_dim(x, (k % n) * size, size, axis=dim)

    def low(v):
        return v.astype(jnp.bfloat16)

    if n == 2 or direct:
        acc = chunk(me)
        for k in range(1, n):
            acc = acc + shift(low(chunk(me + k)), axis, n, k).astype(jnp.float32)
        return acc
    assert n == 4
    half = x.shape[hdim] // 2

    def part(k, which):
        c = chunk(k)
        return lax.slice_in_dim(c, 0, half, axis=hdim) if which == 0 else lax.slice_in_dim(
            c, half, c.shape[hdim], axis=hdim
        )

    from_ahead = shift(low(jnp.stack([part(me - 2, 0), part(me - 1, 1)])), axis, n, -1)
    from_back = shift(low(jnp.stack([part(me + 2, 1), part(me + 1, 0)])), axis, n, 1)
    relay_ahead = shift(low(from_ahead[0].astype(jnp.float32) + part(me - 1, 0)), axis, n, -1)
    relay_back = shift(low(from_back[0].astype(jnp.float32) + part(me + 1, 1)), axis, n, 1)
    first = part(me, 0) + from_back[1].astype(jnp.float32) + relay_ahead.astype(jnp.float32)
    second = part(me, 1) + from_ahead[1].astype(jnp.float32) + relay_back.astype(jnp.float32)
    return jnp.concatenate([first, second], axis=hdim)


def cross(x):
    return lax.ppermute(x, ("xl", "xh"), [(i, 3 - i) for i in range(4)])


def swap_core(x):
    return lax.ppermute(x, "c", [(0, 1), (1, 0)])


def absolute(parts, rows):
    xh = lax.axis_index("xh")
    c = lax.axis_index("c")
    same = jnp.where(c == 0, jnp.concatenate(parts[0:2]), jnp.concatenate(parts[1::-1]))
    other = jnp.where(c == 0, jnp.concatenate(parts[2:4]), jnp.concatenate(parts[3:1:-1]))
    return jnp.where(xh == 0, jnp.concatenate([same, other]), jnp.concatenate([other, same]))


def gather_group(own, axis, n, direct):
    size = own.shape[0] // n
    me = lax.axis_index(axis)
    mine = lax.dynamic_slice_in_dim(own, me * size, size, axis=0)
    other = ring_gather(cross(mine), axis, n, 0, direct)
    partner = swap_core(jnp.concatenate([own, other]))
    rows = own.shape[0]
    return [own, partner[:rows], other, partner[rows:]]


def gather_weights(group, axis, sizes, direct):
    parts = gather_group(jnp.concatenate(group), axis, sizes[axis], direct)
    out = []
    start = 0
    for s in group:
        rows = s.shape[0]
        out.append(absolute([p[start:start + rows] for p in parts], rows))
        start += rows
    return out


def reduce_group(grads, sizes, direct):
    g = lax.axis_index("xh") * 2 + lax.axis_index("c")

    def by_shard(w):
        if w.ndim == 2:
            return w.reshape(4, -1, w.shape[-1])
        blocks, rows, width = w.shape
        return w.reshape(blocks, 4, rows // 4, width).transpose(1, 0, 2, 3).reshape(4, -1, width)

    every = jnp.concatenate([by_shard(w) for w in grads], axis=1)

    def shard(j):
        return lax.dynamic_index_in_dim(every, jnp.bitwise_xor(g, j), 0, False)

    got = swap_core(jnp.stack([shard(1), shard(3)]))
    pair = jnp.stack([shard(0), shard(2)]).astype(jnp.float32) + got.astype(jnp.float32)
    ny, nz = sizes["y"], sizes["z"]
    rows = pair.shape[1]
    own = ring_reduce(pair[0], "y", ny, 0, 1, direct)
    own = ring_reduce(own, "z", nz, 0, 1, True)
    oth = ring_reduce(pair[1].reshape(ny, rows // ny, -1), "z", nz, 1, 2, direct)
    oth = ring_reduce(oth, "y", ny, 0, 2, True).reshape(own.shape)
    low_own = own.astype(jnp.bfloat16)
    low_oth = oth.astype(jnp.bfloat16)
    mine = (
        own
        + lax.ppermute(low_own, "xl", [(0, 1), (1, 0)]).astype(jnp.float32)
        + cross(low_oth).astype(jnp.float32)
        + lax.ppermute(low_oth, "xh", [(0, 1), (1, 0)]).astype(jnp.float32)
    )
    full = ring_gather(mine.astype(jnp.bfloat16), "z", sizes["z"], 0, True)
    full = ring_gather(full, "y", sizes["y"], 0, direct)
    out = []
    start = 0
    for w in grads:
        rows = w.size // (4 * w.shape[-1])
        out.append(full[start:start + rows].astype(jnp.float32))
        start += rows
    return out


def to_sequence(x):
    xh = lax.axis_index("xh")
    c = lax.axis_index("c")
    first = lax.ppermute(lax.dynamic_index_in_dim(x, c, 0, False), GRP, [(0, 0), (1, 2), (2, 1), (3, 3)])
    second = lax.ppermute(lax.dynamic_index_in_dim(x, 1 - c, 0, False), GRP, [(0, 2), (1, 0), (2, 3), (3, 1)])
    return jnp.where(xh == 0, jnp.concatenate([first, second]), jnp.concatenate([second, first]))


def from_sequence(x):
    xh = lax.axis_index("xh")
    c = lax.axis_index("c")
    length = x.shape[0] // 2
    first = jnp.where(xh == 0, x[:length], x[length:])
    second = jnp.where(xh == 0, x[length:], x[:length])
    first = lax.ppermute(first, GRP, [(0, 0), (1, 2), (2, 1), (3, 3)])
    second = lax.ppermute(second, GRP, [(2, 0), (0, 1), (3, 2), (1, 3)])
    return jnp.where(c == 0, jnp.stack([first, second]), jnp.stack([second, first]))


def body(
    tokens, segment, piece_start, w_query, w_key, w_value, w_out, w_gate, w_up, w_down, cotangent
):
    sizes = {"y": lax.axis_size("y"), "z": lax.axis_size("z"), "xl": lax.axis_size("xl")}
    width = tokens.shape[2]
    local_length = tokens.shape[1] * 2
    full_length = segment.shape[1]
    head_count = HEADS
    head_size = HDIM
    scale = head_size ** (-0.5)
    xh = lax.axis_index("xh")
    c = lax.axis_index("c")
    first_row = c * local_length
    rows = first_row + jnp.arange(local_length, dtype=jnp.int32)
    columns = jnp.arange(full_length, dtype=jnp.int32)
    inverse = 10000.0 ** (-jnp.arange(0, head_size, 2).astype(jnp.float32) / head_size)
    angles = rows.astype(jnp.float32)[:, None] * inverse[None, :]
    cosine = jnp.cos(angles)[:, None, :]
    sine = jnp.sin(angles)[:, None, :]

    query_weight, key_weight, value_weight = gather_weights(
        (w_query, w_key, w_value), "y", sizes, True
    )

    both_in = to_sequence(jnp.concatenate([tokens, cotangent], axis=2))
    hidden = both_in[:, :width].astype(jnp.float32)
    grad_result = both_in[:, width:]
    seg_row = lax.dynamic_index_in_dim(segment, xh, 0, False)
    start_row = lax.dynamic_index_in_dim(piece_start, xh, 0, False)

    normed, norm_one_back = jax.vjp(layer_norm, hidden)
    normed_low = normed.astype(jnp.bfloat16)
    query_heads = rotate(
        matmul(normed_low, query_weight).reshape(local_length, head_count, head_size),
        cosine,
        sine,
    ).astype(jnp.bfloat16)
    keys = (
        rotate(
            matmul(normed_low, key_weight).reshape(local_length, head_count, head_size),
            cosine,
            sine,
        )
        .reshape(local_length, width)
        .astype(jnp.bfloat16)
    )
    values = matmul(normed_low, value_weight).astype(jnp.bfloat16)
    out_weight, down_weight = gather_weights((w_out, w_down), "z", sizes, False)
    gate_weight, up_weight = gather_weights((w_gate, w_up), "y", sizes, False)
    mine_kv = jnp.concatenate([keys, values], axis=1)
    both = jnp.concatenate([mine_kv, swap_core(mine_kv)])
    other_row = (1 - c) * local_length
    seg_local = lax.dynamic_slice_in_dim(seg_row, first_row, local_length)
    start_local = lax.dynamic_slice_in_dim(start_row, first_row, local_length)
    key_rows = jnp.concatenate([rows, other_row + jnp.arange(local_length, dtype=jnp.int32)])
    seg_keys = jnp.concatenate([seg_local, lax.dynamic_slice_in_dim(seg_row, other_row, local_length)])
    start_keys = jnp.concatenate(
        [start_local, lax.dynamic_slice_in_dim(start_row, other_row, local_length)]
    )
    masks = (
        rows[:, None],
        seg_local[:, None],
        start_local[:, None],
        seg_keys[None, :],
        start_keys[None, :],
        key_rows[None, :],
    )
    query_flat = query_heads.reshape(local_length, width)
    mixed, log_total = attention_forward(query_flat, both, masks)
    mixed_low = mixed.reshape(local_length, width).astype(jnp.bfloat16)
    after = hidden + matmul(mixed_low, out_weight)
    normed_two, norm_two_back = jax.vjp(layer_norm, after)
    normed_two_low = normed_two.astype(jnp.bfloat16)
    gate = matmul(normed_two_low, gate_weight)
    upper = matmul(normed_two_low, up_weight)
    active, gate_back = jax.vjp(gated, gate, upper)
    active_low = active.astype(jnp.bfloat16)
    result = after + matmul(active_low, down_weight)
    result_low = result.astype(jnp.bfloat16)

    grads = [None] * 7
    grads[6] = contract_rows(active_low, grad_result)
    grad_active = contract_cols(grad_result, down_weight)
    grad_gate, grad_upper = gate_back(grad_active)
    gate_low = grad_gate.astype(jnp.bfloat16)
    upper_low = grad_upper.astype(jnp.bfloat16)
    def blocked_grad(left, right):
        count = right.shape[1] // width
        return jnp.stack(
            [contract_rows(left, right[:, i * width:(i + 1) * width]) for i in range(count)]
        )

    grads[4] = blocked_grad(normed_two_low, gate_low)
    grads[5] = blocked_grad(normed_two_low, upper_low)
    grad_normed_two = contract_cols(gate_low, gate_weight) + contract_cols(upper_low, up_weight)
    grad_after = grad_result.astype(jnp.float32) + norm_two_back(grad_normed_two)[0]
    after_low = grad_after.astype(jnp.bfloat16)
    grads[3] = contract_rows(mixed_low, after_low)
    grad_mixed = (
        contract_cols(after_low, out_weight)
        .astype(jnp.bfloat16)
        .reshape(local_length, head_count, head_size)
    )
    grad_query, grad_keys, grad_values = attention_backward(
        query_flat, both, grad_mixed.reshape(local_length, width), log_total, masks
    )
    grad_query = grad_query.reshape(local_length, head_count, head_size)
    grad_kv = jnp.concatenate([grad_keys, grad_values], axis=1)
    own_kv = grad_kv[:local_length] + swap_core(grad_kv[local_length:])
    own_keys = own_kv[:, :width]
    own_values = own_kv[:, width:]
    query_low = (
        rotate(grad_query, cosine, -sine).reshape(local_length, width).astype(jnp.bfloat16)
    )
    keys_low = (
        rotate(own_keys.reshape(local_length, head_count, head_size), cosine, -sine)
        .reshape(local_length, width)
        .astype(jnp.bfloat16)
    )
    values_low = own_values.astype(jnp.bfloat16)
    grads[0] = contract_rows(normed_low, query_low)
    grads[1] = contract_rows(normed_low, keys_low)
    grads[2] = contract_rows(normed_low, values_low)
    grad_normed = (
        contract_cols(query_low, query_weight)
        + contract_cols(keys_low, key_weight)
        + contract_cols(values_low, value_weight)
    )
    grad_hidden = grad_after + norm_one_back(grad_normed)[0]
    both_out = from_sequence(jnp.concatenate([result_low, grad_hidden.astype(jnp.bfloat16)], axis=1))
    output = both_out[..., :width]
    input_grads = both_out[..., width:]
    blocks, gate_rows = grads[4].shape[0], grads[4].shape[1]
    low = [w.astype(jnp.bfloat16) for w in grads]
    owned = reduce_group(low, sizes, False)
    for i in (4, 5):
        owned[i] = owned[i].reshape(blocks, gate_rows // 4, width).transpose(1, 0, 2).reshape(
            gate_rows // 4, blocks * width
        )

    return (output, input_grads, *owned)


def solution(mesh):
    rep, grp = mesh.devices.shape
    side = int(round((rep // 2) ** 0.5))
    devices = mesh.devices.reshape(side, rep // (2 * side), 2, grp // 2, 2)
    fine = Mesh(devices, ("y", "z", "xl", "xh", "c"))
    seqs = P(REP, GRP, None)
    rows = P(GRP, None)
    placed = (seqs, P(REP, None), P(REP, None), rows, rows, rows, rows, rows, rows, rows, seqs)
    return jax.shard_map(
        body,
        mesh=fine,
        in_specs=placed,
        out_specs=(seqs, seqs, rows, rows, rows, rows, rows, rows, rows),
        check_vma=False,
    )
```

```python
import jax
import jax.numpy as jnp
from jax import lax
from jax.sharding import Mesh
from jax.sharding import PartitionSpec as P
from jax.experimental import pallas as pl
from jax.experimental.pallas import tpu as pltpu

HEADS = 12
HDIM = 64
REP = ("y", "z", "xl")
GRP = ("xh", "c")


def layer_norm(hidden):
    centred = hidden - jnp.mean(hidden, axis=-1, keepdims=True)
    spread = jnp.mean(centred * centred, axis=-1, keepdims=True)
    return centred * lax.rsqrt(spread + 1e-05)


def rotate(heads, cosine, sine):
    half = heads.shape[-1] // 2
    first = heads[..., :half]
    second = heads[..., half:]
    return jnp.concatenate(
        [first * cosine - second * sine, second * cosine + first * sine], axis=-1
    )


def gated(gate, upper):
    return gate / (1.0 + jnp.exp(-gate)) * upper


def matmul(left, right):
    return jnp.dot(left, right, preferred_element_type=jnp.float32)


def contract_rows(left, right):
    return lax.dot_general(
        left, right, (((0,), (0,)), ((), ())), preferred_element_type=jnp.float32
    )


def contract_cols(left, right):
    return lax.dot_general(
        left, right, (((1,), (1,)), ((), ())), preferred_element_type=jnp.float32
    )


def allowed_mask(rq_ref, sq_ref, pq_ref, sk_ref, pk_ref, rk_ref):
    return (sq_ref[...] == sk_ref[...]) & (
        (rk_ref[...] <= rq_ref[...]) | (pq_ref[...] == pk_ref[...])
    )


def attention_forward_kernel(
    q_ref, k_ref, v_ref, rq_ref, sq_ref, pq_ref, sk_ref, pk_ref, rk_ref, o_ref, lse_ref
):
    queries = q_ref.shape[0]
    keys = k_ref.shape[0]
    allowed = allowed_mask(rq_ref, sq_ref, pq_ref, sk_ref, pk_ref, rk_ref)
    scale = HDIM ** (-0.5)
    for h in range(q_ref.shape[1] // HDIM):
        cols = slice(h * HDIM, (h + 1) * HDIM)
        raw = lax.dot_general(
            q_ref[:, cols] * scale, k_ref[:, cols], (((1,), (1,)), ((), ())),
            preferred_element_type=jnp.float32,
        )
        scores = jnp.where(allowed, raw, -1e30)
        highest = jnp.max(scores, axis=1, keepdims=True)
        expd = jnp.exp(scores - highest)
        total = jnp.sum(expd, axis=1, keepdims=True)
        probs_low = (expd / total).astype(jnp.bfloat16)
        o_ref[:, cols] = jnp.dot(probs_low, v_ref[:, cols], preferred_element_type=jnp.float32)
        lse_ref[:, h:h + 1] = highest + jnp.log(total)


def attention_backward_kernel(
    q_ref, k_ref, v_ref, do_ref, lse_ref, rq_ref, sq_ref, pq_ref, sk_ref, pk_ref, rk_ref,
    dq_ref, dk_ref, dv_ref,
):
    queries = q_ref.shape[0]
    keys = k_ref.shape[0]
    allowed = allowed_mask(rq_ref, sq_ref, pq_ref, sk_ref, pk_ref, rk_ref)
    scale = HDIM ** (-0.5)
    for h in range(q_ref.shape[1] // HDIM):
        cols = slice(h * HDIM, (h + 1) * HDIM)
        q = q_ref[:, cols]
        k = k_ref[:, cols]
        v = v_ref[:, cols]
        do = do_ref[:, cols]
        raw = lax.dot_general(q * scale, k, (((1,), (1,)), ((), ())), preferred_element_type=jnp.float32)
        scores = jnp.where(allowed, raw, -1e30)
        probs = jnp.exp(scores - lse_ref[:, h:h + 1])
        grad_probs = lax.dot_general(do, v, (((1,), (1,)), ((), ())), preferred_element_type=jnp.float32)
        inner = jnp.sum(probs * grad_probs, axis=1, keepdims=True)
        grad_raw = (probs * (grad_probs - inner) * scale).astype(jnp.bfloat16)
        dq_ref[:, cols] = jnp.dot(grad_raw, k, preferred_element_type=jnp.float32)
        dk_ref[:, cols] = lax.dot_general(
            grad_raw, q, (((0,), (0,)), ((), ())), preferred_element_type=jnp.float32
        )
        dv_ref[:, cols] = lax.dot_general(
            probs.astype(jnp.bfloat16), do, (((0,), (0,)), ((), ())), preferred_element_type=jnp.float32
        )


def mask_specs(queries, keys):
    column = pl.BlockSpec((queries, 1), lambda i: (0, 0))
    row = pl.BlockSpec((1, keys), lambda i: (0, 0))
    return [column, column, column, row, row, row]


def attention_forward(q, kv, masks):
    queries, width = q.shape
    keys = kv.shape[0]
    block = 2 * HDIM
    pairs = width // block
    return pl.pallas_call(
        attention_forward_kernel,
        grid=(pairs,),
        in_specs=[
            pl.BlockSpec((queries, block), lambda i: (0, i)),
            pl.BlockSpec((keys, block), lambda i: (0, i)),
            pl.BlockSpec((keys, block), lambda i, p=pairs: (0, i + p)),
        ] + mask_specs(queries, keys),
        out_specs=[
            pl.BlockSpec((queries, block), lambda i: (0, i)),
            pl.BlockSpec((None, queries, 2), lambda i: (i, 0, 0)),
        ],
        out_shape=[
            jax.ShapeDtypeStruct((queries, width), jnp.float32),
            jax.ShapeDtypeStruct((pairs, queries, 2), jnp.float32),
        ],
        compiler_params=pltpu.CompilerParams(dimension_semantics=("arbitrary",)),
        cost_estimate=pl.CostEstimate(
            flops=4 * queries * keys * width, transcendentals=queries * keys * HEADS,
            bytes_accessed=2 * (queries + 2 * keys) * width + 4 * queries * width,
        ),
    )(q, kv, kv, *masks)


def attention_backward(q, kv, do, lse, masks):
    queries, width = q.shape
    keys = kv.shape[0]
    block = 2 * HDIM
    pairs = width // block
    return pl.pallas_call(
        attention_backward_kernel,
        grid=(pairs,),
        in_specs=[
            pl.BlockSpec((queries, block), lambda i: (0, i)),
            pl.BlockSpec((keys, block), lambda i: (0, i)),
            pl.BlockSpec((keys, block), lambda i, p=pairs: (0, i + p)),
            pl.BlockSpec((queries, block), lambda i: (0, i)),
            pl.BlockSpec((None, queries, 2), lambda i: (i, 0, 0)),
        ] + mask_specs(queries, keys),
        out_specs=[
            pl.BlockSpec((queries, block), lambda i: (0, i)),
            pl.BlockSpec((keys, block), lambda i: (0, i)),
            pl.BlockSpec((keys, block), lambda i: (0, i)),
        ],
        out_shape=[
            jax.ShapeDtypeStruct((queries, width), jnp.float32),
            jax.ShapeDtypeStruct((keys, width), jnp.float32),
            jax.ShapeDtypeStruct((keys, width), jnp.float32),
        ],
        compiler_params=pltpu.CompilerParams(dimension_semantics=("arbitrary",)),
        cost_estimate=pl.CostEstimate(
            flops=10 * queries * keys * width, transcendentals=queries * keys * HEADS,
            bytes_accessed=2 * (2 * queries + 2 * keys) * width + 4 * (queries + 2 * keys) * width,
        ),
    )(q, kv, kv, do, lse, *masks)


def shift(x, axis, n, step):
    return lax.ppermute(x, axis, [(i, (i + step) % n) for i in range(n)])


def place(buf, piece, index, dim):
    start = [0] * buf.ndim
    start[dim] = index * piece.shape[dim]
    return lax.dynamic_update_slice(buf, piece, start)


def ring_gather(piece, axis, n, dim, direct=False):
    if n == 1:
        return piece
    me = lax.axis_index(axis)
    shape = list(piece.shape)
    shape[dim] *= n
    buf = place(jnp.zeros(shape, piece.dtype), piece, me, dim)
    if n == 2 or direct:
        for k in range(1, n):
            buf = place(buf, shift(piece, axis, n, k), (me - k) % n, dim)
        return buf
    back = piece
    ahead = piece
    for step in range(1, n // 2 + 1):
        if step < n - step:
            back = shift(back, axis, n, 1)
            ahead = shift(ahead, axis, n, -1)
            buf = place(buf, back, (me - step) % n, dim)
            buf = place(buf, ahead, (me + step) % n, dim)
        else:
            half = piece.shape[dim] // 2
            first = shift(lax.slice_in_dim(back, 0, half, axis=dim), axis, n, 1)
            second = shift(lax.slice_in_dim(ahead, half, piece.shape[dim], axis=dim), axis, n, -1)
            buf = place(buf, jnp.concatenate([first, second], axis=dim), (me + step) % n, dim)
    return buf


def ring_reduce(x, axis, n, dim, hdim, direct=False):
    if n == 1:
        return x
    me = lax.axis_index(axis)
    size = x.shape[dim] // n

    def chunk(k):
        return lax.dynamic_slice_in_dim(x, (k % n) * size, size, axis=dim)

    def low(v):
        return v.astype(jnp.bfloat16)

    if n == 2 or direct:
        acc = chunk(me)
        for k in range(1, n):
            acc = acc + shift(low(chunk(me + k)), axis, n, k).astype(jnp.float32)
        return acc
    assert n == 4
    half = x.shape[hdim] // 2

    def part(k, which):
        c = chunk(k)
        return lax.slice_in_dim(c, 0, half, axis=hdim) if which == 0 else lax.slice_in_dim(
            c, half, c.shape[hdim], axis=hdim
        )

    from_ahead = shift(low(jnp.stack([part(me - 2, 0), part(me - 1, 1)])), axis, n, -1)
    from_back = shift(low(jnp.stack([part(me + 2, 1), part(me + 1, 0)])), axis, n, 1)
    relay_ahead = shift(low(from_ahead[0].astype(jnp.float32) + part(me - 1, 0)), axis, n, -1)
    relay_back = shift(low(from_back[0].astype(jnp.float32) + part(me + 1, 1)), axis, n, 1)
    first = part(me, 0) + from_back[1].astype(jnp.float32) + relay_ahead.astype(jnp.float32)
    second = part(me, 1) + from_ahead[1].astype(jnp.float32) + relay_back.astype(jnp.float32)
    return jnp.concatenate([first, second], axis=hdim)


def cross(x):
    return lax.ppermute(x, ("xl", "xh"), [(i, 3 - i) for i in range(4)])


def swap_core(x):
    return lax.ppermute(x, "c", [(0, 1), (1, 0)])


def absolute(parts, rows):
    xh = lax.axis_index("xh")
    c = lax.axis_index("c")
    same = jnp.where(c == 0, jnp.concatenate(parts[0:2]), jnp.concatenate(parts[1::-1]))
    other = jnp.where(c == 0, jnp.concatenate(parts[2:4]), jnp.concatenate(parts[3:1:-1]))
    return jnp.where(xh == 0, jnp.concatenate([same, other]), jnp.concatenate([other, same]))


def gather_group(own, axis, n, direct):
    size = own.shape[0] // n
    me = lax.axis_index(axis)
    mine = lax.dynamic_slice_in_dim(own, me * size, size, axis=0)
    other = ring_gather(cross(mine), axis, n, 0, direct)
    partner = swap_core(jnp.concatenate([own, other]))
    rows = own.shape[0]
    return [own, partner[:rows], other, partner[rows:]]


def gather_weights(group, axis, sizes, direct):
    parts = gather_group(jnp.concatenate(group), axis, sizes[axis], direct)
    out = []
    start = 0
    for s in group:
        rows = s.shape[0]
        out.append(absolute([p[start:start + rows] for p in parts], rows))
        start += rows
    return out


def reduce_group(grads, sizes, direct):
    g = lax.axis_index("xh") * 2 + lax.axis_index("c")

    def by_shard(w):
        if w.ndim == 2:
            return w.reshape(4, -1, w.shape[-1])
        blocks, rows, width = w.shape
        return w.reshape(blocks, 4, rows // 4, width).transpose(1, 0, 2, 3).reshape(4, -1, width)

    every = jnp.concatenate([by_shard(w) for w in grads], axis=1)

    def shard(j):
        return lax.dynamic_index_in_dim(every, jnp.bitwise_xor(g, j), 0, False)

    got = swap_core(jnp.stack([shard(1), shard(3)]))
    pair = jnp.stack([shard(0), shard(2)]).astype(jnp.float32) + got.astype(jnp.float32)
    ny, nz = sizes["y"], sizes["z"]
    rows = pair.shape[1]
    own = ring_reduce(pair[0], "y", ny, 0, 1, direct)
    own = ring_reduce(own, "z", nz, 0, 1, True)
    oth = ring_reduce(pair[1].reshape(ny, rows // ny, -1), "z", nz, 1, 2, direct)
    oth = ring_reduce(oth, "y", ny, 0, 2, True).reshape(own.shape)
    low_own = own.astype(jnp.bfloat16)
    low_oth = oth.astype(jnp.bfloat16)
    mine = (
        own
        + lax.ppermute(low_own, "xl", [(0, 1), (1, 0)]).astype(jnp.float32)
        + cross(low_oth).astype(jnp.float32)
        + lax.ppermute(low_oth, "xh", [(0, 1), (1, 0)]).astype(jnp.float32)
    )
    full = ring_gather(mine.astype(jnp.bfloat16), "z", sizes["z"], 0, True)
    full = ring_gather(full, "y", sizes["y"], 0, direct)
    out = []
    start = 0
    for w in grads:
        rows = w.size // (4 * w.shape[-1])
        out.append(full[start:start + rows].astype(jnp.float32))
        start += rows
    return out


def to_sequence(x):
    xh = lax.axis_index("xh")
    c = lax.axis_index("c")
    first = lax.ppermute(lax.dynamic_index_in_dim(x, c, 0, False), GRP, [(0, 0), (1, 2), (2, 1), (3, 3)])
    second = lax.ppermute(lax.dynamic_index_in_dim(x, 1 - c, 0, False), GRP, [(0, 2), (1, 0), (2, 3), (3, 1)])
    return jnp.where(xh == 0, jnp.concatenate([first, second]), jnp.concatenate([second, first]))


def from_sequence(x):
    xh = lax.axis_index("xh")
    c = lax.axis_index("c")
    length = x.shape[0] // 2
    first = jnp.where(xh == 0, x[:length], x[length:])
    second = jnp.where(xh == 0, x[length:], x[:length])
    first = lax.ppermute(first, GRP, [(0, 0), (1, 2), (2, 1), (3, 3)])
    second = lax.ppermute(second, GRP, [(2, 0), (0, 1), (3, 2), (1, 3)])
    return jnp.where(c == 0, jnp.stack([first, second]), jnp.stack([second, first]))


def body(
    tokens, segment, piece_start, w_query, w_key, w_value, w_out, w_gate, w_up, w_down, cotangent
):
    sizes = {"y": lax.axis_size("y"), "z": lax.axis_size("z"), "xl": lax.axis_size("xl")}
    width = tokens.shape[2]
    local_length = tokens.shape[1] * 2
    full_length = segment.shape[1]
    head_count = HEADS
    head_size = HDIM
    scale = head_size ** (-0.5)
    xh = lax.axis_index("xh")
    c = lax.axis_index("c")
    first_row = c * local_length
    rows = first_row + jnp.arange(local_length, dtype=jnp.int32)
    columns = jnp.arange(full_length, dtype=jnp.int32)
    inverse = 10000.0 ** (-jnp.arange(0, head_size, 2).astype(jnp.float32) / head_size)
    angles = rows.astype(jnp.float32)[:, None] * inverse[None, :]
    cosine = jnp.cos(angles)[:, None, :]
    sine = jnp.sin(angles)[:, None, :]

    query_weight, key_weight, value_weight = gather_weights(
        (w_query, w_key, w_value), "y", sizes, True
    )

    both_in = to_sequence(jnp.concatenate([tokens, cotangent], axis=2))
    hidden = both_in[:, :width].astype(jnp.float32)
    grad_result = both_in[:, width:]
    seg_row = lax.dynamic_index_in_dim(segment, xh, 0, False)
    start_row = lax.dynamic_index_in_dim(piece_start, xh, 0, False)

    normed, norm_one_back = jax.vjp(layer_norm, hidden)
    normed_low = normed.astype(jnp.bfloat16)
    query_heads = rotate(
        matmul(normed_low, query_weight).reshape(local_length, head_count, head_size),
        cosine,
        sine,
    ).astype(jnp.bfloat16)
    keys = (
        rotate(
            matmul(normed_low, key_weight).reshape(local_length, head_count, head_size),
            cosine,
            sine,
        )
        .reshape(local_length, width)
        .astype(jnp.bfloat16)
    )
    values = matmul(normed_low, value_weight).astype(jnp.bfloat16)
    out_weight, down_weight = gather_weights((w_out, w_down), "z", sizes, False)
    gate_weight, up_weight = gather_weights((w_gate, w_up), "y", sizes, False)
    mine_kv = jnp.concatenate([keys, values], axis=1)
    both = jnp.concatenate([mine_kv, swap_core(mine_kv)])
    other_row = (1 - c) * local_length
    seg_local = lax.dynamic_slice_in_dim(seg_row, first_row, local_length)
    start_local = lax.dynamic_slice_in_dim(start_row, first_row, local_length)
    key_rows = jnp.concatenate([rows, other_row + jnp.arange(local_length, dtype=jnp.int32)])
    seg_keys = jnp.concatenate([seg_local, lax.dynamic_slice_in_dim(seg_row, other_row, local_length)])
    start_keys = jnp.concatenate(
        [start_local, lax.dynamic_slice_in_dim(start_row, other_row, local_length)]
    )
    masks = (
        rows[:, None],
        seg_local[:, None],
        start_local[:, None],
        seg_keys[None, :],
        start_keys[None, :],
        key_rows[None, :],
    )
    query_flat = query_heads.reshape(local_length, width)
    mixed, log_total = attention_forward(query_flat, both, masks)
    mixed_low = mixed.reshape(local_length, width).astype(jnp.bfloat16)
    after = hidden + matmul(mixed_low, out_weight)
    normed_two, norm_two_back = jax.vjp(layer_norm, after)
    normed_two_low = normed_two.astype(jnp.bfloat16)
    gate = matmul(normed_two_low, gate_weight)
    upper = matmul(normed_two_low, up_weight)
    active, gate_back = jax.vjp(gated, gate, upper)
    active_low = active.astype(jnp.bfloat16)
    result = after + matmul(active_low, down_weight)
    result_low = result.astype(jnp.bfloat16)

    grads = [None] * 7
    grads[6] = contract_rows(active_low, grad_result)
    grad_active = contract_cols(grad_result, down_weight)
    grad_gate, grad_upper = gate_back(grad_active)
    gate_low = grad_gate.astype(jnp.bfloat16)
    upper_low = grad_upper.astype(jnp.bfloat16)
    def blocked_grad(left, right):
        count = right.shape[1] // width
        return jnp.stack(
            [contract_rows(left, right[:, i * width:(i + 1) * width]) for i in range(count)]
        )

    grads[4] = blocked_grad(normed_two_low, gate_low)
    grads[5] = blocked_grad(normed_two_low, upper_low)
    grad_normed_two = contract_cols(gate_low, gate_weight) + contract_cols(upper_low, up_weight)
    grad_after = grad_result.astype(jnp.float32) + norm_two_back(grad_normed_two)[0]
    after_low = grad_after.astype(jnp.bfloat16)
    grads[3] = contract_rows(mixed_low, after_low)
    grad_mixed = (
        contract_cols(after_low, out_weight)
        .astype(jnp.bfloat16)
        .reshape(local_length, head_count, head_size)
    )
    grad_query, grad_keys, grad_values = attention_backward(
        query_flat, both, grad_mixed.reshape(local_length, width), log_total, masks
    )
    grad_query = grad_query.reshape(local_length, head_count, head_size)
    grad_kv = jnp.concatenate([grad_keys, grad_values], axis=1)
    own_kv = grad_kv[:local_length] + swap_core(grad_kv[local_length:])
    own_keys = own_kv[:, :width]
    own_values = own_kv[:, width:]
    query_low = (
        rotate(grad_query, cosine, -sine).reshape(local_length, width).astype(jnp.bfloat16)
    )
    keys_low = (
        rotate(own_keys.reshape(local_length, head_count, head_size), cosine, -sine)
        .reshape(local_length, width)
        .astype(jnp.bfloat16)
    )
    values_low = own_values.astype(jnp.bfloat16)
    grads[0] = contract_rows(normed_low, query_low)
    grads[1] = contract_rows(normed_low, keys_low)
    grads[2] = contract_rows(normed_low, values_low)
    grad_normed = (
        contract_cols(query_low, query_weight)
        + contract_cols(keys_low, key_weight)
        + contract_cols(values_low, value_weight)
    )
    grad_hidden = grad_after + norm_one_back(grad_normed)[0]
    both_out = from_sequence(jnp.concatenate([result_low, grad_hidden.astype(jnp.bfloat16)], axis=1))
    output = both_out[..., :width]
    input_grads = both_out[..., width:]
    blocks, gate_rows = grads[4].shape[0], grads[4].shape[1]
    low = [w.astype(jnp.bfloat16) for w in grads]
    owned = reduce_group(low, sizes, False)
    for i in (4, 5):
        owned[i] = owned[i].reshape(blocks, gate_rows // 4, width).transpose(1, 0, 2).reshape(
            gate_rows // 4, blocks * width
        )

    return (output, input_grads, *owned)


def solution(mesh):
    rep, grp = mesh.devices.shape
    side = int(round((rep // 2) ** 0.5))
    devices = mesh.devices.reshape(side, rep // (2 * side), 2, grp // 2, 2)
    fine = Mesh(devices, ("y", "z", "xl", "xh", "c"))
    seqs = P(REP, GRP, None)
    rows = P(GRP, None)
    placed = (seqs, P(REP, None), P(REP, None), rows, rows, rows, rows, rows, rows, rows, seqs)
    return jax.shard_map(
        body,
        mesh=fine,
        in_specs=placed,
        out_specs=(seqs, seqs, rows, rows, rows, rows, rows, rows, rows),
        check_vma=False,
    )
```
